128 devices in a mesh: seq: 32 (over x, z_lo, y), head: 2 (over core), dp: 2 (over z_hi).
Axes of the slice: x: 4, y: 4, z: 4 (z_hi: 2, z_lo: 2; z = z_hi * 2 + z_lo), core: 2. Of those that a mesh axis runs over, the one named last changes fastest.
Arguments:
- queries: bfloat16 [16384, 2048], P(('dp', 'seq'), 'head'), parts along dimension 0, may hold values from -32 to 32
- keys: bfloat16 [16384, 2048], P(('dp', 'seq'), 'head'), parts along dimension 0, may hold values from -32 to 32
- values: bfloat16 [16384, 2048], P(('dp', 'seq'), 'head'), parts along dimension 0, may hold values from -6 to 6
- out_grad: bfloat16 [16384, 4096], P(('dp', 'seq')), parts along dimension 0, may hold values from -6 to 6
- proj_weight: bfloat16 [4096, 2048], P(None, 'head'), may hold values from -0.09375 to 0.09375
- layout: int32 [64, 12], replicated, may hold values from -1 to 63, as said below
Outputs:
- query_grad: bfloat16 [16384, 2048], P(('dp', 'seq'), 'head'), parts along dimension 0
- key_grad: bfloat16 [16384, 2048], P(('dp', 'seq'), 'head'), parts along dimension 0
- value_grad: bfloat16 [16384, 2048], P(('dp', 'seq'), 'head'), parts along dimension 0
- proj_grad: float32 [8192, 2048], P(('dp', 'seq'), 'head'), parts along dimension 0
The draws below stay inside these ranges and needn't reach their ends.
There are 2 independent parts, one for each index of `dp`. The reference program is written for one: setup_inputs(seed, part) draws one part's arguments, and reference() takes and returns one part's arrays. A program takes and returns all parts, laid end to end along the dimension named above; an argument that names none is the same for every part. Nothing has to cross between parts.
Inputs may be any that keep to these rules, and one draw needn't show every extreme that they name: `layout`: row i lists, in increasing order, some of the blocks j < i - 7 whose remainder modulo 16 equals one offset, below 8 and shared by all rows (the last row lists all of them), then the blocks max(0, i - w + 1) to i for a window w of its own between 1 and 8, and ends with -1 in the unused entries; a row whose block follows a block of that remainder has w = 8.
All inputs are finite; a program needn't handle non-finite values.
Results may differ from the reference program's by a relative error of at most 0.03.
Values may be sent and summed in bfloat16 or wider, within the bound.
A program may use at most 192 MiB of HBM per device.

```python
import jax
import jax.numpy as jnp
from jax import lax

D = 4096
HEADS = 16
HD = 128
BLK = 128
LOCAL = 8
STRIDE = 16
NB = 64
TOKENS = 8192
HF = 2048
NSUM = 4
KMAX = 12


def draw_layout(key, part):
    offset_block = jax.random.randint(jax.random.fold_in(key, 21), (), 0, STRIDE - LOCAL, dtype=jnp.int32)
    row_ids = jnp.arange(NB, dtype=jnp.int32)[:, None]
    sum_ids = jnp.arange(NSUM, dtype=jnp.int32)[None, :]
    win_ids = jnp.arange(LOCAL, dtype=jnp.int32)[None, :]
    reach_row = row_ids - LOCAL - offset_block
    strided_count = jnp.where(reach_row >= 0, jnp.maximum(reach_row, 0) // STRIDE + 1, 0)
    keep_far = jax.random.randint(jax.random.fold_in(key, 22), (NB, NSUM), 0, 4, dtype=jnp.int32) > 0
    keep_far = keep_far | (row_ids == NB - 1)
    far_entry = offset_block + STRIDE * sum_ids
    far_valid = (sum_ids < strided_count) & keep_far
    window_len = jnp.minimum(jax.random.randint(jax.random.fold_in(key, 23), (NB, 1), LOCAL // 2, LOCAL + LOCAL // 2, dtype=jnp.int32), LOCAL)
    window_len = jnp.where(row_ids % STRIDE == offset_block + 1, LOCAL, window_len)
    near_entry = row_ids - LOCAL + 1 + win_ids
    near_valid = (win_ids >= LOCAL - window_len) & (near_entry >= 0)
    entries = jnp.concatenate([jnp.broadcast_to(far_entry, (NB, NSUM)), near_entry], axis=1)
    valid = jnp.concatenate([far_valid, near_valid], axis=1)
    col_ids = jnp.arange(KMAX, dtype=jnp.int32)[None, :]
    sort_key = jnp.where(valid, 0, KMAX) + col_ids
    order = jnp.argsort(sort_key, axis=1, stable=True).astype(jnp.int32)
    sorted_entries = jnp.take_along_axis(entries, order, axis=1)
    sorted_valid = jnp.take_along_axis(valid, order, axis=1)
    table = jnp.where(sorted_valid, sorted_entries, -1)
    return table.astype(jnp.int32)


def draw_queries(key, part):
    drawn_rows = jax.random.normal(jax.random.fold_in(key, 1), (TOKENS, HF), jnp.float32)
    return jnp.clip(drawn_rows, -32.0, 32.0).astype(jnp.bfloat16)


def draw_keys(key, part):
    drawn_rows = jax.random.normal(jax.random.fold_in(key, 3), (TOKENS, HF), jnp.float32)
    return jnp.clip(drawn_rows, -32.0, 32.0).astype(jnp.bfloat16)


def strengthened(drawn, rng, source, target, shards_of, factor):
    owner, partner = [(jnp.arange(drawn.shape[position]) // (drawn.shape[position] // shards_of)).reshape([-1 if axis == position else 1 for axis in range(drawn.ndim)]) for position in (source, target)]
    chosen = jax.random.permutation(rng, shards_of)[partner]
    strong = (owner == chosen) | (owner == (partner + shards_of // 2) % shards_of)
    return jnp.where(strong, factor * drawn, drawn)


def shard_levels(own_key, shape, split, least, high):
    loudness = 1.0
    for axis_at, parts in split:
        draws = jax.random.uniform(jax.random.fold_in(jax.random.fold_in(own_key, 6), axis_at), (parts,), jnp.float32, least / len(split), high / len(split))
        loudness = loudness * jnp.repeat(jnp.exp(draws), shape[axis_at] // parts).reshape((-1,) + (1,) * (len(shape) - 1 - axis_at))
    return loudness


def normal_values(stream_key, extent, deviation, limit, shards=(), kind=jnp.bfloat16):
    values = jax.random.normal(stream_key, extent, jnp.float32) * deviation
    if len(shards) > 0:
        values = shard_levels(stream_key, extent, shards, -0.22, 0.18) * values
    return jnp.clip(values, min=-limit, max=limit).astype(kind)


def bell_draw_with(rng, shape, spread, bound, cuts, heavy, kind=jnp.bfloat16):
    values = spread * jax.random.normal(rng, shape, jnp.float32)
    if cuts:
        values = values * shard_levels(rng, shape, cuts, -0.22, 0.18)
    return jnp.clip(strengthened(values, jax.random.fold_in(rng, 3), *heavy), -bound, bound).astype(kind)


def setup_inputs(seed: int = 0, part: int = 0) -> dict:
    splits = jax.random.split(jax.random.key(seed), 7)
    own_keys = jax.random.split(jax.random.fold_in(splits[6], part), 7)
    return {
        "queries": draw_queries(jax.random.fold_in(jax.random.fold_in(splits[6], part), 71), part),
        "keys": draw_keys(jax.random.fold_in(jax.random.fold_in(splits[6], part), 71), part),
        "values": normal_values(own_keys[2], (TOKENS, HF), 1.0, 6.0, ((0, 32), (1, 2))),
        "out_grad": bell_draw_with(own_keys[3], (TOKENS, D), 1.0, 6.0, ((0, 32),), (0, 1, 32, 2.75)),
        "proj_weight": normal_values(splits[4], (D, HF), D ** -0.5, 0.09375, ((1, 2),)),
        "layout": draw_layout(jax.random.fold_in(splits[6], 71), part),
    }


def reference(queries, keys, values, out_grad, proj_weight, layout):
    score_scale = HD ** -0.5
    block_count = TOKENS // BLK
    table_width = layout.shape[1]
    attn_grad = jnp.dot(out_grad, proj_weight, preferred_element_type=jnp.float32).astype(jnp.bfloat16)
    query_blocks = queries.reshape(block_count, BLK, HEADS, HD)
    key_blocks = keys.reshape(block_count, BLK, HEADS, HD)
    value_blocks = values.reshape(block_count, BLK, HEADS, HD)
    grad_blocks = attn_grad.reshape(block_count, BLK, HEADS, HD)
    offsets = jnp.arange(BLK, dtype=jnp.int32)

    def block_step(totals, block_index):
        key_total, value_total = totals
        table_row = layout[block_index]
        safe_row = jnp.maximum(table_row, 0).astype(jnp.int32)
        query_rows = query_blocks[block_index].astype(jnp.float32)
        grad_rows = grad_blocks[block_index].astype(jnp.float32)
        key_rows = key_blocks[safe_row].astype(jnp.float32).reshape(table_width * BLK, HEADS, HD)
        value_rows = value_blocks[safe_row].astype(jnp.float32).reshape(table_width * BLK, HEADS, HD)
        query_pos = block_index * BLK + offsets
        key_pos = (safe_row[:, None] * BLK + offsets[None, :]).reshape(-1)
        listed_cols = jnp.repeat(table_row >= 0, BLK)
        allowed = listed_cols[None, :] & (key_pos[None, :] <= query_pos[:, None])
        scores = jnp.einsum("ahd,chd->hac", query_rows, key_rows) * score_scale
        scores = jnp.where(allowed[None], scores, -jnp.inf)
        row_top = jnp.max(scores, axis=-1, keepdims=True)
        log_total = row_top + jnp.log(jnp.sum(jnp.exp(scores - row_top), axis=-1, keepdims=True))
        weights = jnp.exp(scores - log_total)
        weights_low = lax.optimization_barrier(weights.astype(jnp.bfloat16)).astype(jnp.float32)
        out_rows = jnp.einsum("hac,chd->ahd", weights_low, value_rows).astype(jnp.bfloat16)
        out_back = lax.optimization_barrier(out_rows).astype(jnp.float32)
        delta_rows = jnp.transpose(jnp.sum(out_back * grad_rows, axis=-1))[:, :, None]
        grad_weights = jnp.einsum("ahd,chd->hac", grad_rows, value_rows)
        dscore = lax.optimization_barrier((score_scale * weights * (grad_weights - delta_rows)).astype(jnp.bfloat16)).astype(jnp.float32)
        query_part = jnp.einsum("hac,chd->ahd", dscore, key_rows).astype(jnp.bfloat16)
        key_part = jnp.einsum("hac,ahd->chd", dscore, query_rows).reshape(table_width, BLK, HEADS, HD)
        value_part = jnp.einsum("hac,ahd->chd", weights_low, grad_rows).reshape(table_width, BLK, HEADS, HD)
        key_total = key_total.at[safe_row].add(key_part)
        value_total = value_total.at[safe_row].add(value_part)
        return (key_total, value_total), (out_rows, query_part)

    zeros_grad = jnp.zeros((block_count, BLK, HEADS, HD), jnp.float32)
    totals, outputs = lax.scan(block_step, (zeros_grad, zeros_grad), jnp.arange(block_count, dtype=jnp.int32))
    out_blocks, query_parts = outputs
    attn_out = out_blocks.reshape(TOKENS, HEADS * HD)
    proj_grad = jnp.dot(out_grad.T, attn_out, preferred_element_type=jnp.float32)
    query_grad = query_parts.reshape(TOKENS, HEADS * HD)
    key_grad = totals[0].reshape(TOKENS, HEADS * HD).astype(jnp.bfloat16)
    value_grad = totals[1].reshape(TOKENS, HEADS * HD).astype(jnp.bfloat16)
    return (query_grad, key_grad, value_grad, proj_grad)
```

```python
import jax
import jax.numpy as jnp
from jax import lax
from jax.sharding import PartitionSpec as P

HD = 128
BLK = 128
LOCAL = 8
STRIDE = 16


def passed_along(block, axis, distance):
    devices = range(lax.axis_size(axis))
    route = [(i - distance, i) for i in devices if i - distance in devices]
    return lax.ppermute(block, axis, route)


def listed(table_rows, block_ids):
    hit = jnp.any(table_rows[:, None, :] == block_ids[:, :, None], axis=2)
    return hit & (block_ids >= 0)


def local(queries, keys, values, out_grad, proj_weight, layout):
    tok_dev = queries.shape[0]
    width = queries.shape[1]
    heads_here = width // HD
    blocks_dev = tok_dev // BLK
    block_count = layout.shape[0]
    summary_count = block_count // STRIDE
    score_scale = HD ** (-0.5)
    me = lax.axis_index("seq")
    first_block = me * blocks_dev
    offset_block = layout[block_count - 1, 0] % STRIDE
    reach_back = (LOCAL - 2) // blocks_dev + 1
    span_blocks = [
        min(blocks_dev, LOCAL - 1 - hop_index * blocks_dev) for hop_index in range(reach_back)
    ]
    back_blocks = sum(span_blocks)
    pool_blocks = back_blocks + blocks_dev

    attn_grad = jnp.dot(out_grad, proj_weight, preferred_element_type=jnp.float32).astype(
        jnp.bfloat16
    )
    kv = jnp.concatenate([keys, values], axis=1)

    near = []
    for distance in range(reach_back, 0, -1):
        rows_needed = span_blocks[distance - 1] * BLK
        near.append(passed_along(kv[tok_dev - rows_needed :], "seq", distance))
    pool_kv = jnp.concatenate(near + [kv], axis=0)

    far_ids = jnp.arange(summary_count, dtype=jnp.int32) * STRIDE + offset_block
    far_owner = far_ids // blocks_dev
    far_local = far_ids % blocks_dev
    kv_blocks = kv.reshape(blocks_dev, BLK, 2 * width)
    far_mine = jnp.where(
        (far_owner == me)[:, None, None], jnp.take(kv_blocks, far_local, axis=0), jnp.zeros_like(kv_blocks[:1])
    ).reshape(summary_count * BLK, 2 * width)
    far_part = lax.psum_scatter(far_mine, "seq", scatter_dimension=0, tiled=True)
    far_kv = lax.all_gather(far_part, "seq", axis=0, tiled=True)

    all_kv = jnp.concatenate([pool_kv, far_kv], axis=0)
    key_rows = all_kv[:, :width].reshape(-1, heads_here, HD)
    value_rows = all_kv[:, width:].reshape(-1, heads_here, HD)
    query_rows = queries.reshape(tok_dev, heads_here, HD)
    grad_rows = attn_grad.reshape(tok_dev, heads_here, HD)

    own_ids = first_block + jnp.arange(blocks_dev, dtype=jnp.int32)
    table_rows = lax.dynamic_slice_in_dim(layout, first_block, blocks_dev, 0)
    pool_ids = first_block - back_blocks + jnp.arange(pool_blocks, dtype=jnp.int32)
    pool_ids_b = jnp.broadcast_to(pool_ids[None, :], (blocks_dev, pool_blocks))
    plain = (pool_ids_b % STRIDE != offset_block) | (pool_ids_b == own_ids[:, None])
    pool_ok = listed(table_rows, pool_ids_b) & plain
    far_ids_b = jnp.broadcast_to(far_ids[None, :], (blocks_dev, summary_count))
    far_ok = listed(table_rows, far_ids_b) & (far_ids_b < own_ids[:, None])
    block_ok = jnp.concatenate([pool_ok, far_ok], axis=1)
    token_ok = jnp.repeat(jnp.repeat(block_ok, BLK, axis=0), BLK, axis=1)
    query_pos = jnp.arange(tok_dev, dtype=jnp.int32)
    pool_pos = jnp.arange(pool_blocks * BLK, dtype=jnp.int32) - back_blocks * BLK
    causal = jnp.concatenate(
        [
            pool_pos[None, :] <= query_pos[:, None],
            jnp.ones((tok_dev, summary_count * BLK), jnp.bool_),
        ],
        axis=1,
    )
    allowed = token_ok & causal

    scores = (
        jnp.einsum("qhd,khd->hqk", query_rows, key_rows, preferred_element_type=jnp.float32)
        * score_scale
    )
    scores = jnp.where(allowed[None], scores, -jnp.inf)
    row_top = jnp.max(scores, axis=-1, keepdims=True)
    log_total = row_top + jnp.log(jnp.sum(jnp.exp(scores - row_top), axis=-1, keepdims=True))
    probs = jnp.exp(scores - log_total)
    probs_low = probs.astype(jnp.bfloat16)
    attn_out = jnp.einsum(
        "hqk,khd->qhd", probs_low, value_rows, preferred_element_type=jnp.float32
    ).astype(jnp.bfloat16)
    delta = jnp.transpose(
        jnp.sum(attn_out.astype(jnp.float32) * grad_rows.astype(jnp.float32), axis=-1)
    )[..., None]
    dprobs = jnp.einsum("qhd,khd->hqk", grad_rows, value_rows, preferred_element_type=jnp.float32)
    dscores = (score_scale * probs * (dprobs - delta)).astype(jnp.bfloat16)
    query_grad = jnp.einsum(
        "hqk,khd->qhd", dscores, key_rows, preferred_element_type=jnp.float32
    ).astype(jnp.bfloat16)
    key_part = jnp.einsum("hqk,qhd->khd", dscores, query_rows, preferred_element_type=jnp.float32)
    value_part = jnp.einsum(
        "hqk,qhd->khd", probs_low, grad_rows, preferred_element_type=jnp.float32
    )
    grad_kv = jnp.concatenate(
        [key_part.reshape(-1, width), value_part.reshape(-1, width)], axis=1
    )

    far_grad = grad_kv[pool_blocks * BLK :]
    far_sum = lax.all_gather(
        lax.psum_scatter(far_grad, "seq", scatter_dimension=0, tiled=True), "seq", axis=0, tiled=True
    ).reshape(summary_count, BLK, 2 * width)
    is_summary = own_ids % STRIDE == offset_block
    summary_slot = jnp.minimum(own_ids // STRIDE, summary_count - 1)
    far_add = jnp.where(is_summary[:, None, None], jnp.take(far_sum, summary_slot, axis=0), 0.0)

    own_grad = grad_kv[back_blocks * BLK : pool_blocks * BLK]
    pool_start = 0
    for distance in range(reach_back, 0, -1):
        rows_needed = span_blocks[distance - 1] * BLK
        back = passed_along(grad_kv[pool_start : pool_start + rows_needed], "seq", -distance)
        own_grad = own_grad.at[tok_dev - rows_needed :].add(back)
        pool_start = pool_start + rows_needed
    total = own_grad.reshape(blocks_dev, BLK, 2 * width) + far_add
    total = total.reshape(tok_dev, 2 * width).astype(jnp.bfloat16)

    proj_grad = lax.psum_scatter(
        lax.dot_general(
            out_grad,
            attn_out.reshape(tok_dev, width),
            (((0,), (0,)), ((), ())),
            preferred_element_type=jnp.float32,
        ),
        "seq",
        scatter_dimension=0,
        tiled=True,
    )
    return (
        query_grad.reshape(tok_dev, width),
        total[:, :width],
        total[:, width:],
        proj_grad,
    )


def solution(mesh):
    return jax.shard_map(
        local,
        mesh=mesh,
        in_specs=(
            P(("dp", "seq"), "head"),
            P(("dp", "seq"), "head"),
            P(("dp", "seq"), "head"),
            P(("dp", "seq"), None),
            P(None, "head"),
            P(),
        ),
        out_specs=(
            P(("dp", "seq"), "head"),
            P(("dp", "seq"), "head"),
            P(("dp", "seq"), "head"),
            P(("dp", "seq"), "head"),
        ),
        check_vma=False,
    )
```

```python
import jax
import jax.numpy as jnp
from jax import lax
from jax.sharding import PartitionSpec as P

HD = 128
BLK = 128
LOCAL = 8
STRIDE = 16


def passed_along(block, axis, distance):
    devices = range(lax.axis_size(axis))
    route = [(i - distance, i) for i in devices if i - distance in devices]
    return lax.ppermute(block, axis, route)


def listed(table_rows, block_ids):
    hit = jnp.any(table_rows[:, None, :] == block_ids[:, :, None], axis=2)
    return hit & (block_ids >= 0)


def local(queries, keys, values, out_grad, proj_weight, layout):
    tok_dev = queries.shape[0]
    width = queries.shape[1]
    heads_here = width // HD
    blocks_dev = tok_dev // BLK
    block_count = layout.shape[0]
    summary_count = block_count // STRIDE
    score_scale = HD ** (-0.5)
    me = lax.axis_index("seq")
    first_block = me * blocks_dev
    offset_block = layout[block_count - 1, 0] % STRIDE
    reach_back = (LOCAL - 2) // blocks_dev + 1
    span_blocks = [
        min(blocks_dev, LOCAL - 1 - hop_index * blocks_dev) for hop_index in range(reach_back)
    ]
    back_blocks = sum(span_blocks)
    pool_blocks = back_blocks + blocks_dev

    attn_grad = jnp.dot(out_grad, proj_weight, preferred_element_type=jnp.float32).astype(
        jnp.bfloat16
    )
    kv = jnp.concatenate([keys, values], axis=1)

    near = []
    for distance in range(reach_back, 0, -1):
        rows_needed = span_blocks[distance - 1] * BLK
        near.append(passed_along(kv[tok_dev - rows_needed :], "seq", distance))
    pool_kv = jnp.concatenate(near + [kv], axis=0)

    seq_size = lax.axis_size("seq")
    group = STRIDE // blocks_dev
    groups = seq_size // group
    assert groups == summary_count and blocks_dev <= STRIDE
    far_ids = jnp.arange(summary_count, dtype=jnp.int32) * STRIDE + offset_block
    lead = offset_block // blocks_dev
    sum_local = offset_block % blocks_dev
    in_group = me % group
    my_group = me // group
    rel = (in_group - lead) % group
    held = lax.dynamic_index_in_dim(kv.reshape(blocks_dev, BLK, 2 * width), sum_local, 0, keepdims=False)
    hop = 1
    while hop < group:
        route = [(g * group + (r - hop) % group, g * group + r) for g in range(groups) for r in range(group)]
        moved = lax.ppermute(held, "seq", route)
        held = jnp.where((rel >= hop) & (rel < 2 * hop), moved, held)
        hop *= 2
    gathered = held[None]
    span = 1
    while span < groups:
        route = [(d, d ^ (span * group)) for d in range(seq_size)]
        moved = lax.ppermute(gathered, "seq", route)
        upper = (my_group // span) % 2 == 1
        gathered = jnp.where(
            upper, jnp.concatenate([moved, gathered], 0), jnp.concatenate([gathered, moved], 0)
        )
        span *= 2
    far_kv = gathered.reshape(summary_count * BLK, 2 * width)

    all_kv = jnp.concatenate([pool_kv, far_kv], axis=0)
    key_rows = all_kv[:, :width].reshape(-1, heads_here, HD)
    value_rows = all_kv[:, width:].reshape(-1, heads_here, HD)
    query_rows = queries.reshape(tok_dev, heads_here, HD)
    grad_rows = attn_grad.reshape(tok_dev, heads_here, HD)

    own_ids = first_block + jnp.arange(blocks_dev, dtype=jnp.int32)
    table_rows = lax.dynamic_slice_in_dim(layout, first_block, blocks_dev, 0)
    pool_ids = first_block - back_blocks + jnp.arange(pool_blocks, dtype=jnp.int32)
    pool_ids_b = jnp.broadcast_to(pool_ids[None, :], (blocks_dev, pool_blocks))
    plain = (pool_ids_b % STRIDE != offset_block) | (pool_ids_b == own_ids[:, None])
    pool_ok = listed(table_rows, pool_ids_b) & plain
    far_ids_b = jnp.broadcast_to(far_ids[None, :], (blocks_dev, summary_count))
    far_ok = listed(table_rows, far_ids_b) & (far_ids_b < own_ids[:, None])
    block_ok = jnp.concatenate([pool_ok, far_ok], axis=1)
    token_ok = jnp.repeat(jnp.repeat(block_ok, BLK, axis=0), BLK, axis=1)
    query_pos = jnp.arange(tok_dev, dtype=jnp.int32)
    pool_pos = jnp.arange(pool_blocks * BLK, dtype=jnp.int32) - back_blocks * BLK
    causal = jnp.concatenate(
        [
            pool_pos[None, :] <= query_pos[:, None],
            jnp.ones((tok_dev, summary_count * BLK), jnp.bool_),
        ],
        axis=1,
    )
    allowed = token_ok & causal

    scores = (
        jnp.einsum("qhd,khd->hqk", query_rows, key_rows, preferred_element_type=jnp.float32)
        * score_scale
    )
    scores = jnp.where(allowed[None], scores, -jnp.inf)
    row_top = jnp.max(scores, axis=-1, keepdims=True)
    log_total = row_top + jnp.log(jnp.sum(jnp.exp(scores - row_top), axis=-1, keepdims=True))
    probs = jnp.exp(scores - log_total)
    probs_low = probs.astype(jnp.bfloat16)
    attn_out = jnp.einsum(
        "hqk,khd->qhd", probs_low, value_rows, preferred_element_type=jnp.float32
    ).astype(jnp.bfloat16)
    delta = jnp.transpose(
        jnp.sum(attn_out.astype(jnp.float32) * grad_rows.astype(jnp.float32), axis=-1)
    )[..., None]
    dprobs = jnp.einsum("qhd,khd->hqk", grad_rows, value_rows, preferred_element_type=jnp.float32)
    dscores = (score_scale * probs * (dprobs - delta)).astype(jnp.bfloat16)
    query_grad = jnp.einsum(
        "hqk,khd->qhd", dscores, key_rows, preferred_element_type=jnp.float32
    ).astype(jnp.bfloat16)
    key_part = jnp.einsum("hqk,qhd->khd", dscores, query_rows, preferred_element_type=jnp.float32)
    value_part = jnp.einsum(
        "hqk,qhd->khd", probs_low, grad_rows, preferred_element_type=jnp.float32
    )
    grad_kv = jnp.concatenate(
        [key_part.reshape(-1, width), value_part.reshape(-1, width)], axis=1
    )

    part = grad_kv[pool_blocks * BLK :].reshape(summary_count, BLK, 2 * width)
    span = groups // 2
    while span >= 1:
        half = part.shape[0] // 2
        upper = (my_group // span) % 2 == 1
        keep = jnp.where(upper, part[half:], part[:half])
        send = jnp.where(upper, part[:half], part[half:])
        route = [(d, d ^ (span * group)) for d in range(seq_size)]
        part = keep + lax.ppermute(send, "seq", route)
        span //= 2
    part = part[0]
    hop = group // 2
    while hop >= 1:
        route = [(g * group + (r + hop) % group, g * group + r) for g in range(groups) for r in range(group)]
        moved = lax.ppermute(part, "seq", route)
        part = jnp.where(rel < hop, part + moved, part)
        hop //= 2
    own_local = jnp.arange(blocks_dev, dtype=jnp.int32)
    far_here = (rel == 0) & (own_local == sum_local)
    far_add = jnp.where(far_here[:, None, None], part[None], 0.0)

    own_grad = grad_kv[back_blocks * BLK : pool_blocks * BLK]
    pool_start = 0
    for distance in range(reach_back, 0, -1):
        rows_needed = span_blocks[distance - 1] * BLK
        back = passed_along(grad_kv[pool_start : pool_start + rows_needed], "seq", -distance)
        own_grad = own_grad.at[tok_dev - rows_needed :].add(back)
        pool_start = pool_start + rows_needed
    total = own_grad.reshape(blocks_dev, BLK, 2 * width) + far_add
    total = total.reshape(tok_dev, 2 * width).astype(jnp.bfloat16)

    proj_grad = lax.psum_scatter(
        lax.dot_general(
            out_grad,
            attn_out.reshape(tok_dev, width),
            (((0,), (0,)), ((), ())),
            preferred_element_type=jnp.float32,
        ),
        "seq",
        scatter_dimension=0,
        tiled=True,
    )
    return (
        query_grad.reshape(tok_dev, width),
        total[:, :width],
        total[:, width:],
        proj_grad,
    )


def solution(mesh):
    return jax.shard_map(
        local,
        mesh=mesh,
        in_specs=(
            P(("dp", "seq"), "head"),
            P(("dp", "seq"), "head"),
            P(("dp", "seq"), "head"),
            P(("dp", "seq"), None),
            P(None, "head"),
            P(),
        ),
        out_specs=(
            P(("dp", "seq"), "head"),
            P(("dp", "seq"), "head"),
            P(("dp", "seq"), "head"),
            P(("dp", "seq"), "head"),
        ),
        check_vma=False,
    )
```

```python
import jax
import jax.numpy as jnp
from jax import lax
from jax.sharding import PartitionSpec as P

HD = 128
BLK = 128
LOCAL = 8
STRIDE = 16


def passed_along(block, axis, distance):
    devices = range(lax.axis_size(axis))
    route = [(i - distance, i) for i in devices if i - distance in devices]
    return lax.ppermute(block, axis, route)


def listed(table_rows, block_ids):
    hit = jnp.any(table_rows[:, None, :] == block_ids[:, :, None], axis=2)
    return hit & (block_ids >= 0)


def local(queries, keys, values, out_grad, proj_weight, layout):
    tok_dev = queries.shape[0]
    width = queries.shape[1]
    heads_here = width // HD
    blocks_dev = tok_dev // BLK
    block_count = layout.shape[0]
    summary_count = block_count // STRIDE
    score_scale = HD ** (-0.5)
    me = lax.axis_index("seq")
    first_block = me * blocks_dev
    offset_block = layout[block_count - 1, 0] % STRIDE
    reach_back = (LOCAL - 2) // blocks_dev + 1
    span_blocks = [
        min(blocks_dev, LOCAL - 1 - hop_index * blocks_dev) for hop_index in range(reach_back)
    ]
    back_blocks = sum(span_blocks)
    pool_blocks = back_blocks + blocks_dev

    attn_grad = jnp.dot(out_grad, proj_weight, preferred_element_type=jnp.float32).astype(
        jnp.bfloat16
    )
    kv = jnp.concatenate([keys, values], axis=1)

    near = []
    for distance in range(reach_back, 0, -1):
        rows_needed = span_blocks[distance - 1] * BLK
        near.append(passed_along(kv[tok_dev - rows_needed :], "seq", distance))
    pool_kv = jnp.concatenate(near + [kv], axis=0)

    seq_size = lax.axis_size("seq")
    group = STRIDE // blocks_dev
    groups = seq_size // group
    assert groups == summary_count and blocks_dev <= STRIDE
    far_ids = jnp.arange(summary_count, dtype=jnp.int32) * STRIDE + offset_block
    lead = offset_block // blocks_dev
    sum_local = offset_block % blocks_dev
    in_group = me % group
    my_group = me // group
    rel = (in_group - lead) % group
    held = lax.dynamic_index_in_dim(kv.reshape(blocks_dev, BLK, 2 * width), sum_local, 0, keepdims=False)
    hop = 1
    while hop < group:
        route = [(g * group + (r - hop) % group, g * group + r) for g in range(groups) for r in range(group)]
        moved = lax.ppermute(held, "seq", route)
        held = jnp.where((rel >= hop) & (rel < 2 * hop), moved, held)
        hop *= 2
    gathered = held[None]
    span = 1
    while span < groups:
        route = [(d, d ^ (span * group)) for d in range(seq_size)]
        moved = lax.ppermute(gathered, "seq", route)
        upper = (my_group // span) % 2 == 1
        gathered = jnp.where(
            upper, jnp.concatenate([moved, gathered], 0), jnp.concatenate([gathered, moved], 0)
        )
        span *= 2
    far_kv = gathered.reshape(summary_count * BLK, 2 * width)

    all_kv = jnp.concatenate([pool_kv, far_kv], axis=0)
    key_rows = all_kv[:, :width].reshape(-1, heads_here, HD)
    value_rows = all_kv[:, width:].reshape(-1, heads_here, HD)
    query_rows = queries.reshape(tok_dev, heads_here, HD)
    grad_rows = attn_grad.reshape(tok_dev, heads_here, HD)

    own_ids = first_block + jnp.arange(blocks_dev, dtype=jnp.int32)
    table_rows = lax.dynamic_slice_in_dim(layout, first_block, blocks_dev, 0)
    pool_ids = first_block - back_blocks + jnp.arange(pool_blocks, dtype=jnp.int32)
    pool_ids_b = jnp.broadcast_to(pool_ids[None, :], (blocks_dev, pool_blocks))
    plain = (pool_ids_b % STRIDE != offset_block) | (pool_ids_b == own_ids[:, None])
    pool_ok = listed(table_rows, pool_ids_b) & plain
    far_ids_b = jnp.broadcast_to(far_ids[None, :], (blocks_dev, summary_count))
    far_ok = listed(table_rows, far_ids_b) & (far_ids_b < own_ids[:, None])
    block_ok = jnp.concatenate([pool_ok, far_ok], axis=1)
    token_ok = jnp.repeat(jnp.repeat(block_ok, BLK, axis=0), BLK, axis=1)
    query_pos = jnp.arange(tok_dev, dtype=jnp.int32)
    pool_pos = jnp.arange(pool_blocks * BLK, dtype=jnp.int32) - back_blocks * BLK
    causal = jnp.concatenate(
        [
            pool_pos[None, :] <= query_pos[:, None],
            jnp.ones((tok_dev, summary_count * BLK), jnp.bool_),
        ],
        axis=1,
    )
    allowed = token_ok & causal

    scores = (
        jnp.einsum("qhd,khd->hqk", query_rows, key_rows, preferred_element_type=jnp.float32)
        * score_scale
    )
    scores = jnp.where(allowed[None], scores, -jnp.inf)
    row_top = jnp.max(scores, axis=-1, keepdims=True)
    log_total = row_top + jnp.log(jnp.sum(jnp.exp(scores - row_top), axis=-1, keepdims=True))
    probs = jnp.exp(scores - log_total)
    probs_low = probs.astype(jnp.bfloat16)
    attn_out = jnp.einsum(
        "hqk,khd->qhd", probs_low, value_rows, preferred_element_type=jnp.float32
    ).astype(jnp.bfloat16)
    delta = jnp.transpose(
        jnp.sum(attn_out.astype(jnp.float32) * grad_rows.astype(jnp.float32), axis=-1)
    )[..., None]
    dprobs = jnp.einsum("qhd,khd->hqk", grad_rows, value_rows, preferred_element_type=jnp.float32)
    dscores = (score_scale * probs * (dprobs - delta)).astype(jnp.bfloat16)
    query_grad = jnp.einsum(
        "hqk,khd->qhd", dscores, key_rows, preferred_element_type=jnp.float32
    ).astype(jnp.bfloat16)
    key_part = jnp.einsum("hqk,qhd->khd", dscores, query_rows, preferred_element_type=jnp.float32)
    value_part = jnp.einsum(
        "hqk,qhd->khd", probs_low, grad_rows, preferred_element_type=jnp.float32
    )
    grad_kv = jnp.concatenate(
        [key_part.reshape(-1, width), value_part.reshape(-1, width)], axis=1
    )

    part = grad_kv[pool_blocks * BLK :].reshape(summary_count, BLK, 2 * width)
    span = groups // 2
    while span >= 1:
        half = part.shape[0] // 2
        upper = (my_group // span) % 2 == 1
        keep = jnp.where(upper, part[half:], part[:half])
        send = jnp.where(upper, part[:half], part[half:])
        route = [(d, d ^ (span * group)) for d in range(seq_size)]
        part = keep + lax.ppermute(send.astype(jnp.bfloat16), "seq", route).astype(jnp.float32)
        span //= 2
    part = part[0]
    hop = group // 2
    while hop >= 1:
        route = [(g * group + (r + hop) % group, g * group + r) for g in range(groups) for r in range(group)]
        moved = lax.ppermute(part.astype(jnp.bfloat16), "seq", route).astype(jnp.float32)
        part = jnp.where(rel < hop, part + moved, part)
        hop //= 2
    own_local = jnp.arange(blocks_dev, dtype=jnp.int32)
    far_here = (rel == 0) & (own_local == sum_local)
    far_add = jnp.where(far_here[:, None, None], part[None], 0.0)

    own_grad = grad_kv[back_blocks * BLK : pool_blocks * BLK]
    pool_start = 0
    for distance in range(reach_back, 0, -1):
        rows_needed = span_blocks[distance - 1] * BLK
        back = passed_along(
            grad_kv[pool_start : pool_start + rows_needed].astype(jnp.bfloat16), "seq", -distance
        ).astype(jnp.float32)
        own_grad = own_grad.at[tok_dev - rows_needed :].add(back)
        pool_start = pool_start + rows_needed
    total = own_grad.reshape(blocks_dev, BLK, 2 * width) + far_add
    total = total.reshape(tok_dev, 2 * width).astype(jnp.bfloat16)

    proj_grad = lax.psum_scatter(
        lax.dot_general(
            out_grad,
            attn_out.reshape(tok_dev, width),
            (((0,), (0,)), ((), ())),
            preferred_element_type=jnp.float32,
        ),
        "seq",
        scatter_dimension=0,
        tiled=True,
    )
    return (
        query_grad.reshape(tok_dev, width),
        total[:, :width],
        total[:, width:],
        proj_grad,
    )


def solution(mesh):
    return jax.shard_map(
        local,
        mesh=mesh,
        in_specs=(
            P(("dp", "seq"), "head"),
            P(("dp", "seq"), "head"),
            P(("dp", "seq"), "head"),
            P(("dp", "seq"), None),
            P(None, "head"),
            P(),
        ),
        out_specs=(
            P(("dp", "seq"), "head"),
            P(("dp", "seq"), "head"),
            P(("dp", "seq"), "head"),
            P(("dp", "seq"), "head"),
        ),
        check_vma=False,
    )
```

```python
import jax
import jax.numpy as jnp
from jax import lax
from jax.sharding import PartitionSpec as P

HD = 128
BLK = 128
LOCAL = 8
STRIDE = 16


def passed_along(block, axis, distance):
    devices = range(lax.axis_size(axis))
    route = [(i - distance, i) for i in devices if i - distance in devices]
    return lax.ppermute(block, axis, route)


def listed(table_rows, block_ids):
    hit = jnp.any(table_rows[:, None, :] == block_ids[:, :, None], axis=2)
    return hit & (block_ids >= 0)


def local(queries, keys, values, out_grad, proj_weight, layout):
    tok_dev = queries.shape[0]
    width = queries.shape[1]
    heads_here = width // HD
    blocks_dev = tok_dev // BLK
    block_count = layout.shape[0]
    summary_count = block_count // STRIDE
    score_scale = HD ** (-0.5)
    me = lax.axis_index("seq")
    first_block = me * blocks_dev
    offset_block = layout[block_count - 1, 0] % STRIDE
    reach_back = (LOCAL - 2) // blocks_dev + 1
    span_blocks = [
        min(blocks_dev, LOCAL - 1 - hop_index * blocks_dev) for hop_index in range(reach_back)
    ]
    back_blocks = sum(span_blocks)
    pool_blocks = back_blocks + blocks_dev

    attn_grad = jnp.dot(out_grad, proj_weight, preferred_element_type=jnp.float32).astype(
        jnp.bfloat16
    )
    kv = jnp.concatenate([keys, values], axis=1)

    near = []
    for distance in range(reach_back, 0, -1):
        rows_needed = span_blocks[distance - 1] * BLK
        near.append(passed_along(kv[tok_dev - rows_needed :], "seq", distance))
    pool_kv = jnp.concatenate(near + [kv], axis=0)

    seq_size = lax.axis_size("seq")
    group = STRIDE // blocks_dev
    groups = seq_size // group
    assert groups == summary_count and blocks_dev <= STRIDE
    far_ids = jnp.arange(summary_count, dtype=jnp.int32) * STRIDE + offset_block
    lead = offset_block // blocks_dev
    sum_local = offset_block % blocks_dev
    in_group = me % group
    my_group = me // group
    rel = (in_group - lead) % group
    held = lax.dynamic_index_in_dim(kv.reshape(blocks_dev, BLK, 2 * width), sum_local, 0, keepdims=False)
    hop = 1
    while hop < group:
        route = [(g * group + (r - hop) % group, g * group + r) for g in range(groups) for r in range(group)]
        moved = lax.ppermute(held, "seq", route)
        held = jnp.where((rel >= hop) & (rel < 2 * hop), moved, held)
        hop *= 2
    gathered = held[None]
    span = 1
    while span < groups:
        route = [(d, d ^ (span * group)) for d in range(seq_size)]
        moved = lax.ppermute(gathered, "seq", route)
        upper = (my_group // span) % 2 == 1
        gathered = jnp.where(
            upper, jnp.concatenate([moved, gathered], 0), jnp.concatenate([gathered, moved], 0)
        )
        span *= 2
    far_kv = gathered.reshape(summary_count * BLK, 2 * width)

    all_kv = jnp.concatenate([pool_kv, far_kv], axis=0)
    key_rows = all_kv[:, :width].reshape(-1, heads_here, HD)
    value_rows = all_kv[:, width:].reshape(-1, heads_here, HD)
    query_rows = queries.reshape(tok_dev, heads_here, HD)
    grad_rows = attn_grad.reshape(tok_dev, heads_here, HD)

    own_ids = first_block + jnp.arange(blocks_dev, dtype=jnp.int32)
    table_rows = lax.dynamic_slice_in_dim(layout, first_block, blocks_dev, 0)
    pool_ids = first_block - back_blocks + jnp.arange(pool_blocks, dtype=jnp.int32)
    pool_ids_b = jnp.broadcast_to(pool_ids[None, :], (blocks_dev, pool_blocks))
    plain = (pool_ids_b % STRIDE != offset_block) | (pool_ids_b == own_ids[:, None])
    pool_ok = listed(table_rows, pool_ids_b) & plain
    far_ids_b = jnp.broadcast_to(far_ids[None, :], (blocks_dev, summary_count))
    far_ok = listed(table_rows, far_ids_b) & (far_ids_b < own_ids[:, None])
    block_ok = jnp.concatenate([pool_ok, far_ok], axis=1)
    token_ok = jnp.repeat(jnp.repeat(block_ok, BLK, axis=0), BLK, axis=1)
    query_pos = jnp.arange(tok_dev, dtype=jnp.int32)
    pool_pos = jnp.arange(pool_blocks * BLK, dtype=jnp.int32) - back_blocks * BLK
    causal = jnp.concatenate(
        [
            pool_pos[None, :] <= query_pos[:, None],
            jnp.ones((tok_dev, summary_count * BLK), jnp.bool_),
        ],
        axis=1,
    )
    allowed = token_ok & causal

    scores = (
        jnp.einsum("qhd,khd->hqk", query_rows, key_rows, preferred_element_type=jnp.float32)
        * score_scale
    )
    scores = jnp.where(allowed[None], scores, -jnp.inf)
    row_top = jnp.max(scores, axis=-1, keepdims=True)
    log_total = row_top + jnp.log(jnp.sum(jnp.exp(scores - row_top), axis=-1, keepdims=True))
    probs = jnp.exp(scores - log_total)
    probs_low = probs.astype(jnp.bfloat16)
    attn_out = jnp.einsum(
        "hqk,khd->qhd", probs_low, value_rows, preferred_element_type=jnp.float32
    ).astype(jnp.bfloat16)
    delta = jnp.transpose(
        jnp.sum(attn_out.astype(jnp.float32) * grad_rows.astype(jnp.float32), axis=-1)
    )[..., None]
    dprobs = jnp.einsum("qhd,khd->hqk", grad_rows, value_rows, preferred_element_type=jnp.float32)
    dscores = (score_scale * probs * (dprobs - delta)).astype(jnp.bfloat16)
    query_grad = jnp.einsum(
        "hqk,khd->qhd", dscores, key_rows, preferred_element_type=jnp.float32
    ).astype(jnp.bfloat16)
    key_part = jnp.einsum("hqk,qhd->khd", dscores, query_rows, preferred_element_type=jnp.float32)
    value_part = jnp.einsum(
        "hqk,qhd->khd", probs_low, grad_rows, preferred_element_type=jnp.float32
    )
    grad_kv = jnp.concatenate(
        [key_part.reshape(-1, width), value_part.reshape(-1, width)], axis=1
    )

    part = grad_kv[pool_blocks * BLK :].reshape(summary_count, BLK, 2 * width)
    span = groups // 2
    while span >= 1:
        half = part.shape[0] // 2
        upper = (my_group // span) % 2 == 1
        keep = jnp.where(upper, part[half:], part[:half])
        send = jnp.where(upper, part[:half], part[half:])
        route = [(d, d ^ (span * group)) for d in range(seq_size)]
        part = keep + lax.ppermute(send.astype(jnp.bfloat16), "seq", route).astype(jnp.float32)
        span //= 2
    part = part[0]
    hop = group // 2
    while hop >= 1:
        route = [(g * group + (r + hop) % group, g * group + r) for g in range(groups) for r in range(group)]
        moved = lax.ppermute(part.astype(jnp.bfloat16), "seq", route).astype(jnp.float32)
        part = jnp.where(rel < hop, part + moved, part)
        hop //= 2
    own_local = jnp.arange(blocks_dev, dtype=jnp.int32)
    far_here = (rel == 0) & (own_local == sum_local)
    far_add = jnp.where(far_here[:, None, None], part[None], 0.0)

    own_grad = grad_kv[back_blocks * BLK : pool_blocks * BLK]
    pool_start = 0
    for distance in range(reach_back, 0, -1):
        rows_needed = span_blocks[distance - 1] * BLK
        back = passed_along(
            grad_kv[pool_start : pool_start + rows_needed].astype(jnp.bfloat16), "seq", -distance
        ).astype(jnp.float32)
        own_grad = own_grad.at[tok_dev - rows_needed :].add(back)
        pool_start = pool_start + rows_needed
    total = own_grad.reshape(blocks_dev, BLK, 2 * width) + far_add
    total = total.reshape(tok_dev, 2 * width).astype(jnp.bfloat16)

    proj_grad = lax.psum_scatter(
        lax.dot_general(
            out_grad,
            attn_out.reshape(tok_dev, width),
            (((0,), (0,)), ((), ())),
            preferred_element_type=jnp.float32,
        ).astype(jnp.bfloat16),
        "seq",
        scatter_dimension=0,
        tiled=True,
    ).astype(jnp.float32)
    return (
        query_grad.reshape(tok_dev, width),
        total[:, :width],
        total[:, width:],
        proj_grad,
    )


def solution(mesh):
    return jax.shard_map(
        local,
        mesh=mesh,
        in_specs=(
            P(("dp", "seq"), "head"),
            P(("dp", "seq"), "head"),
            P(("dp", "seq"), "head"),
            P(("dp", "seq"), None),
            P(None, "head"),
            P(),
        ),
        out_specs=(
            P(("dp", "seq"), "head"),
            P(("dp", "seq"), "head"),
            P(("dp", "seq"), "head"),
            P(("dp", "seq"), "head"),
        ),
        check_vma=False,
    )
```

```python
import functools

import jax
import jax.numpy as jnp
from jax import lax
from jax.experimental import pallas as pl
from jax.experimental.pallas import tpu as pltpu
from jax.sharding import PartitionSpec as P

HD = 128
BLK = 128
LOCAL = 8
STRIDE = 16


def passed_along(block, axis, distance):
    devices = range(lax.axis_size(axis))
    route = [(i - distance, i) for i in devices if i - distance in devices]
    return lax.ppermute(block, axis, route)


def listed(table_rows, block_ids):
    hit = jnp.any(table_rows[:, None, :] == block_ids[:, :, None], axis=2)
    return hit & (block_ids >= 0)


def exchange_kernel(dims, ctl_ref, kv_ref, win_out, far_out, win_buf, hop_buf, cross1, cross2, held, pair, sends, recvs):
    seq_size, group, spans = dims
    groups = seq_size // group
    me = lax.axis_index("seq")
    in_group = me % group
    base = me - in_group
    my_group = me // group
    lead = ctl_ref[0]
    sum_local = ctl_ref[1]
    rel = (in_group - lead + group) % group
    mesh_id = pl.DeviceIdType.MESH

    def ring(step):
        return (me + step + seq_size) % seq_size

    def in_ring(step):
        return base + (in_group + step + group) % group

    def across(span):
        upper = (my_group // span) % 2
        return me + span * group - 2 * span * group * upper

    barrier = pltpu.get_barrier_semaphore()
    partners = []
    for distance in range(1, len(spans) + 1):
        partners += [ring(distance), ring(-distance)]
    hop = 1
    while hop < group:
        partners += [in_ring(hop), in_ring(-hop)]
        hop *= 2
    span = 1
    while span < groups:
        partners += [across(span), across(span)]
        span *= 2
    for partner in partners:
        pl.semaphore_signal(barrier, 1, device_id={"seq": partner}, device_id_type=mesh_id)
    pl.semaphore_wait(barrier, len(partners))

    tok_dev = kv_ref.shape[0]
    window = []
    start = 0
    for distance in range(len(spans), 0, -1):
        rows = spans[distance - 1] * BLK
        copy = pltpu.make_async_remote_copy(
            src_ref=kv_ref.at[pl.ds(tok_dev - rows, rows)],
            dst_ref=win_buf.at[pl.ds(start, rows)],
            send_sem=sends.at[distance - 1],
            recv_sem=recvs.at[distance - 1],
            device_id={"seq": ring(distance)},
            device_id_type=mesh_id,
        )
        copy.start()
        window.append(copy)
        start += rows

    mine = kv_ref[0:BLK, :]
    for block in range(1, tok_dev // BLK):
        mine = jnp.where(sum_local == block, kv_ref[block * BLK : (block + 1) * BLK, :], mine)
    held[...] = mine
    slot = len(spans)
    hop = 1
    stage = 0
    while hop < group:
        copy = pltpu.make_async_remote_copy(
            src_ref=held,
            dst_ref=hop_buf.at[stage],
            send_sem=sends.at[slot],
            recv_sem=recvs.at[slot],
            device_id={"seq": in_ring(hop)},
            device_id_type=mesh_id,
        )
        copy.start()
        copy.wait()
        take = (rel >= hop) & (rel < 2 * hop)
        held[...] = jnp.where(take, hop_buf[stage], held[...])
        slot += 1
        stage += 1
        hop *= 2

    copy = pltpu.make_async_remote_copy(
        src_ref=held,
        dst_ref=cross1,
        send_sem=sends.at[slot],
        recv_sem=recvs.at[slot],
        device_id={"seq": across(1)},
        device_id_type=mesh_id,
    )
    copy.start()
    copy.wait()
    upper = (my_group % 2) == 1
    pair[0] = jnp.where(upper, cross1[...], held[...])
    pair[1] = jnp.where(upper, held[...], cross1[...])
    slot += 1
    copy = pltpu.make_async_remote_copy(
        src_ref=pair,
        dst_ref=cross2,
        send_sem=sends.at[slot],
        recv_sem=recvs.at[slot],
        device_id={"seq": across(2)},
        device_id_type=mesh_id,
    )
    copy.start()
    copy.wait()
    upper = ((my_group // 2) % 2) == 1
    for index in range(2):
        far_out[index] = jnp.where(upper, cross2[index], pair[index])
        far_out[2 + index] = jnp.where(upper, pair[index], cross2[index])
    for copy in window:
        copy.wait()
    win_out[...] = win_buf[...]


def exchange(kv, lead, sum_local, spans, seq_size, group):
    tok_dev, cols = kv.shape
    back_rows = sum(spans) * BLK
    groups = seq_size // group
    copies = len(spans) + 5
    ctl = jnp.stack([lead, sum_local]).astype(jnp.int32)
    return pl.pallas_call(
        functools.partial(exchange_kernel, (seq_size, group, spans)),
        out_shape=(
            jax.ShapeDtypeStruct((back_rows, cols), kv.dtype),
            jax.ShapeDtypeStruct((groups, BLK, cols), kv.dtype),
        ),
        in_specs=[
            pl.BlockSpec(memory_space=pltpu.SMEM),
            pl.BlockSpec(memory_space=pltpu.VMEM),
        ],
        out_specs=(
            pl.BlockSpec(memory_space=pltpu.VMEM),
            pl.BlockSpec(memory_space=pltpu.VMEM),
        ),
        scratch_shapes=[
            pltpu.VMEM((back_rows, cols), kv.dtype),
            pltpu.VMEM((3, BLK, cols), kv.dtype),
            pltpu.VMEM((BLK, cols), kv.dtype),
            pltpu.VMEM((2, BLK, cols), kv.dtype),
            pltpu.VMEM((BLK, cols), kv.dtype),
            pltpu.VMEM((2, BLK, cols), kv.dtype),
            pltpu.SemaphoreType.DMA((copies,)),
            pltpu.SemaphoreType.DMA((copies,)),
        ],
        compiler_params=pltpu.CompilerParams(
            collective_id=0, has_side_effects=True, vmem_limit_bytes=48 * 1024 * 1024
        ),
    )(ctl, kv)


def local(queries, keys, values, out_grad, proj_weight, layout):
    tok_dev = queries.shape[0]
    width = queries.shape[1]
    heads_here = width // HD
    blocks_dev = tok_dev // BLK
    block_count = layout.shape[0]
    summary_count = block_count // STRIDE
    score_scale = HD ** (-0.5)
    me = lax.axis_index("seq")
    first_block = me * blocks_dev
    offset_block = layout[block_count - 1, 0] % STRIDE
    reach_back = (LOCAL - 2) // blocks_dev + 1
    span_blocks = [
        min(blocks_dev, LOCAL - 1 - hop_index * blocks_dev) for hop_index in range(reach_back)
    ]
    back_blocks = sum(span_blocks)
    pool_blocks = back_blocks + blocks_dev

    attn_grad = jnp.dot(out_grad, proj_weight, preferred_element_type=jnp.float32).astype(
        jnp.bfloat16
    )
    kv = jnp.concatenate([keys, values], axis=1)

    seq_size = lax.axis_size("seq")
    group = STRIDE // blocks_dev
    groups = seq_size // group
    assert groups == summary_count == 4 and group == 8
    far_ids = jnp.arange(summary_count, dtype=jnp.int32) * STRIDE + offset_block
    lead = offset_block // blocks_dev
    sum_local = offset_block % blocks_dev
    in_group = me % group
    my_group = me // group
    rel = (in_group - lead) % group
    win_kv, far_blocks = exchange(kv, lead, sum_local, span_blocks, seq_size, group)
    pool_kv = jnp.concatenate([win_kv, kv], axis=0)
    far_kv = far_blocks.reshape(summary_count * BLK, 2 * width)

    all_kv = jnp.concatenate([pool_kv, far_kv], axis=0)
    key_rows = all_kv[:, :width].reshape(-1, heads_here, HD)
    value_rows = all_kv[:, width:].reshape(-1, heads_here, HD)
    query_rows = queries.reshape(tok_dev, heads_here, HD)
    grad_rows = attn_grad.reshape(tok_dev, heads_here, HD)

    own_ids = first_block + jnp.arange(blocks_dev, dtype=jnp.int32)
    table_rows = lax.dynamic_slice_in_dim(layout, first_block, blocks_dev, 0)
    pool_ids = first_block - back_blocks + jnp.arange(pool_blocks, dtype=jnp.int32)
    pool_ids_b = jnp.broadcast_to(pool_ids[None, :], (blocks_dev, pool_blocks))
    plain = (pool_ids_b % STRIDE != offset_block) | (pool_ids_b == own_ids[:, None])
    pool_ok = listed(table_rows, pool_ids_b) & plain
    far_ids_b = jnp.broadcast_to(far_ids[None, :], (blocks_dev, summary_count))
    far_ok = listed(table_rows, far_ids_b) & (far_ids_b < own_ids[:, None])
    block_ok = jnp.concatenate([pool_ok, far_ok], axis=1)
    token_ok = jnp.repeat(jnp.repeat(block_ok, BLK, axis=0), BLK, axis=1)
    query_pos = jnp.arange(tok_dev, dtype=jnp.int32)
    pool_pos = jnp.arange(pool_blocks * BLK, dtype=jnp.int32) - back_blocks * BLK
    causal = jnp.concatenate(
        [
            pool_pos[None, :] <= query_pos[:, None],
            jnp.ones((tok_dev, summary_count * BLK), jnp.bool_),
        ],
        axis=1,
    )
    allowed = token_ok & causal

    scores = (
        jnp.einsum("qhd,khd->hqk", query_rows, key_rows, preferred_element_type=jnp.float32)
        * score_scale
    )
    scores = jnp.where(allowed[None], scores, -jnp.inf)
    row_top = jnp.max(scores, axis=-1, keepdims=True)
    log_total = row_top + jnp.log(jnp.sum(jnp.exp(scores - row_top), axis=-1, keepdims=True))
    probs = jnp.exp(scores - log_total)
    probs_low = probs.astype(jnp.bfloat16)
    attn_out = jnp.einsum(
        "hqk,khd->qhd", probs_low, value_rows, preferred_element_type=jnp.float32
    ).astype(jnp.bfloat16)
    delta = jnp.transpose(
        jnp.sum(attn_out.astype(jnp.float32) * grad_rows.astype(jnp.float32), axis=-1)
    )[..., None]
    dprobs = jnp.einsum("qhd,khd->hqk", grad_rows, value_rows, preferred_element_type=jnp.float32)
    dscores = (score_scale * probs * (dprobs - delta)).astype(jnp.bfloat16)
    query_grad = jnp.einsum(
        "hqk,khd->qhd", dscores, key_rows, preferred_element_type=jnp.float32
    ).astype(jnp.bfloat16)
    key_part = jnp.einsum("hqk,qhd->khd", dscores, query_rows, preferred_element_type=jnp.float32)
    value_part = jnp.einsum(
        "hqk,qhd->khd", probs_low, grad_rows, preferred_element_type=jnp.float32
    )
    grad_kv = jnp.concatenate(
        [key_part.reshape(-1, width), value_part.reshape(-1, width)], axis=1
    )

    part = grad_kv[pool_blocks * BLK :].reshape(summary_count, BLK, 2 * width)
    span = groups // 2
    while span >= 1:
        half = part.shape[0] // 2
        upper = (my_group // span) % 2 == 1
        keep = jnp.where(upper, part[half:], part[:half])
        send = jnp.where(upper, part[:half], part[half:])
        route = [(d, d ^ (span * group)) for d in range(seq_size)]
        part = keep + lax.ppermute(send.astype(jnp.bfloat16), "seq", route).astype(jnp.float32)
        span //= 2
    part = part[0]
    hop = group // 2
    while hop >= 1:
        route = [(g * group + (r + hop) % group, g * group + r) for g in range(groups) for r in range(group)]
        moved = lax.ppermute(part.astype(jnp.bfloat16), "seq", route).astype(jnp.float32)
        part = jnp.where(rel < hop, part + moved, part)
        hop //= 2
    own_local = jnp.arange(blocks_dev, dtype=jnp.int32)
    far_here = (rel == 0) & (own_local == sum_local)
    far_add = jnp.where(far_here[:, None, None], part[None], 0.0)

    own_grad = grad_kv[back_blocks * BLK : pool_blocks * BLK]
    pool_start = 0
    for distance in range(reach_back, 0, -1):
        rows_needed = span_blocks[distance - 1] * BLK
        back = passed_along(
            grad_kv[pool_start : pool_start + rows_needed].astype(jnp.bfloat16), "seq", -distance
        ).astype(jnp.float32)
        own_grad = own_grad.at[tok_dev - rows_needed :].add(back)
        pool_start = pool_start + rows_needed
    total = own_grad.reshape(blocks_dev, BLK, 2 * width) + far_add
    total = total.reshape(tok_dev, 2 * width).astype(jnp.bfloat16)

    proj_grad = lax.psum_scatter(
        lax.dot_general(
            out_grad,
            attn_out.reshape(tok_dev, width),
            (((0,), (0,)), ((), ())),
            preferred_element_type=jnp.float32,
        ),
        "seq",
        scatter_dimension=0,
        tiled=True,
    )
    return (
        query_grad.reshape(tok_dev, width),
        total[:, :width],
        total[:, width:],
        proj_grad,
    )


def solution(mesh):
    return jax.shard_map(
        local,
        mesh=mesh,
        in_specs=(
            P(("dp", "seq"), "head"),
            P(("dp", "seq"), "head"),
            P(("dp", "seq"), "head"),
            P(("dp", "seq"), None),
            P(None, "head"),
            P(),
        ),
        out_specs=(
            P(("dp", "seq"), "head"),
            P(("dp", "seq"), "head"),
            P(("dp", "seq"), "head"),
            P(("dp", "seq"), "head"),
        ),
        check_vma=False,
    )
```

```python
import functools

import jax
import jax.numpy as jnp
from jax import lax
from jax.experimental import pallas as pl
from jax.experimental.pallas import tpu as pltpu
from jax.sharding import PartitionSpec as P

HD = 128
BLK = 128
LOCAL = 8
STRIDE = 16


def passed_along(block, axis, distance):
    devices = range(lax.axis_size(axis))
    route = [(i - distance, i) for i in devices if i - distance in devices]
    return lax.ppermute(block, axis, route)


def listed(table_rows, block_ids):
    hit = jnp.any(table_rows[:, None, :] == block_ids[:, :, None], axis=2)
    return hit & (block_ids >= 0)


def exchange_kernel(dims, ctl_ref, kv_ref, win_out, far_out, win_buf, hop_buf, cross1, cross2, held, pair, sends, recvs):
    seq_size, group, spans = dims
    groups = seq_size // group
    me = lax.axis_index("seq")
    in_group = me % group
    base = me - in_group
    my_group = me // group
    lead = ctl_ref[0]
    sum_local = ctl_ref[1]
    rel = (in_group - lead + group) % group
    mesh_id = pl.DeviceIdType.MESH

    def ring(step):
        return (me + step + seq_size) % seq_size

    def in_ring(step):
        return base + (in_group + step + group) % group

    def across(span):
        upper = (my_group // span) % 2
        return me + span * group - 2 * span * group * upper

    barrier = pltpu.get_barrier_semaphore()
    partners = []
    for distance in range(1, len(spans) + 1):
        partners += [ring(distance), ring(-distance)]
    hop = 1
    while hop < group:
        partners += [in_ring(hop), in_ring(-hop)]
        hop *= 2
    span = 1
    while span < groups:
        partners += [across(span), across(span)]
        span *= 2
    for partner in partners:
        pl.semaphore_signal(barrier, 1, device_id={"seq": partner}, device_id_type=mesh_id)
    pl.semaphore_wait(barrier, len(partners))

    tok_dev = kv_ref.shape[0]
    mine = kv_ref[0:BLK, :]
    for block in range(1, tok_dev // BLK):
        mine = jnp.where(sum_local == block, kv_ref[block * BLK : (block + 1) * BLK, :], mine)
    held[...] = mine
    slot = len(spans)
    hop = 1
    stage = 0
    while hop < group:
        copy = pltpu.make_async_remote_copy(
            src_ref=held,
            dst_ref=hop_buf.at[stage],
            send_sem=sends.at[slot],
            recv_sem=recvs.at[slot],
            device_id={"seq": in_ring(hop)},
            device_id_type=mesh_id,
        )
        copy.start()
        copy.wait()
        take = (rel >= hop) & (rel < 2 * hop)
        held[...] = jnp.where(take, hop_buf[stage], held[...])
        slot += 1
        stage += 1
        hop *= 2

    copy = pltpu.make_async_remote_copy(
        src_ref=held,
        dst_ref=cross1,
        send_sem=sends.at[slot],
        recv_sem=recvs.at[slot],
        device_id={"seq": across(1)},
        device_id_type=mesh_id,
    )
    copy.start()
    copy.wait()
    upper = (my_group % 2) == 1
    pair[0] = jnp.where(upper, cross1[...], held[...])
    pair[1] = jnp.where(upper, held[...], cross1[...])
    slot += 1
    window = []
    start = 0
    for distance in range(len(spans), 0, -1):
        rows = spans[distance - 1] * BLK
        copy = pltpu.make_async_remote_copy(
            src_ref=kv_ref.at[pl.ds(tok_dev - rows, rows)],
            dst_ref=win_buf.at[pl.ds(start, rows)],
            send_sem=sends.at[distance - 1],
            recv_sem=recvs.at[distance - 1],
            device_id={"seq": ring(distance)},
            device_id_type=mesh_id,
        )
        copy.start()
        window.append(copy)
        start += rows

    copy = pltpu.make_async_remote_copy(
        src_ref=pair,
        dst_ref=cross2,
        send_sem=sends.at[slot],
        recv_sem=recvs.at[slot],
        device_id={"seq": across(2)},
        device_id_type=mesh_id,
    )
    copy.start()
    copy.wait()
    upper = ((my_group // 2) % 2) == 1
    for index in range(2):
        far_out[index] = jnp.where(upper, cross2[index], pair[index])
        far_out[2 + index] = jnp.where(upper, pair[index], cross2[index])
    for copy in window:
        copy.wait()
    win_out[...] = win_buf[...]


def exchange(kv, lead, sum_local, spans, seq_size, group):
    tok_dev, cols = kv.shape
    back_rows = sum(spans) * BLK
    groups = seq_size // group
    copies = len(spans) + 5
    ctl = jnp.stack([lead, sum_local]).astype(jnp.int32)
    return pl.pallas_call(
        functools.partial(exchange_kernel, (seq_size, group, spans)),
        out_shape=(
            jax.ShapeDtypeStruct((back_rows, cols), kv.dtype),
            jax.ShapeDtypeStruct((groups, BLK, cols), kv.dtype),
        ),
        in_specs=[
            pl.BlockSpec(memory_space=pltpu.SMEM),
            pl.BlockSpec(memory_space=pltpu.VMEM),
        ],
        out_specs=(
            pl.BlockSpec(memory_space=pltpu.VMEM),
            pl.BlockSpec(memory_space=pltpu.VMEM),
        ),
        scratch_shapes=[
            pltpu.VMEM((back_rows, cols), kv.dtype),
            pltpu.VMEM((3, BLK, cols), kv.dtype),
            pltpu.VMEM((BLK, cols), kv.dtype),
            pltpu.VMEM((2, BLK, cols), kv.dtype),
            pltpu.VMEM((BLK, cols), kv.dtype),
            pltpu.VMEM((2, BLK, cols), kv.dtype),
            pltpu.SemaphoreType.DMA((copies,)),
            pltpu.SemaphoreType.DMA((copies,)),
        ],
        compiler_params=pltpu.CompilerParams(
            collective_id=0, has_side_effects=True, vmem_limit_bytes=48 * 1024 * 1024
        ),
    )(ctl, kv)


def local(queries, keys, values, out_grad, proj_weight, layout):
    tok_dev = queries.shape[0]
    width = queries.shape[1]
    heads_here = width // HD
    blocks_dev = tok_dev // BLK
    block_count = layout.shape[0]
    summary_count = block_count // STRIDE
    score_scale = HD ** (-0.5)
    me = lax.axis_index("seq")
    first_block = me * blocks_dev
    offset_block = layout[block_count - 1, 0] % STRIDE
    reach_back = (LOCAL - 2) // blocks_dev + 1
    span_blocks = [
        min(blocks_dev, LOCAL - 1 - hop_index * blocks_dev) for hop_index in range(reach_back)
    ]
    back_blocks = sum(span_blocks)
    pool_blocks = back_blocks + blocks_dev

    attn_grad = jnp.dot(out_grad, proj_weight, preferred_element_type=jnp.float32).astype(
        jnp.bfloat16
    )
    kv = jnp.concatenate([keys, values], axis=1)

    seq_size = lax.axis_size("seq")
    group = STRIDE // blocks_dev
    groups = seq_size // group
    assert groups == summary_count == 4 and group == 8
    far_ids = jnp.arange(summary_count, dtype=jnp.int32) * STRIDE + offset_block
    lead = offset_block // blocks_dev
    sum_local = offset_block % blocks_dev
    in_group = me % group
    my_group = me // group
    rel = (in_group - lead) % group
    win_kv, far_blocks = exchange(kv, lead, sum_local, span_blocks, seq_size, group)
    pool_kv = jnp.concatenate([win_kv, kv], axis=0)
    far_kv = far_blocks.reshape(summary_count * BLK, 2 * width)

    all_kv = jnp.concatenate([pool_kv, far_kv], axis=0)
    key_rows = all_kv[:, :width].reshape(-1, heads_here, HD)
    value_rows = all_kv[:, width:].reshape(-1, heads_here, HD)
    query_rows = queries.reshape(tok_dev, heads_here, HD)
    grad_rows = attn_grad.reshape(tok_dev, heads_here, HD)

    own_ids = first_block + jnp.arange(blocks_dev, dtype=jnp.int32)
    table_rows = lax.dynamic_slice_in_dim(layout, first_block, blocks_dev, 0)
    pool_ids = first_block - back_blocks + jnp.arange(pool_blocks, dtype=jnp.int32)
    pool_ids_b = jnp.broadcast_to(pool_ids[None, :], (blocks_dev, pool_blocks))
    plain = (pool_ids_b % STRIDE != offset_block) | (pool_ids_b == own_ids[:, None])
    pool_ok = listed(table_rows, pool_ids_b) & plain
    far_ids_b = jnp.broadcast_to(far_ids[None, :], (blocks_dev, summary_count))
    far_ok = listed(table_rows, far_ids_b) & (far_ids_b < own_ids[:, None])
    block_ok = jnp.concatenate([pool_ok, far_ok], axis=1)
    token_ok = jnp.repeat(jnp.repeat(block_ok, BLK, axis=0), BLK, axis=1)
    query_pos = jnp.arange(tok_dev, dtype=jnp.int32)
    pool_pos = jnp.arange(pool_blocks * BLK, dtype=jnp.int32) - back_blocks * BLK
    causal = jnp.concatenate(
        [
            pool_pos[None, :] <= query_pos[:, None],
            jnp.ones((tok_dev, summary_count * BLK), jnp.bool_),
        ],
        axis=1,
    )
    allowed = token_ok & causal

    scores = (
        jnp.einsum("qhd,khd->hqk", query_rows, key_rows, preferred_element_type=jnp.float32)
        * score_scale
    )
    scores = jnp.where(allowed[None], scores, -jnp.inf)
    row_top = jnp.max(scores, axis=-1, keepdims=True)
    log_total = row_top + jnp.log(jnp.sum(jnp.exp(scores - row_top), axis=-1, keepdims=True))
    probs = jnp.exp(scores - log_total)
    probs_low = probs.astype(jnp.bfloat16)
    attn_out = jnp.einsum(
        "hqk,khd->qhd", probs_low, value_rows, preferred_element_type=jnp.float32
    ).astype(jnp.bfloat16)
    delta = jnp.transpose(
        jnp.sum(attn_out.astype(jnp.float32) * grad_rows.astype(jnp.float32), axis=-1)
    )[..., None]
    dprobs = jnp.einsum("qhd,khd->hqk", grad_rows, value_rows, preferred_element_type=jnp.float32)
    dscores = (score_scale * probs * (dprobs - delta)).astype(jnp.bfloat16)
    query_grad = jnp.einsum(
        "hqk,khd->qhd", dscores, key_rows, preferred_element_type=jnp.float32
    ).astype(jnp.bfloat16)
    key_part = jnp.einsum("hqk,qhd->khd", dscores, query_rows, preferred_element_type=jnp.float32)
    value_part = jnp.einsum(
        "hqk,qhd->khd", probs_low, grad_rows, preferred_element_type=jnp.float32
    )
    grad_kv = jnp.concatenate(
        [key_part.reshape(-1, width), value_part.reshape(-1, width)], axis=1
    )

    part = grad_kv[pool_blocks * BLK :].reshape(summary_count, BLK, 2 * width)
    span = groups // 2
    while span >= 1:
        half = part.shape[0] // 2
        upper = (my_group // span) % 2 == 1
        keep = jnp.where(upper, part[half:], part[:half])
        send = jnp.where(upper, part[:half], part[half:])
        route = [(d, d ^ (span * group)) for d in range(seq_size)]
        part = keep + lax.ppermute(send.astype(jnp.bfloat16), "seq", route).astype(jnp.float32)
        span //= 2
    part = part[0]
    hop = group // 2
    while hop >= 1:
        route = [(g * group + (r + hop) % group, g * group + r) for g in range(groups) for r in range(group)]
        moved = lax.ppermute(part.astype(jnp.bfloat16), "seq", route).astype(jnp.float32)
        part = jnp.where(rel < hop, part + moved, part)
        hop //= 2
    own_local = jnp.arange(blocks_dev, dtype=jnp.int32)
    far_here = (rel == 0) & (own_local == sum_local)
    far_add = jnp.where(far_here[:, None, None], part[None], 0.0)

    own_grad = grad_kv[back_blocks * BLK : pool_blocks * BLK]
    pool_start = 0
    for distance in range(reach_back, 0, -1):
        rows_needed = span_blocks[distance - 1] * BLK
        back = passed_along(
            grad_kv[pool_start : pool_start + rows_needed].astype(jnp.bfloat16), "seq", -distance
        ).astype(jnp.float32)
        own_grad = own_grad.at[tok_dev - rows_needed :].add(back)
        pool_start = pool_start + rows_needed
    total = own_grad.reshape(blocks_dev, BLK, 2 * width) + far_add
    total = total.reshape(tok_dev, 2 * width).astype(jnp.bfloat16)

    proj_grad = lax.psum_scatter(
        lax.dot_general(
            out_grad,
            attn_out.reshape(tok_dev, width),
            (((0,), (0,)), ((), ())),
            preferred_element_type=jnp.float32,
        ),
        "seq",
        scatter_dimension=0,
        tiled=True,
    )
    return (
        query_grad.reshape(tok_dev, width),
        total[:, :width],
        total[:, width:],
        proj_grad,
    )


def solution(mesh):
    return jax.shard_map(
        local,
        mesh=mesh,
        in_specs=(
            P(("dp", "seq"), "head"),
            P(("dp", "seq"), "head"),
            P(("dp", "seq"), "head"),
            P(("dp", "seq"), None),
            P(None, "head"),
            P(),
        ),
        out_specs=(
            P(("dp", "seq"), "head"),
            P(("dp", "seq"), "head"),
            P(("dp", "seq"), "head"),
            P(("dp", "seq"), "head"),
        ),
        check_vma=False,
    )
```

```python
import functools

import jax
import jax.numpy as jnp
from jax import lax
from jax.experimental import pallas as pl
from jax.experimental.pallas import tpu as pltpu
from jax.sharding import PartitionSpec as P

HD = 128
BLK = 128
LOCAL = 8
STRIDE = 16


def passed_along(block, axis, distance):
    devices = range(lax.axis_size(axis))
    route = [(i - distance, i) for i in devices if i - distance in devices]
    return lax.ppermute(block, axis, route)


def listed(table_rows, block_ids):
    hit = jnp.any(table_rows[:, None, :] == block_ids[:, :, None], axis=2)
    return hit & (block_ids >= 0)


def exchange_kernel(dims, ctl_ref, kv_ref, win_out, far_out, win_buf, hop_buf, cross1, cross2, held, pair, sends, recvs):
    seq_size, group, spans = dims
    groups = seq_size // group
    me = lax.axis_index("seq")
    in_group = me % group
    base = me - in_group
    my_group = me // group
    lead = ctl_ref[0]
    sum_local = ctl_ref[1]
    rel = (in_group - lead + group) % group
    mesh_id = pl.DeviceIdType.MESH

    def ring(step):
        return (me + step + seq_size) % seq_size

    def in_ring(step):
        return base + (in_group + step + group) % group

    def across(span):
        upper = (my_group // span) % 2
        return me + span * group - 2 * span * group * upper

    barrier = pltpu.get_barrier_semaphore()
    partners = []
    for distance in range(1, len(spans) + 1):
        partners += [ring(distance), ring(-distance)]
    hop = 1
    while hop < group:
        partners += [in_ring(hop), in_ring(-hop)]
        hop *= 2
    span = 1
    while span < groups:
        partners += [across(span), across(span)]
        span *= 2
    for partner in partners:
        pl.semaphore_signal(barrier, 1, device_id={"seq": partner}, device_id_type=mesh_id)
    pl.semaphore_wait(barrier, len(partners))

    tok_dev = kv_ref.shape[0]
    mine = kv_ref[0:BLK, :]
    for block in range(1, tok_dev // BLK):
        mine = jnp.where(sum_local == block, kv_ref[block * BLK : (block + 1) * BLK, :], mine)
    held[...] = mine
    slot = len(spans)
    hop = 1
    stage = 0
    while hop < group:
        copy = pltpu.make_async_remote_copy(
            src_ref=held,
            dst_ref=hop_buf.at[stage],
            send_sem=sends.at[slot],
            recv_sem=recvs.at[slot],
            device_id={"seq": in_ring(hop)},
            device_id_type=mesh_id,
        )
        copy.start()
        copy.wait()
        take = (rel >= hop) & (rel < 2 * hop)
        held[...] = jnp.where(take, hop_buf[stage], held[...])
        slot += 1
        stage += 1
        hop *= 2

    copy = pltpu.make_async_remote_copy(
        src_ref=held,
        dst_ref=cross1,
        send_sem=sends.at[slot],
        recv_sem=recvs.at[slot],
        device_id={"seq": across(1)},
        device_id_type=mesh_id,
    )
    copy.start()
    copy.wait()
    upper = (my_group % 2) == 1
    pair[0] = jnp.where(upper, cross1[...], held[...])
    pair[1] = jnp.where(upper, held[...], cross1[...])
    slot += 1
    window = []
    start = 0
    for distance in range(len(spans), 0, -1):
        rows = spans[distance - 1] * BLK
        copy = pltpu.make_async_remote_copy(
            src_ref=kv_ref.at[pl.ds(tok_dev - rows, rows)],
            dst_ref=win_buf.at[pl.ds(start, rows)],
            send_sem=sends.at[distance - 1],
            recv_sem=recvs.at[distance - 1],
            device_id={"seq": ring(distance)},
            device_id_type=mesh_id,
        )
        copy.start()
        window.append(copy)
        start += rows

    copy = pltpu.make_async_remote_copy(
        src_ref=pair,
        dst_ref=cross2,
        send_sem=sends.at[slot],
        recv_sem=recvs.at[slot],
        device_id={"seq": across(2)},
        device_id_type=mesh_id,
    )
    copy.start()
    copy.wait()
    upper = ((my_group // 2) % 2) == 1
    for index in range(2):
        far_out[index] = jnp.where(upper, cross2[index], pair[index])
        far_out[2 + index] = jnp.where(upper, pair[index], cross2[index])
    for copy in window:
        copy.wait()
    win_out[...] = win_buf[...]


def exchange(kv, lead, sum_local, spans, seq_size, group):
    tok_dev, cols = kv.shape
    back_rows = sum(spans) * BLK
    groups = seq_size // group
    copies = len(spans) + 5
    ctl = jnp.stack([lead, sum_local]).astype(jnp.int32)
    return pl.pallas_call(
        functools.partial(exchange_kernel, (seq_size, group, spans)),
        out_shape=(
            jax.ShapeDtypeStruct((back_rows, cols), kv.dtype),
            jax.ShapeDtypeStruct((groups, BLK, cols), kv.dtype),
        ),
        in_specs=[
            pl.BlockSpec(memory_space=pltpu.SMEM),
            pl.BlockSpec(memory_space=pltpu.VMEM),
        ],
        out_specs=(
            pl.BlockSpec(memory_space=pltpu.VMEM),
            pl.BlockSpec(memory_space=pltpu.VMEM),
        ),
        scratch_shapes=[
            pltpu.VMEM((back_rows, cols), kv.dtype),
            pltpu.VMEM((3, BLK, cols), kv.dtype),
            pltpu.VMEM((BLK, cols), kv.dtype),
            pltpu.VMEM((2, BLK, cols), kv.dtype),
            pltpu.VMEM((BLK, cols), kv.dtype),
            pltpu.VMEM((2, BLK, cols), kv.dtype),
            pltpu.SemaphoreType.DMA((copies,)),
            pltpu.SemaphoreType.DMA((copies,)),
        ],
        compiler_params=pltpu.CompilerParams(
            collective_id=0, has_side_effects=True, vmem_limit_bytes=48 * 1024 * 1024
        ),
    )(ctl, kv)


def forward_kernel(scale, q_ref, k_ref, v_ref, bias_ref, o_ref):
    scores = lax.dot_general(
        q_ref[...], k_ref[...], (((1,), (1,)), ((), ())), preferred_element_type=jnp.float32
    )
    scores = scores * scale + bias_ref[...]
    row_top = jnp.max(scores, axis=1, keepdims=True)
    log_total = row_top + jnp.log(jnp.sum(jnp.exp(scores - row_top), axis=1, keepdims=True))
    probs_low = jnp.exp(scores - log_total).astype(jnp.bfloat16)
    o_ref[...] = jnp.dot(probs_low, v_ref[...], preferred_element_type=jnp.float32).astype(o_ref.dtype)


def attention_out(queries, all_kv, bias, scale):
    rows, width = queries.shape
    keys_total = all_kv.shape[0]
    heads_here = width // HD
    return pl.pallas_call(
        functools.partial(forward_kernel, scale),
        out_shape=jax.ShapeDtypeStruct((rows, width), jnp.bfloat16),
        grid=(heads_here,),
        in_specs=[
            pl.BlockSpec((rows, HD), lambda h: (0, h)),
            pl.BlockSpec((keys_total, HD), lambda h: (0, h)),
            pl.BlockSpec((keys_total, HD), lambda h: (0, h + heads_here)),
            pl.BlockSpec((rows, keys_total), lambda h: (0, 0)),
        ],
        out_specs=pl.BlockSpec((rows, HD), lambda h: (0, h)),
        cost_estimate=pl.CostEstimate(
            flops=4 * rows * keys_total * width,
            transcendentals=2 * rows * keys_total * heads_here,
            bytes_accessed=2 * (2 * rows * width + 2 * keys_total * width) + 4 * rows * keys_total,
        ),
    )(queries, all_kv, all_kv, bias)


def local(queries, keys, values, out_grad, proj_weight, layout):
    tok_dev = queries.shape[0]
    width = queries.shape[1]
    heads_here = width // HD
    blocks_dev = tok_dev // BLK
    block_count = layout.shape[0]
    summary_count = block_count // STRIDE
    score_scale = HD ** (-0.5)
    me = lax.axis_index("seq")
    first_block = me * blocks_dev
    offset_block = layout[block_count - 1, 0] % STRIDE
    reach_back = (LOCAL - 2) // blocks_dev + 1
    span_blocks = [
        min(blocks_dev, LOCAL - 1 - hop_index * blocks_dev) for hop_index in range(reach_back)
    ]
    back_blocks = sum(span_blocks)
    pool_blocks = back_blocks + blocks_dev

    attn_grad = jnp.dot(out_grad, proj_weight, preferred_element_type=jnp.float32).astype(
        jnp.bfloat16
    )
    kv = jnp.concatenate([keys, values], axis=1)

    seq_size = lax.axis_size("seq")
    group = STRIDE // blocks_dev
    groups = seq_size // group
    assert groups == summary_count == 4 and group == 8
    far_ids = jnp.arange(summary_count, dtype=jnp.int32) * STRIDE + offset_block
    lead = offset_block // blocks_dev
    sum_local = offset_block % blocks_dev
    in_group = me % group
    my_group = me // group
    rel = (in_group - lead) % group
    win_kv, far_blocks = exchange(kv, lead, sum_local, span_blocks, seq_size, group)
    pool_kv = jnp.concatenate([win_kv, kv], axis=0)
    far_kv = far_blocks.reshape(summary_count * BLK, 2 * width)

    all_kv = jnp.concatenate([pool_kv, far_kv], axis=0)
    key_rows = all_kv[:, :width].reshape(-1, heads_here, HD)
    value_rows = all_kv[:, width:].reshape(-1, heads_here, HD)
    query_rows = queries.reshape(tok_dev, heads_here, HD)
    grad_rows = attn_grad.reshape(tok_dev, heads_here, HD)

    own_ids = first_block + jnp.arange(blocks_dev, dtype=jnp.int32)
    table_rows = lax.dynamic_slice_in_dim(layout, first_block, blocks_dev, 0)
    pool_ids = first_block - back_blocks + jnp.arange(pool_blocks, dtype=jnp.int32)
    pool_ids_b = jnp.broadcast_to(pool_ids[None, :], (blocks_dev, pool_blocks))
    plain = (pool_ids_b % STRIDE != offset_block) | (pool_ids_b == own_ids[:, None])
    pool_ok = listed(table_rows, pool_ids_b) & plain
    far_ids_b = jnp.broadcast_to(far_ids[None, :], (blocks_dev, summary_count))
    far_ok = listed(table_rows, far_ids_b) & (far_ids_b < own_ids[:, None])
    block_ok = jnp.concatenate([pool_ok, far_ok], axis=1)
    token_ok = jnp.repeat(jnp.repeat(block_ok, BLK, axis=0), BLK, axis=1)
    query_pos = jnp.arange(tok_dev, dtype=jnp.int32)
    pool_pos = jnp.arange(pool_blocks * BLK, dtype=jnp.int32) - back_blocks * BLK
    causal = jnp.concatenate(
        [
            pool_pos[None, :] <= query_pos[:, None],
            jnp.ones((tok_dev, summary_count * BLK), jnp.bool_),
        ],
        axis=1,
    )
    allowed = token_ok & causal

    scores = (
        jnp.einsum("qhd,khd->hqk", query_rows, key_rows, preferred_element_type=jnp.float32)
        * score_scale
    )
    scores = jnp.where(allowed[None], scores, -jnp.inf)
    row_top = jnp.max(scores, axis=-1, keepdims=True)
    log_total = row_top + jnp.log(jnp.sum(jnp.exp(scores - row_top), axis=-1, keepdims=True))
    probs = jnp.exp(scores - log_total)
    probs_low = probs.astype(jnp.bfloat16)
    bias = jnp.where(allowed, 0.0, -jnp.inf).astype(jnp.float32)
    attn_out = attention_out(queries, all_kv, bias, score_scale).reshape(tok_dev, heads_here, HD)
    delta = jnp.transpose(
        jnp.sum(attn_out.astype(jnp.float32) * grad_rows.astype(jnp.float32), axis=-1)
    )[..., None]
    dprobs = jnp.einsum("qhd,khd->hqk", grad_rows, value_rows, preferred_element_type=jnp.float32)
    dscores = (score_scale * probs * (dprobs - delta)).astype(jnp.bfloat16)
    query_grad = jnp.einsum(
        "hqk,khd->qhd", dscores, key_rows, preferred_element_type=jnp.float32
    ).astype(jnp.bfloat16)
    key_part = jnp.einsum("hqk,qhd->khd", dscores, query_rows, preferred_element_type=jnp.float32)
    value_part = jnp.einsum(
        "hqk,qhd->khd", probs_low, grad_rows, preferred_element_type=jnp.float32
    )
    grad_kv = jnp.concatenate(
        [key_part.reshape(-1, width), value_part.reshape(-1, width)], axis=1
    )

    part = grad_kv[pool_blocks * BLK :].reshape(summary_count, BLK, 2 * width)
    span = groups // 2
    while span >= 1:
        half = part.shape[0] // 2
        upper = (my_group // span) % 2 == 1
        keep = jnp.where(upper, part[half:], part[:half])
        send = jnp.where(upper, part[:half], part[half:])
        route = [(d, d ^ (span * group)) for d in range(seq_size)]
        part = keep + lax.ppermute(send.astype(jnp.bfloat16), "seq", route).astype(jnp.float32)
        span //= 2
    part = part[0]
    hop = group // 2
    while hop >= 1:
        route = [(g * group + (r + hop) % group, g * group + r) for g in range(groups) for r in range(group)]
        moved = lax.ppermute(part.astype(jnp.bfloat16), "seq", route).astype(jnp.float32)
        part = jnp.where(rel < hop, part + moved, part)
        hop //= 2
    own_local = jnp.arange(blocks_dev, dtype=jnp.int32)
    far_here = (rel == 0) & (own_local == sum_local)
    far_add = jnp.where(far_here[:, None, None], part[None], 0.0)

    own_grad = grad_kv[back_blocks * BLK : pool_blocks * BLK]
    pool_start = 0
    for distance in range(reach_back, 0, -1):
        rows_needed = span_blocks[distance - 1] * BLK
        back = passed_along(
            grad_kv[pool_start : pool_start + rows_needed].astype(jnp.bfloat16), "seq", -distance
        ).astype(jnp.float32)
        own_grad = own_grad.at[tok_dev - rows_needed :].add(back)
        pool_start = pool_start + rows_needed
    total = own_grad.reshape(blocks_dev, BLK, 2 * width) + far_add
    total = total.reshape(tok_dev, 2 * width).astype(jnp.bfloat16)

    proj_grad = lax.psum_scatter(
        lax.dot_general(
            out_grad,
            attn_out.reshape(tok_dev, width),
            (((0,), (0,)), ((), ())),
            preferred_element_type=jnp.float32,
        ),
        "seq",
        scatter_dimension=0,
        tiled=True,
    )
    return (
        query_grad.reshape(tok_dev, width),
        total[:, :width],
        total[:, width:],
        proj_grad,
    )


def solution(mesh):
    return jax.shard_map(
        local,
        mesh=mesh,
        in_specs=(
            P(("dp", "seq"), "head"),
            P(("dp", "seq"), "head"),
            P(("dp", "seq"), "head"),
            P(("dp", "seq"), None),
            P(None, "head"),
            P(),
        ),
        out_specs=(
            P(("dp", "seq"), "head"),
            P(("dp", "seq"), "head"),
            P(("dp", "seq"), "head"),
            P(("dp", "seq"), "head"),
        ),
        check_vma=False,
    )
```

```python
import functools

import jax
import jax.numpy as jnp
from jax import lax
from jax.experimental import pallas as pl
from jax.experimental.pallas import tpu as pltpu
from jax.sharding import PartitionSpec as P

HD = 128
BLK = 128
LOCAL = 8
STRIDE = 16


def passed_along(block, axis, distance):
    devices = range(lax.axis_size(axis))
    route = [(i - distance, i) for i in devices if i - distance in devices]
    return lax.ppermute(block, axis, route)


def listed(table_rows, block_ids):
    hit = jnp.any(table_rows[:, None, :] == block_ids[:, :, None], axis=2)
    return hit & (block_ids >= 0)


def exchange_kernel(dims, ctl_ref, kv_ref, win_out, far_out, win_buf, hop_buf, cross1, cross2, held, pair, sends, recvs):
    seq_size, group, spans = dims
    groups = seq_size // group
    me = lax.axis_index("seq")
    in_group = me % group
    base = me - in_group
    my_group = me // group
    lead = ctl_ref[0]
    sum_local = ctl_ref[1]
    rel = (in_group - lead + group) % group
    mesh_id = pl.DeviceIdType.MESH

    def ring(step):
        return (me + step + seq_size) % seq_size

    def in_ring(step):
        return base + (in_group + step + group) % group

    def across(span):
        upper = (my_group // span) % 2
        return me + span * group - 2 * span * group * upper

    barrier = pltpu.get_barrier_semaphore()
    partners = []
    for distance in range(1, len(spans) + 1):
        partners += [ring(distance), ring(-distance)]
    hop = 1
    while hop < group:
        partners += [in_ring(hop), in_ring(-hop)]
        hop *= 2
    span = 1
    while span < groups:
        partners += [across(span), across(span)]
        span *= 2
    for partner in partners:
        pl.semaphore_signal(barrier, 1, device_id={"seq": partner}, device_id_type=mesh_id)
    pl.semaphore_wait(barrier, len(partners))

    tok_dev = kv_ref.shape[0]
    mine = kv_ref[0:BLK, :]
    for block in range(1, tok_dev // BLK):
        mine = jnp.where(sum_local == block, kv_ref[block * BLK : (block + 1) * BLK, :], mine)
    held[...] = mine
    slot = len(spans)
    hop = 1
    stage = 0
    while hop < group:
        copy = pltpu.make_async_remote_copy(
            src_ref=held,
            dst_ref=hop_buf.at[stage],
            send_sem=sends.at[slot],
            recv_sem=recvs.at[slot],
            device_id={"seq": in_ring(hop)},
            device_id_type=mesh_id,
        )
        copy.start()
        copy.wait()
        take = (rel >= hop) & (rel < 2 * hop)
        held[...] = jnp.where(take, hop_buf[stage], held[...])
        slot += 1
        stage += 1
        hop *= 2

    copy = pltpu.make_async_remote_copy(
        src_ref=held,
        dst_ref=cross1,
        send_sem=sends.at[slot],
        recv_sem=recvs.at[slot],
        device_id={"seq": across(1)},
        device_id_type=mesh_id,
    )
    copy.start()
    copy.wait()
    upper = (my_group % 2) == 1
    pair[0] = jnp.where(upper, cross1[...], held[...])
    pair[1] = jnp.where(upper, held[...], cross1[...])
    slot += 1
    window = []
    start = 0
    for distance in range(len(spans), 0, -1):
        rows = spans[distance - 1] * BLK
        copy = pltpu.make_async_remote_copy(
            src_ref=kv_ref.at[pl.ds(tok_dev - rows, rows)],
            dst_ref=win_buf.at[pl.ds(start, rows)],
            send_sem=sends.at[distance - 1],
            recv_sem=recvs.at[distance - 1],
            device_id={"seq": ring(distance)},
            device_id_type=mesh_id,
        )
        copy.start()
        window.append(copy)
        start += rows

    copy = pltpu.make_async_remote_copy(
        src_ref=pair,
        dst_ref=cross2,
        send_sem=sends.at[slot],
        recv_sem=recvs.at[slot],
        device_id={"seq": across(2)},
        device_id_type=mesh_id,
    )
    copy.start()
    copy.wait()
    upper = ((my_group // 2) % 2) == 1
    for index in range(2):
        far_out[index] = jnp.where(upper, cross2[index], pair[index])
        far_out[2 + index] = jnp.where(upper, pair[index], cross2[index])
    for copy in window:
        copy.wait()
    win_out[...] = win_buf[...]


def exchange(kv, lead, sum_local, spans, seq_size, group):
    tok_dev, cols = kv.shape
    back_rows = sum(spans) * BLK
    groups = seq_size // group
    copies = len(spans) + 5
    ctl = jnp.stack([lead, sum_local]).astype(jnp.int32)
    return pl.pallas_call(
        functools.partial(exchange_kernel, (seq_size, group, spans)),
        out_shape=(
            jax.ShapeDtypeStruct((back_rows, cols), kv.dtype),
            jax.ShapeDtypeStruct((groups, BLK, cols), kv.dtype),
        ),
        in_specs=[
            pl.BlockSpec(memory_space=pltpu.SMEM),
            pl.BlockSpec(memory_space=pltpu.VMEM),
        ],
        out_specs=(
            pl.BlockSpec(memory_space=pltpu.VMEM),
            pl.BlockSpec(memory_space=pltpu.VMEM),
        ),
        scratch_shapes=[
            pltpu.VMEM((back_rows, cols), kv.dtype),
            pltpu.VMEM((3, BLK, cols), kv.dtype),
            pltpu.VMEM((BLK, cols), kv.dtype),
            pltpu.VMEM((2, BLK, cols), kv.dtype),
            pltpu.VMEM((BLK, cols), kv.dtype),
            pltpu.VMEM((2, BLK, cols), kv.dtype),
            pltpu.SemaphoreType.DMA((copies,)),
            pltpu.SemaphoreType.DMA((copies,)),
        ],
        compiler_params=pltpu.CompilerParams(
            collective_id=0, has_side_effects=True, vmem_limit_bytes=48 * 1024 * 1024
        ),
    )(ctl, kv)


def forward_kernel(scale, q_ref, k_ref, v_ref, bias_ref, o_ref):
    scores = lax.dot_general(
        q_ref[...], k_ref[...], (((1,), (1,)), ((), ())), preferred_element_type=jnp.float32
    )
    scores = scores * scale + bias_ref[...]
    row_top = jnp.max(scores, axis=1, keepdims=True)
    log_total = row_top + jnp.log(jnp.sum(jnp.exp(scores - row_top), axis=1, keepdims=True))
    probs_low = jnp.exp(scores - log_total).astype(jnp.bfloat16)
    o_ref[...] = jnp.dot(probs_low, v_ref[...], preferred_element_type=jnp.float32).astype(o_ref.dtype)


def attention_out(queries, all_kv, bias, scale):
    rows, width = queries.shape
    keys_total = all_kv.shape[0]
    heads_here = width // HD
    return pl.pallas_call(
        functools.partial(forward_kernel, scale),
        out_shape=jax.ShapeDtypeStruct((rows, width), jnp.bfloat16),
        grid=(heads_here,),
        in_specs=[
            pl.BlockSpec((rows, HD), lambda h: (0, h)),
            pl.BlockSpec((keys_total, HD), lambda h: (0, h)),
            pl.BlockSpec((keys_total, HD), lambda h: (0, h + heads_here)),
            pl.BlockSpec((rows, keys_total), lambda h: (0, 0)),
        ],
        out_specs=pl.BlockSpec((rows, HD), lambda h: (0, h)),
        cost_estimate=pl.CostEstimate(
            flops=4 * rows * keys_total * width,
            transcendentals=2 * rows * keys_total * heads_here,
            bytes_accessed=2 * (2 * rows * width + 2 * keys_total * width) + 4 * rows * keys_total,
        ),
    )(queries, all_kv, all_kv, bias)


def local(queries, keys, values, out_grad, proj_weight, layout):
    tok_dev = queries.shape[0]
    width = queries.shape[1]
    heads_here = width // HD
    blocks_dev = tok_dev // BLK
    block_count = layout.shape[0]
    summary_count = block_count // STRIDE
    score_scale = HD ** (-0.5)
    me = lax.axis_index("seq")
    first_block = me * blocks_dev
    offset_block = layout[block_count - 1, 0] % STRIDE
    reach_back = (LOCAL - 2) // blocks_dev + 1
    span_blocks = [
        min(blocks_dev, LOCAL - 1 - hop_index * blocks_dev) for hop_index in range(reach_back)
    ]
    back_blocks = sum(span_blocks)
    pool_blocks = back_blocks + blocks_dev

    attn_grad = jnp.dot(out_grad, proj_weight, preferred_element_type=jnp.float32).astype(
        jnp.bfloat16
    )
    kv = jnp.concatenate([keys, values], axis=1)

    seq_size = lax.axis_size("seq")
    group = STRIDE // blocks_dev
    groups = seq_size // group
    assert groups == summary_count == 4 and group == 8
    far_ids = jnp.arange(summary_count, dtype=jnp.int32) * STRIDE + offset_block
    lead = offset_block // blocks_dev
    sum_local = offset_block % blocks_dev
    in_group = me % group
    my_group = me // group
    rel = (in_group - lead) % group
    win_kv, far_blocks = exchange(kv, lead, sum_local, span_blocks, seq_size, group)
    pool_kv = jnp.concatenate([win_kv, kv], axis=0)
    far_kv = far_blocks.reshape(summary_count * BLK, 2 * width)

    all_kv = jnp.concatenate([pool_kv, far_kv], axis=0)
    key_rows = all_kv[:, :width].reshape(-1, heads_here, HD)
    value_rows = all_kv[:, width:].reshape(-1, heads_here, HD)
    query_rows = queries.reshape(tok_dev, heads_here, HD)
    grad_rows = attn_grad.reshape(tok_dev, heads_here, HD)

    own_ids = first_block + jnp.arange(blocks_dev, dtype=jnp.int32)
    table_rows = lax.dynamic_slice_in_dim(layout, first_block, blocks_dev, 0)
    pool_ids = first_block - back_blocks + jnp.arange(pool_blocks, dtype=jnp.int32)
    pool_ids_b = jnp.broadcast_to(pool_ids[None, :], (blocks_dev, pool_blocks))
    plain = (pool_ids_b % STRIDE != offset_block) | (pool_ids_b == own_ids[:, None])
    pool_ok = listed(table_rows, pool_ids_b) & plain
    far_ids_b = jnp.broadcast_to(far_ids[None, :], (blocks_dev, summary_count))
    far_ok = listed(table_rows, far_ids_b) & (far_ids_b < own_ids[:, None])
    block_ok = jnp.concatenate([pool_ok, far_ok], axis=1)
    token_ok = jnp.repeat(jnp.repeat(block_ok, BLK, axis=0), BLK, axis=1)
    query_pos = jnp.arange(tok_dev, dtype=jnp.int32)
    pool_pos = jnp.arange(pool_blocks * BLK, dtype=jnp.int32) - back_blocks * BLK
    causal = jnp.concatenate(
        [
            pool_pos[None, :] <= query_pos[:, None],
            jnp.ones((tok_dev, summary_count * BLK), jnp.bool_),
        ],
        axis=1,
    )
    allowed = token_ok & causal

    scores = (
        jnp.einsum("qhd,khd->hqk", query_rows, key_rows, preferred_element_type=jnp.float32)
        * score_scale
    )
    scores = jnp.where(allowed[None], scores, -jnp.inf)
    row_top = jnp.max(scores, axis=-1, keepdims=True)
    log_total = row_top + jnp.log(jnp.sum(jnp.exp(scores - row_top), axis=-1, keepdims=True))
    probs = jnp.exp(scores - log_total)
    probs_low = probs.astype(jnp.bfloat16)
    bias = jnp.where(allowed, 0.0, -jnp.inf).astype(jnp.float32)
    attn_out = attention_out(queries, all_kv, bias, score_scale).reshape(tok_dev, heads_here, HD)
    delta = jnp.transpose(
        jnp.sum(attn_out.astype(jnp.float32) * grad_rows.astype(jnp.float32), axis=-1)
    )[..., None]
    dprobs = jnp.einsum("qhd,khd->hqk", grad_rows, value_rows, preferred_element_type=jnp.float32)
    dscores = (score_scale * probs * (dprobs - delta)).astype(jnp.bfloat16)
    query_grad = jnp.einsum(
        "hqk,khd->qhd", dscores, key_rows, preferred_element_type=jnp.float32
    ).astype(jnp.bfloat16)
    key_part = jnp.einsum("hqk,qhd->khd", dscores, query_rows, preferred_element_type=jnp.float32)
    value_part = jnp.einsum(
        "hqk,qhd->khd", probs_low, grad_rows, preferred_element_type=jnp.float32
    )
    grad_kv = jnp.concatenate(
        [key_part.reshape(-1, width), value_part.reshape(-1, width)], axis=1
    )

    proj_part = lax.dot_general(
        out_grad,
        attn_out.reshape(tok_dev, width),
        (((0,), (0,)), ((), ())),
        preferred_element_type=jnp.float32,
    )
    proj_rows = proj_part.shape[0] // seq_size
    far_grad = grad_kv[pool_blocks * BLK :].reshape(seq_size, -1, proj_part.shape[1])
    joined = jnp.concatenate([proj_part.reshape(seq_size, proj_rows, -1), far_grad], axis=1)
    mine = lax.psum_scatter(
        joined.reshape(-1, proj_part.shape[1]), "seq", scatter_dimension=0, tiled=True
    )
    proj_grad = mine[:proj_rows]
    chunk = mine[proj_rows:].reshape(1, -1, 2 * width)
    hop = 1
    while hop < group:
        route = [(g * group + r, g * group + (r ^ hop)) for g in range(groups) for r in range(group)]
        moved = lax.ppermute(chunk, "seq", route)
        upper = (in_group // hop) % 2 == 1
        chunk = jnp.where(
            upper, jnp.concatenate([moved, chunk], 0), jnp.concatenate([chunk, moved], 0)
        )
        hop *= 2
    part = chunk.reshape(BLK, 2 * width)
    own_local = jnp.arange(blocks_dev, dtype=jnp.int32)
    far_here = (rel == 0) & (own_local == sum_local)
    far_add = jnp.where(far_here[:, None, None], part[None], 0.0)

    own_grad = grad_kv[back_blocks * BLK : pool_blocks * BLK]
    pool_start = 0
    for distance in range(reach_back, 0, -1):
        rows_needed = span_blocks[distance - 1] * BLK
        back = passed_along(
            grad_kv[pool_start : pool_start + rows_needed].astype(jnp.bfloat16), "seq", -distance
        ).astype(jnp.float32)
        own_grad = own_grad.at[tok_dev - rows_needed :].add(back)
        pool_start = pool_start + rows_needed
    total = own_grad.reshape(blocks_dev, BLK, 2 * width) + far_add
    total = total.reshape(tok_dev, 2 * width).astype(jnp.bfloat16)

    return (
        query_grad.reshape(tok_dev, width),
        total[:, :width],
        total[:, width:],
        proj_grad,
    )


def solution(mesh):
    return jax.shard_map(
        local,
        mesh=mesh,
        in_specs=(
            P(("dp", "seq"), "head"),
            P(("dp", "seq"), "head"),
            P(("dp", "seq"), "head"),
            P(("dp", "seq"), None),
            P(None, "head"),
            P(),
        ),
        out_specs=(
            P(("dp", "seq"), "head"),
            P(("dp", "seq"), "head"),
            P(("dp", "seq"), "head"),
            P(("dp", "seq"), "head"),
        ),
        check_vma=False,
    )
```

```python
import functools

import jax
import jax.numpy as jnp
from jax import lax
from jax.experimental import pallas as pl
from jax.experimental.pallas import tpu as pltpu
from jax.sharding import PartitionSpec as P

HD = 128
BLK = 128
LOCAL = 8
STRIDE = 16


def passed_along(block, axis, distance):
    devices = range(lax.axis_size(axis))
    route = [(i - distance, i) for i in devices if i - distance in devices]
    return lax.ppermute(block, axis, route)


def listed(table_rows, block_ids):
    hit = jnp.any(table_rows[:, None, :] == block_ids[:, :, None], axis=2)
    return hit & (block_ids >= 0)


def exchange_kernel(dims, ctl_ref, kv_ref, win_out, far_out, win_buf, hop_buf, cross1, cross2, held, pair, sends, recvs):
    seq_size, group, spans = dims
    groups = seq_size // group
    me = lax.axis_index("seq")
    in_group = me % group
    base = me - in_group
    my_group = me // group
    lead = ctl_ref[0]
    sum_local = ctl_ref[1]
    rel = (in_group - lead + group) % group
    mesh_id = pl.DeviceIdType.MESH

    def ring(step):
        return (me + step + seq_size) % seq_size

    def in_ring(step):
        return base + (in_group + step + group) % group

    def across(span):
        upper = (my_group // span) % 2
        return me + span * group - 2 * span * group * upper

    barrier = pltpu.get_barrier_semaphore()
    partners = []
    for distance in range(1, len(spans) + 1):
        partners += [ring(distance), ring(-distance)]
    hop = 1
    while hop < group:
        partners += [in_ring(hop), in_ring(-hop)]
        hop *= 2
    span = 1
    while span < groups:
        partners += [across(span), across(span)]
        span *= 2
    for partner in partners:
        pl.semaphore_signal(barrier, 1, device_id={"seq": partner}, device_id_type=mesh_id)
    pl.semaphore_wait(barrier, len(partners))

    tok_dev = kv_ref.shape[0]
    window = []
    starts = {}
    start = 0
    for distance in range(len(spans), 0, -1):
        starts[distance] = start
        start += spans[distance - 1] * BLK

    def send_window(distance):
        rows = spans[distance - 1] * BLK
        copy = pltpu.make_async_remote_copy(
            src_ref=kv_ref.at[pl.ds(tok_dev - rows, rows)],
            dst_ref=win_buf.at[pl.ds(starts[distance], rows)],
            send_sem=sends.at[distance - 1],
            recv_sem=recvs.at[distance - 1],
            device_id={"seq": ring(distance)},
            device_id_type=mesh_id,
        )
        copy.start()
        window.append(copy)

    for distance in range(len(spans), 2, -1):
        send_window(distance)

    mine = kv_ref[0:BLK, :]
    for block in range(1, tok_dev // BLK):
        mine = jnp.where(sum_local == block, kv_ref[block * BLK : (block + 1) * BLK, :], mine)
    held[...] = mine
    slot = len(spans)
    hop = 1
    stage = 0
    while hop < group:
        copy = pltpu.make_async_remote_copy(
            src_ref=held,
            dst_ref=hop_buf.at[stage],
            send_sem=sends.at[slot],
            recv_sem=recvs.at[slot],
            device_id={"seq": in_ring(hop)},
            device_id_type=mesh_id,
        )
        copy.start()
        copy.wait()
        take = (rel >= hop) & (rel < 2 * hop)
        held[...] = jnp.where(take, hop_buf[stage], held[...])
        slot += 1
        stage += 1
        hop *= 2

    for distance in range(min(2, len(spans)), 0, -1):
        send_window(distance)

    copy = pltpu.make_async_remote_copy(
        src_ref=held,
        dst_ref=cross1,
        send_sem=sends.at[slot],
        recv_sem=recvs.at[slot],
        device_id={"seq": across(1)},
        device_id_type=mesh_id,
    )
    copy.start()
    copy.wait()
    upper = (my_group % 2) == 1
    pair[0] = jnp.where(upper, cross1[...], held[...])
    pair[1] = jnp.where(upper, held[...], cross1[...])
    slot += 1
    copy = pltpu.make_async_remote_copy(
        src_ref=pair,
        dst_ref=cross2,
        send_sem=sends.at[slot],
        recv_sem=recvs.at[slot],
        device_id={"seq": across(2)},
        device_id_type=mesh_id,
    )
    copy.start()
    copy.wait()
    upper = ((my_group // 2) % 2) == 1
    for index in range(2):
        far_out[index] = jnp.where(upper, cross2[index], pair[index])
        far_out[2 + index] = jnp.where(upper, pair[index], cross2[index])
    for copy in window:
        copy.wait()
    win_out[...] = win_buf[...]


def exchange(kv, lead, sum_local, spans, seq_size, group):
    tok_dev, cols = kv.shape
    back_rows = sum(spans) * BLK
    groups = seq_size // group
    copies = len(spans) + 5
    ctl = jnp.stack([lead, sum_local]).astype(jnp.int32)
    return pl.pallas_call(
        functools.partial(exchange_kernel, (seq_size, group, spans)),
        out_shape=(
            jax.ShapeDtypeStruct((back_rows, cols), kv.dtype),
            jax.ShapeDtypeStruct((groups, BLK, cols), kv.dtype),
        ),
        in_specs=[
            pl.BlockSpec(memory_space=pltpu.SMEM),
            pl.BlockSpec(memory_space=pltpu.VMEM),
        ],
        out_specs=(
            pl.BlockSpec(memory_space=pltpu.VMEM),
            pl.BlockSpec(memory_space=pltpu.VMEM),
        ),
        scratch_shapes=[
            pltpu.VMEM((back_rows, cols), kv.dtype),
            pltpu.VMEM((3, BLK, cols), kv.dtype),
            pltpu.VMEM((BLK, cols), kv.dtype),
            pltpu.VMEM((2, BLK, cols), kv.dtype),
            pltpu.VMEM((BLK, cols), kv.dtype),
            pltpu.VMEM((2, BLK, cols), kv.dtype),
            pltpu.SemaphoreType.DMA((copies,)),
            pltpu.SemaphoreType.DMA((copies,)),
        ],
        compiler_params=pltpu.CompilerParams(
            collective_id=0, has_side_effects=True, vmem_limit_bytes=48 * 1024 * 1024
        ),
    )(ctl, kv)


def forward_kernel(scale, q_ref, k_ref, v_ref, bias_ref, o_ref):
    scores = lax.dot_general(
        q_ref[...], k_ref[...], (((1,), (1,)), ((), ())), preferred_element_type=jnp.float32
    )
    scores = scores * scale + bias_ref[...]
    row_top = jnp.max(scores, axis=1, keepdims=True)
    log_total = row_top + jnp.log(jnp.sum(jnp.exp(scores - row_top), axis=1, keepdims=True))
    probs_low = jnp.exp(scores - log_total).astype(jnp.bfloat16)
    o_ref[...] = jnp.dot(probs_low, v_ref[...], preferred_element_type=jnp.float32).astype(o_ref.dtype)


def attention_out(queries, all_kv, bias, scale):
    rows, width = queries.shape
    keys_total = all_kv.shape[0]
    heads_here = width // HD
    return pl.pallas_call(
        functools.partial(forward_kernel, scale),
        out_shape=jax.ShapeDtypeStruct((rows, width), jnp.bfloat16),
        grid=(heads_here,),
        in_specs=[
            pl.BlockSpec((rows, HD), lambda h: (0, h)),
            pl.BlockSpec((keys_total, HD), lambda h: (0, h)),
            pl.BlockSpec((keys_total, HD), lambda h: (0, h + heads_here)),
            pl.BlockSpec((rows, keys_total), lambda h: (0, 0)),
        ],
        out_specs=pl.BlockSpec((rows, HD), lambda h: (0, h)),
        cost_estimate=pl.CostEstimate(
            flops=4 * rows * keys_total * width,
            transcendentals=2 * rows * keys_total * heads_here,
            bytes_accessed=2 * (2 * rows * width + 2 * keys_total * width) + 4 * rows * keys_total,
        ),
    )(queries, all_kv, all_kv, bias)


def local(queries, keys, values, out_grad, proj_weight, layout):
    tok_dev = queries.shape[0]
    width = queries.shape[1]
    heads_here = width // HD
    blocks_dev = tok_dev // BLK
    block_count = layout.shape[0]
    summary_count = block_count // STRIDE
    score_scale = HD ** (-0.5)
    me = lax.axis_index("seq")
    first_block = me * blocks_dev
    offset_block = layout[block_count - 1, 0] % STRIDE
    reach_back = (LOCAL - 2) // blocks_dev + 1
    span_blocks = [
        min(blocks_dev, LOCAL - 1 - hop_index * blocks_dev) for hop_index in range(reach_back)
    ]
    back_blocks = sum(span_blocks)
    pool_blocks = back_blocks + blocks_dev

    attn_grad = jnp.dot(out_grad, proj_weight, preferred_element_type=jnp.float32).astype(
        jnp.bfloat16
    )
    kv = jnp.concatenate([keys, values], axis=1)

    seq_size = lax.axis_size("seq")
    group = STRIDE // blocks_dev
    groups = seq_size // group
    assert groups == summary_count == 4 and group == 8
    far_ids = jnp.arange(summary_count, dtype=jnp.int32) * STRIDE + offset_block
    lead = offset_block // blocks_dev
    sum_local = offset_block % blocks_dev
    in_group = me % group
    my_group = me // group
    rel = (in_group - lead) % group
    win_kv, far_blocks = exchange(kv, lead, sum_local, span_blocks, seq_size, group)
    pool_kv = jnp.concatenate([win_kv, kv], axis=0)
    far_kv = far_blocks.reshape(summary_count * BLK, 2 * width)

    all_kv = jnp.concatenate([pool_kv, far_kv], axis=0)
    key_rows = all_kv[:, :width].reshape(-1, heads_here, HD)
    value_rows = all_kv[:, width:].reshape(-1, heads_here, HD)
    query_rows = queries.reshape(tok_dev, heads_here, HD)
    grad_rows = attn_grad.reshape(tok_dev, heads_here, HD)

    own_ids = first_block + jnp.arange(blocks_dev, dtype=jnp.int32)
    table_rows = lax.dynamic_slice_in_dim(layout, first_block, blocks_dev, 0)
    pool_ids = first_block - back_blocks + jnp.arange(pool_blocks, dtype=jnp.int32)
    pool_ids_b = jnp.broadcast_to(pool_ids[None, :], (blocks_dev, pool_blocks))
    plain = (pool_ids_b % STRIDE != offset_block) | (pool_ids_b == own_ids[:, None])
    pool_ok = listed(table_rows, pool_ids_b) & plain
    far_ids_b = jnp.broadcast_to(far_ids[None, :], (blocks_dev, summary_count))
    far_ok = listed(table_rows, far_ids_b) & (far_ids_b < own_ids[:, None])
    block_ok = jnp.concatenate([pool_ok, far_ok], axis=1)
    token_ok = jnp.repeat(jnp.repeat(block_ok, BLK, axis=0), BLK, axis=1)
    query_pos = jnp.arange(tok_dev, dtype=jnp.int32)
    pool_pos = jnp.arange(pool_blocks * BLK, dtype=jnp.int32) - back_blocks * BLK
    causal = jnp.concatenate(
        [
            pool_pos[None, :] <= query_pos[:, None],
            jnp.ones((tok_dev, summary_count * BLK), jnp.bool_),
        ],
        axis=1,
    )
    allowed = token_ok & causal

    scores = (
        jnp.einsum("qhd,khd->hqk", query_rows, key_rows, preferred_element_type=jnp.float32)
        * score_scale
    )
    scores = jnp.where(allowed[None], scores, -jnp.inf)
    row_top = jnp.max(scores, axis=-1, keepdims=True)
    log_total = row_top + jnp.log(jnp.sum(jnp.exp(scores - row_top), axis=-1, keepdims=True))
    probs = jnp.exp(scores - log_total)
    probs_low = probs.astype(jnp.bfloat16)
    bias = jnp.where(allowed, 0.0, -jnp.inf).astype(jnp.float32)
    attn_out = attention_out(queries, all_kv, bias, score_scale).reshape(tok_dev, heads_here, HD)
    delta = jnp.transpose(
        jnp.sum(attn_out.astype(jnp.float32) * grad_rows.astype(jnp.float32), axis=-1)
    )[..., None]
    dprobs = jnp.einsum("qhd,khd->hqk", grad_rows, value_rows, preferred_element_type=jnp.float32)
    dscores = (score_scale * probs * (dprobs - delta)).astype(jnp.bfloat16)
    query_grad = jnp.einsum(
        "hqk,khd->qhd", dscores, key_rows, preferred_element_type=jnp.float32
    ).astype(jnp.bfloat16)
    key_part = jnp.einsum("hqk,qhd->khd", dscores, query_rows, preferred_element_type=jnp.float32)
    value_part = jnp.einsum(
        "hqk,qhd->khd", probs_low, grad_rows, preferred_element_type=jnp.float32
    )
    grad_kv = jnp.concatenate(
        [key_part.reshape(-1, width), value_part.reshape(-1, width)], axis=1
    )

    part = grad_kv[pool_blocks * BLK :].reshape(summary_count, BLK, 2 * width)
    span = groups // 2
    while span >= 1:
        half = part.shape[0] // 2
        upper = (my_group // span) % 2 == 1
        keep = jnp.where(upper, part[half:], part[:half])
        send = jnp.where(upper, part[:half], part[half:])
        route = [(d, d ^ (span * group)) for d in range(seq_size)]
        part = keep + lax.ppermute(send.astype(jnp.bfloat16), "seq", route).astype(jnp.float32)
        span //= 2
    part = part[0]
    hop = group // 2
    while hop >= 1:
        route = [(g * group + (r + hop) % group, g * group + r) for g in range(groups) for r in range(group)]
        moved = lax.ppermute(part.astype(jnp.bfloat16), "seq", route).astype(jnp.float32)
        part = jnp.where(rel < hop, part + moved, part)
        hop //= 2
    own_local = jnp.arange(blocks_dev, dtype=jnp.int32)
    far_here = (rel == 0) & (own_local == sum_local)
    far_add = jnp.where(far_here[:, None, None], part[None], 0.0)

    own_grad = grad_kv[back_blocks * BLK : pool_blocks * BLK]
    pool_start = 0
    for distance in range(reach_back, 0, -1):
        rows_needed = span_blocks[distance - 1] * BLK
        back = passed_along(
            grad_kv[pool_start : pool_start + rows_needed].astype(jnp.bfloat16), "seq", -distance
        ).astype(jnp.float32)
        own_grad = own_grad.at[tok_dev - rows_needed :].add(back)
        pool_start = pool_start + rows_needed
    total = own_grad.reshape(blocks_dev, BLK, 2 * width) + far_add
    total = total.reshape(tok_dev, 2 * width).astype(jnp.bfloat16)

    proj_grad = lax.psum_scatter(
        lax.dot_general(
            out_grad,
            attn_out.reshape(tok_dev, width),
            (((0,), (0,)), ((), ())),
            preferred_element_type=jnp.float32,
        ),
        "seq",
        scatter_dimension=0,
        tiled=True,
    )
    return (
        query_grad.reshape(tok_dev, width),
        total[:, :width],
        total[:, width:],
        proj_grad,
    )


def solution(mesh):
    return jax.shard_map(
        local,
        mesh=mesh,
        in_specs=(
            P(("dp", "seq"), "head"),
            P(("dp", "seq"), "head"),
            P(("dp", "seq"), "head"),
            P(("dp", "seq"), None),
            P(None, "head"),
            P(),
        ),
        out_specs=(
            P(("dp", "seq"), "head"),
            P(("dp", "seq"), "head"),
            P(("dp", "seq"), "head"),
            P(("dp", "seq"), "head"),
        ),
        check_vma=False,
    )
```

```python
import functools

import jax
import jax.numpy as jnp
from jax import lax
from jax.experimental import pallas as pl
from jax.experimental.pallas import tpu as pltpu
from jax.sharding import PartitionSpec as P

HD = 128
BLK = 128
LOCAL = 8
STRIDE = 16


def passed_along(block, axis, distance):
    devices = range(lax.axis_size(axis))
    route = [(i - distance, i) for i in devices if i - distance in devices]
    return lax.ppermute(block, axis, route)


def listed(table_rows, block_ids):
    hit = jnp.any(table_rows[:, None, :] == block_ids[:, :, None], axis=2)
    return hit & (block_ids >= 0)


def exchange_kernel(dims, ctl_ref, kv_ref, win_out, far_out, win_buf, hop_buf, cross1, cross2, held, pair, sends, recvs):
    seq_size, group, spans = dims
    groups = seq_size // group
    me = lax.axis_index("seq")
    in_group = me % group
    base = me - in_group
    my_group = me // group
    lead = ctl_ref[0]
    sum_local = ctl_ref[1]
    rel = (in_group - lead + group) % group
    mesh_id = pl.DeviceIdType.MESH

    def ring(step):
        return (me + step + seq_size) % seq_size

    def in_ring(step):
        return base + (in_group + step + group) % group

    def across(span):
        upper = (my_group // span) % 2
        return me + span * group - 2 * span * group * upper

    barrier = pltpu.get_barrier_semaphore()
    partners = []
    for distance in range(1, len(spans) + 1):
        partners += [ring(distance), ring(-distance)]
    hop = 1
    while hop < group:
        partners += [in_ring(hop), in_ring(-hop)]
        hop *= 2
    span = 1
    while span < groups:
        partners += [across(span), across(span)]
        span *= 2
    for partner in partners:
        pl.semaphore_signal(barrier, 1, device_id={"seq": partner}, device_id_type=mesh_id)
    pl.semaphore_wait(barrier, len(partners))

    tok_dev = kv_ref.shape[0]
    window = []
    starts = {}
    start = 0
    for distance in range(len(spans), 0, -1):
        starts[distance] = start
        start += spans[distance - 1] * BLK

    def send_window(distance):
        rows = spans[distance - 1] * BLK
        copy = pltpu.make_async_remote_copy(
            src_ref=kv_ref.at[pl.ds(tok_dev - rows, rows)],
            dst_ref=win_buf.at[pl.ds(starts[distance], rows)],
            send_sem=sends.at[distance - 1],
            recv_sem=recvs.at[distance - 1],
            device_id={"seq": ring(distance)},
            device_id_type=mesh_id,
        )
        copy.start()
        window.append(copy)

    mine = kv_ref[0:BLK, :]
    for block in range(1, tok_dev // BLK):
        mine = jnp.where(sum_local == block, kv_ref[block * BLK : (block + 1) * BLK, :], mine)
    held[...] = mine
    slot = len(spans)
    hop = 1
    stage = 0
    while hop < group:
        copy = pltpu.make_async_remote_copy(
            src_ref=held,
            dst_ref=hop_buf.at[stage],
            send_sem=sends.at[slot],
            recv_sem=recvs.at[slot],
            device_id={"seq": in_ring(hop)},
            device_id_type=mesh_id,
        )
        copy.start()
        copy.wait()
        take = (rel >= hop) & (rel < 2 * hop)
        held[...] = jnp.where(take, hop_buf[stage], held[...])
        slot += 1
        stage += 1
        hop *= 2

    copy = pltpu.make_async_remote_copy(
        src_ref=held,
        dst_ref=cross1,
        send_sem=sends.at[slot],
        recv_sem=recvs.at[slot],
        device_id={"seq": across(1)},
        device_id_type=mesh_id,
    )
    copy.start()
    copy.wait()
    upper = (my_group % 2) == 1
    pair[0] = jnp.where(upper, cross1[...], held[...])
    pair[1] = jnp.where(upper, held[...], cross1[...])
    slot += 1
    copy = pltpu.make_async_remote_copy(
        src_ref=pair,
        dst_ref=cross2,
        send_sem=sends.at[slot],
        recv_sem=recvs.at[slot],
        device_id={"seq": across(2)},
        device_id_type=mesh_id,
    )
    copy.start()
    copy.wait()
    for distance in range(len(spans), 0, -1):
        send_window(distance)
    upper = ((my_group // 2) % 2) == 1
    for index in range(2):
        far_out[index] = jnp.where(upper, cross2[index], pair[index])
        far_out[2 + index] = jnp.where(upper, pair[index], cross2[index])
    for copy in window:
        copy.wait()
    win_out[...] = win_buf[...]


def exchange(kv, lead, sum_local, spans, seq_size, group):
    tok_dev, cols = kv.shape
    back_rows = sum(spans) * BLK
    groups = seq_size // group
    copies = len(spans) + 5
    ctl = jnp.stack([lead, sum_local]).astype(jnp.int32)
    return pl.pallas_call(
        functools.partial(exchange_kernel, (seq_size, group, spans)),
        out_shape=(
            jax.ShapeDtypeStruct((back_rows, cols), kv.dtype),
            jax.ShapeDtypeStruct((groups, BLK, cols), kv.dtype),
        ),
        in_specs=[
            pl.BlockSpec(memory_space=pltpu.SMEM),
            pl.BlockSpec(memory_space=pltpu.VMEM),
        ],
        out_specs=(
            pl.BlockSpec(memory_space=pltpu.VMEM),
            pl.BlockSpec(memory_space=pltpu.VMEM),
        ),
        scratch_shapes=[
            pltpu.VMEM((back_rows, cols), kv.dtype),
            pltpu.VMEM((3, BLK, cols), kv.dtype),
            pltpu.VMEM((BLK, cols), kv.dtype),
            pltpu.VMEM((2, BLK, cols), kv.dtype),
            pltpu.VMEM((BLK, cols), kv.dtype),
            pltpu.VMEM((2, BLK, cols), kv.dtype),
            pltpu.SemaphoreType.DMA((copies,)),
            pltpu.SemaphoreType.DMA((copies,)),
        ],
        compiler_params=pltpu.CompilerParams(
            collective_id=0, has_side_effects=True, vmem_limit_bytes=48 * 1024 * 1024
        ),
    )(ctl, kv)


def forward_kernel(scale, q_ref, k_ref, v_ref, bias_ref, o_ref):
    scores = lax.dot_general(
        q_ref[...], k_ref[...], (((1,), (1,)), ((), ())), preferred_element_type=jnp.float32
    )
    scores = scores * scale + bias_ref[...]
    row_top = jnp.max(scores, axis=1, keepdims=True)
    log_total = row_top + jnp.log(jnp.sum(jnp.exp(scores - row_top), axis=1, keepdims=True))
    probs_low = jnp.exp(scores - log_total).astype(jnp.bfloat16)
    o_ref[...] = jnp.dot(probs_low, v_ref[...], preferred_element_type=jnp.float32).astype(o_ref.dtype)


def attention_out(queries, all_kv, bias, scale):
    rows, width = queries.shape
    keys_total = all_kv.shape[0]
    heads_here = width // HD
    return pl.pallas_call(
        functools.partial(forward_kernel, scale),
        out_shape=jax.ShapeDtypeStruct((rows, width), jnp.bfloat16),
        grid=(heads_here,),
        in_specs=[
            pl.BlockSpec((rows, HD), lambda h: (0, h)),
            pl.BlockSpec((keys_total, HD), lambda h: (0, h)),
            pl.BlockSpec((keys_total, HD), lambda h: (0, h + heads_here)),
            pl.BlockSpec((rows, keys_total), lambda h: (0, 0)),
        ],
        out_specs=pl.BlockSpec((rows, HD), lambda h: (0, h)),
        cost_estimate=pl.CostEstimate(
            flops=4 * rows * keys_total * width,
            transcendentals=2 * rows * keys_total * heads_here,
            bytes_accessed=2 * (2 * rows * width + 2 * keys_total * width) + 4 * rows * keys_total,
        ),
    )(queries, all_kv, all_kv, bias)


def local(queries, keys, values, out_grad, proj_weight, layout):
    tok_dev = queries.shape[0]
    width = queries.shape[1]
    heads_here = width // HD
    blocks_dev = tok_dev // BLK
    block_count = layout.shape[0]
    summary_count = block_count // STRIDE
    score_scale = HD ** (-0.5)
    me = lax.axis_index("seq")
    first_block = me * blocks_dev
    offset_block = layout[block_count - 1, 0] % STRIDE
    reach_back = (LOCAL - 2) // blocks_dev + 1
    span_blocks = [
        min(blocks_dev, LOCAL - 1 - hop_index * blocks_dev) for hop_index in range(reach_back)
    ]
    back_blocks = sum(span_blocks)
    pool_blocks = back_blocks + blocks_dev

    attn_grad = jnp.dot(out_grad, proj_weight, preferred_element_type=jnp.float32).astype(
        jnp.bfloat16
    )
    kv = jnp.concatenate([keys, values], axis=1)

    seq_size = lax.axis_size("seq")
    group = STRIDE // blocks_dev
    groups = seq_size // group
    assert groups == summary_count == 4 and group == 8
    far_ids = jnp.arange(summary_count, dtype=jnp.int32) * STRIDE + offset_block
    lead = offset_block // blocks_dev
    sum_local = offset_block % blocks_dev
    in_group = me % group
    my_group = me // group
    rel = (in_group - lead) % group
    win_kv, far_blocks = exchange(kv, lead, sum_local, span_blocks, seq_size, group)
    pool_kv = jnp.concatenate([win_kv, kv], axis=0)
    far_kv = far_blocks.reshape(summary_count * BLK, 2 * width)

    all_kv = jnp.concatenate([pool_kv, far_kv], axis=0)
    key_rows = all_kv[:, :width].reshape(-1, heads_here, HD)
    value_rows = all_kv[:, width:].reshape(-1, heads_here, HD)
    query_rows = queries.reshape(tok_dev, heads_here, HD)
    grad_rows = attn_grad.reshape(tok_dev, heads_here, HD)

    own_ids = first_block + jnp.arange(blocks_dev, dtype=jnp.int32)
    table_rows = lax.dynamic_slice_in_dim(layout, first_block, blocks_dev, 0)
    pool_ids = first_block - back_blocks + jnp.arange(pool_blocks, dtype=jnp.int32)
    pool_ids_b = jnp.broadcast_to(pool_ids[None, :], (blocks_dev, pool_blocks))
    plain = (pool_ids_b % STRIDE != offset_block) | (pool_ids_b == own_ids[:, None])
    pool_ok = listed(table_rows, pool_ids_b) & plain
    far_ids_b = jnp.broadcast_to(far_ids[None, :], (blocks_dev, summary_count))
    far_ok = listed(table_rows, far_ids_b) & (far_ids_b < own_ids[:, None])
    block_ok = jnp.concatenate([pool_ok, far_ok], axis=1)
    token_ok = jnp.repeat(jnp.repeat(block_ok, BLK, axis=0), BLK, axis=1)
    query_pos = jnp.arange(tok_dev, dtype=jnp.int32)
    pool_pos = jnp.arange(pool_blocks * BLK, dtype=jnp.int32) - back_blocks * BLK
    causal = jnp.concatenate(
        [
            pool_pos[None, :] <= query_pos[:, None],
            jnp.ones((tok_dev, summary_count * BLK), jnp.bool_),
        ],
        axis=1,
    )
    allowed = token_ok & causal

    scores = (
        jnp.einsum("qhd,khd->hqk", query_rows, key_rows, preferred_element_type=jnp.float32)
        * score_scale
    )
    scores = jnp.where(allowed[None], scores, -jnp.inf)
    row_top = jnp.max(scores, axis=-1, keepdims=True)
    log_total = row_top + jnp.log(jnp.sum(jnp.exp(scores - row_top), axis=-1, keepdims=True))
    probs = jnp.exp(scores - log_total)
    probs_low = probs.astype(jnp.bfloat16)
    bias = jnp.where(allowed, 0.0, -jnp.inf).astype(jnp.float32)
    attn_out = attention_out(queries, all_kv, bias, score_scale).reshape(tok_dev, heads_here, HD)
    delta = jnp.transpose(
        jnp.sum(attn_out.astype(jnp.float32) * grad_rows.astype(jnp.float32), axis=-1)
    )[..., None]
    dprobs = jnp.einsum("qhd,khd->hqk", grad_rows, value_rows, preferred_element_type=jnp.float32)
    dscores = (score_scale * probs * (dprobs - delta)).astype(jnp.bfloat16)
    query_grad = jnp.einsum(
        "hqk,khd->qhd", dscores, key_rows, preferred_element_type=jnp.float32
    ).astype(jnp.bfloat16)
    key_part = jnp.einsum("hqk,qhd->khd", dscores, query_rows, preferred_element_type=jnp.float32)
    value_part = jnp.einsum(
        "hqk,qhd->khd", probs_low, grad_rows, preferred_element_type=jnp.float32
    )
    grad_kv = jnp.concatenate(
        [key_part.reshape(-1, width), value_part.reshape(-1, width)], axis=1
    )

    part = grad_kv[pool_blocks * BLK :].reshape(summary_count, BLK, 2 * width)
    span = groups // 2
    while span >= 1:
        half = part.shape[0] // 2
        upper = (my_group // span) % 2 == 1
        keep = jnp.where(upper, part[half:], part[:half])
        send = jnp.where(upper, part[:half], part[half:])
        route = [(d, d ^ (span * group)) for d in range(seq_size)]
        part = keep + lax.ppermute(send.astype(jnp.bfloat16), "seq", route).astype(jnp.float32)
        span //= 2
    part = part[0]
    hop = group // 2
    while hop >= 1:
        route = [(g * group + (r + hop) % group, g * group + r) for g in range(groups) for r in range(group)]
        moved = lax.ppermute(part.astype(jnp.bfloat16), "seq", route).astype(jnp.float32)
        part = jnp.where(rel < hop, part + moved, part)
        hop //= 2
    own_local = jnp.arange(blocks_dev, dtype=jnp.int32)
    far_here = (rel == 0) & (own_local == sum_local)
    far_add = jnp.where(far_here[:, None, None], part[None], 0.0)

    own_grad = grad_kv[back_blocks * BLK : pool_blocks * BLK]
    pool_start = 0
    for distance in range(reach_back, 0, -1):
        rows_needed = span_blocks[distance - 1] * BLK
        back = passed_along(
            grad_kv[pool_start : pool_start + rows_needed].astype(jnp.bfloat16), "seq", -distance
        ).astype(jnp.float32)
        own_grad = own_grad.at[tok_dev - rows_needed :].add(back)
        pool_start = pool_start + rows_needed
    total = own_grad.reshape(blocks_dev, BLK, 2 * width) + far_add
    total = total.reshape(tok_dev, 2 * width).astype(jnp.bfloat16)

    proj_grad = lax.psum_scatter(
        lax.dot_general(
            out_grad,
            attn_out.reshape(tok_dev, width),
            (((0,), (0,)), ((), ())),
            preferred_element_type=jnp.float32,
        ),
        "seq",
        scatter_dimension=0,
        tiled=True,
    )
    return (
        query_grad.reshape(tok_dev, width),
        total[:, :width],
        total[:, width:],
        proj_grad,
    )


def solution(mesh):
    return jax.shard_map(
        local,
        mesh=mesh,
        in_specs=(
            P(("dp", "seq"), "head"),
            P(("dp", "seq"), "head"),
            P(("dp", "seq"), "head"),
            P(("dp", "seq"), None),
            P(None, "head"),
            P(),
        ),
        out_specs=(
            P(("dp", "seq"), "head"),
            P(("dp", "seq"), "head"),
            P(("dp", "seq"), "head"),
            P(("dp", "seq"), "head"),
        ),
        check_vma=False,
    )
```

```python
import functools

import jax
import jax.numpy as jnp
from jax import lax
from jax.experimental import pallas as pl
from jax.experimental.pallas import tpu as pltpu
from jax.sharding import PartitionSpec as P

HD = 128
BLK = 128
LOCAL = 8
STRIDE = 16


def passed_along(block, axis, distance):
    devices = range(lax.axis_size(axis))
    route = [(i - distance, i) for i in devices if i - distance in devices]
    return lax.ppermute(block, axis, route)


def listed(table_rows, block_ids):
    hit = jnp.any(table_rows[:, None, :] == block_ids[:, :, None], axis=2)
    return hit & (block_ids >= 0)


def exchange_kernel(dims, ctl_ref, kv_ref, win_out, far_out, win_buf, hop_buf, cross1, cross2, held, pair, sends, recvs):
    seq_size, group, spans = dims
    groups = seq_size // group
    me = lax.axis_index("seq")
    in_group = me % group
    base = me - in_group
    my_group = me // group
    lead = ctl_ref[0]
    sum_local = ctl_ref[1]
    lanes = group // 2
    lane = in_group % lanes
    lane_base = in_group - lane
    rel_lane = (lane - lead + lanes) % lanes
    mesh_id = pl.DeviceIdType.MESH

    def ring(step):
        return (me + step + seq_size) % seq_size

    def in_ring(step):
        return base + lane_base + (lane + step + lanes) % lanes

    def flip():
        return me + lanes - 2 * lanes * (in_group // lanes)

    def across(span):
        upper = (my_group // span) % 2
        return me + span * group - 2 * span * group * upper

    barrier = pltpu.get_barrier_semaphore()
    partners = []
    for distance in range(1, len(spans) + 1):
        partners += [ring(distance), ring(-distance)]
    for hop in (1, 2):
        partners += [in_ring(hop), in_ring(-hop)]
    partners += [flip(), flip()]
    span = 1
    while span < groups:
        partners += [across(span), across(span)]
        span *= 2
    for partner in partners:
        pl.semaphore_signal(barrier, 1, device_id={"seq": partner}, device_id_type=mesh_id)
    pl.semaphore_wait(barrier, len(partners))

    tok_dev = kv_ref.shape[0]
    window = []
    starts = {}
    start = 0
    for distance in range(len(spans), 0, -1):
        starts[distance] = start
        start += spans[distance - 1] * BLK

    def send_window(distance):
        rows = spans[distance - 1] * BLK
        copy = pltpu.make_async_remote_copy(
            src_ref=kv_ref.at[pl.ds(tok_dev - rows, rows)],
            dst_ref=win_buf.at[pl.ds(starts[distance], rows)],
            send_sem=sends.at[distance - 1],
            recv_sem=recvs.at[distance - 1],
            device_id={"seq": ring(distance)},
            device_id_type=mesh_id,
        )
        copy.start()
        window.append(copy)

    mine = kv_ref[0:BLK, :]
    for block in range(1, tok_dev // BLK):
        mine = jnp.where(sum_local == block, kv_ref[block * BLK : (block + 1) * BLK, :], mine)
    held[...] = mine
    slot = len(spans)
    steps = [(in_ring(1), rel_lane == 1), (in_ring(2), rel_lane >= 2), (flip(), in_group >= lanes)]
    for stage, (target, take) in enumerate(steps):
        copy = pltpu.make_async_remote_copy(
            src_ref=held,
            dst_ref=hop_buf.at[stage],
            send_sem=sends.at[slot],
            recv_sem=recvs.at[slot],
            device_id={"seq": target},
            device_id_type=mesh_id,
        )
        copy.start()
        copy.wait()
        held[...] = jnp.where(take, hop_buf[stage], held[...])
        slot += 1

    copy = pltpu.make_async_remote_copy(
        src_ref=held,
        dst_ref=cross1,
        send_sem=sends.at[slot],
        recv_sem=recvs.at[slot],
        device_id={"seq": across(1)},
        device_id_type=mesh_id,
    )
    copy.start()
    copy.wait()
    upper = (my_group % 2) == 1
    pair[0] = jnp.where(upper, cross1[...], held[...])
    pair[1] = jnp.where(upper, held[...], cross1[...])
    slot += 1
    copy = pltpu.make_async_remote_copy(
        src_ref=pair,
        dst_ref=cross2,
        send_sem=sends.at[slot],
        recv_sem=recvs.at[slot],
        device_id={"seq": across(2)},
        device_id_type=mesh_id,
    )
    copy.start()
    copy.wait()
    for distance in range(len(spans), 0, -1):
        send_window(distance)
    upper = ((my_group // 2) % 2) == 1
    for index in range(2):
        far_out[index] = jnp.where(upper, cross2[index], pair[index])
        far_out[2 + index] = jnp.where(upper, pair[index], cross2[index])
    for copy in window:
        copy.wait()
    win_out[...] = win_buf[...]


def exchange(kv, lead, sum_local, spans, seq_size, group):
    tok_dev, cols = kv.shape
    back_rows = sum(spans) * BLK
    groups = seq_size // group
    copies = len(spans) + 5
    ctl = jnp.stack([lead, sum_local]).astype(jnp.int32)
    return pl.pallas_call(
        functools.partial(exchange_kernel, (seq_size, group, spans)),
        out_shape=(
            jax.ShapeDtypeStruct((back_rows, cols), kv.dtype),
            jax.ShapeDtypeStruct((groups, BLK, cols), kv.dtype),
        ),
        in_specs=[
            pl.BlockSpec(memory_space=pltpu.SMEM),
            pl.BlockSpec(memory_space=pltpu.VMEM),
        ],
        out_specs=(
            pl.BlockSpec(memory_space=pltpu.VMEM),
            pl.BlockSpec(memory_space=pltpu.VMEM),
        ),
        scratch_shapes=[
            pltpu.VMEM((back_rows, cols), kv.dtype),
            pltpu.VMEM((3, BLK, cols), kv.dtype),
            pltpu.VMEM((BLK, cols), kv.dtype),
            pltpu.VMEM((2, BLK, cols), kv.dtype),
            pltpu.VMEM((BLK, cols), kv.dtype),
            pltpu.VMEM((2, BLK, cols), kv.dtype),
            pltpu.SemaphoreType.DMA((copies,)),
            pltpu.SemaphoreType.DMA((copies,)),
        ],
        compiler_params=pltpu.CompilerParams(
            collective_id=0, has_side_effects=True, vmem_limit_bytes=48 * 1024 * 1024
        ),
    )(ctl, kv)


def forward_kernel(scale, q_ref, k_ref, v_ref, bias_ref, o_ref):
    scores = lax.dot_general(
        q_ref[...], k_ref[...], (((1,), (1,)), ((), ())), preferred_element_type=jnp.float32
    )
    scores = scores * scale + bias_ref[...]
    row_top = jnp.max(scores, axis=1, keepdims=True)
    log_total = row_top + jnp.log(jnp.sum(jnp.exp(scores - row_top), axis=1, keepdims=True))
    probs_low = jnp.exp(scores - log_total).astype(jnp.bfloat16)
    o_ref[...] = jnp.dot(probs_low, v_ref[...], preferred_element_type=jnp.float32).astype(o_ref.dtype)


def attention_out(queries, all_kv, bias, scale):
    rows, width = queries.shape
    keys_total = all_kv.shape[0]
    heads_here = width // HD
    return pl.pallas_call(
        functools.partial(forward_kernel, scale),
        out_shape=jax.ShapeDtypeStruct((rows, width), jnp.bfloat16),
        grid=(heads_here,),
        in_specs=[
            pl.BlockSpec((rows, HD), lambda h: (0, h)),
            pl.BlockSpec((keys_total, HD), lambda h: (0, h)),
            pl.BlockSpec((keys_total, HD), lambda h: (0, h + heads_here)),
            pl.BlockSpec((rows, keys_total), lambda h: (0, 0)),
        ],
        out_specs=pl.BlockSpec((rows, HD), lambda h: (0, h)),
        cost_estimate=pl.CostEstimate(
            flops=4 * rows * keys_total * width,
            transcendentals=2 * rows * keys_total * heads_here,
            bytes_accessed=2 * (2 * rows * width + 2 * keys_total * width) + 4 * rows * keys_total,
        ),
    )(queries, all_kv, all_kv, bias)


def local(queries, keys, values, out_grad, proj_weight, layout):
    tok_dev = queries.shape[0]
    width = queries.shape[1]
    heads_here = width // HD
    blocks_dev = tok_dev // BLK
    block_count = layout.shape[0]
    summary_count = block_count // STRIDE
    score_scale = HD ** (-0.5)
    me = lax.axis_index("seq")
    first_block = me * blocks_dev
    offset_block = layout[block_count - 1, 0] % STRIDE
    reach_back = (LOCAL - 2) // blocks_dev + 1
    span_blocks = [
        min(blocks_dev, LOCAL - 1 - hop_index * blocks_dev) for hop_index in range(reach_back)
    ]
    back_blocks = sum(span_blocks)
    pool_blocks = back_blocks + blocks_dev

    attn_grad = jnp.dot(out_grad, proj_weight, preferred_element_type=jnp.float32).astype(
        jnp.bfloat16
    )
    kv = jnp.concatenate([keys, values], axis=1)

    seq_size = lax.axis_size("seq")
    group = STRIDE // blocks_dev
    groups = seq_size // group
    assert groups == summary_count == 4 and group == 8
    assert (STRIDE - LOCAL) // blocks_dev <= group // 2
    far_ids = jnp.arange(summary_count, dtype=jnp.int32) * STRIDE + offset_block
    lead = offset_block // blocks_dev
    sum_local = offset_block % blocks_dev
    in_group = me % group
    my_group = me // group
    rel = (in_group - lead) % group
    win_kv, far_blocks = exchange(kv, lead, sum_local, span_blocks, seq_size, group)
    pool_kv = jnp.concatenate([win_kv, kv], axis=0)
    far_kv = far_blocks.reshape(summary_count * BLK, 2 * width)

    all_kv = jnp.concatenate([pool_kv, far_kv], axis=0)
    key_rows = all_kv[:, :width].reshape(-1, heads_here, HD)
    value_rows = all_kv[:, width:].reshape(-1, heads_here, HD)
    query_rows = queries.reshape(tok_dev, heads_here, HD)
    grad_rows = attn_grad.reshape(tok_dev, heads_here, HD)

    own_ids = first_block + jnp.arange(blocks_dev, dtype=jnp.int32)
    table_rows = lax.dynamic_slice_in_dim(layout, first_block, blocks_dev, 0)
    pool_ids = first_block - back_blocks + jnp.arange(pool_blocks, dtype=jnp.int32)
    pool_ids_b = jnp.broadcast_to(pool_ids[None, :], (blocks_dev, pool_blocks))
    plain = (pool_ids_b % STRIDE != offset_block) | (pool_ids_b == own_ids[:, None])
    pool_ok = listed(table_rows, pool_ids_b) & plain
    far_ids_b = jnp.broadcast_to(far_ids[None, :], (blocks_dev, summary_count))
    far_ok = listed(table_rows, far_ids_b) & (far_ids_b < own_ids[:, None])
    block_ok = jnp.concatenate([pool_ok, far_ok], axis=1)
    token_ok = jnp.repeat(jnp.repeat(block_ok, BLK, axis=0), BLK, axis=1)
    query_pos = jnp.arange(tok_dev, dtype=jnp.int32)
    pool_pos = jnp.arange(pool_blocks * BLK, dtype=jnp.int32) - back_blocks * BLK
    causal = jnp.concatenate(
        [
            pool_pos[None, :] <= query_pos[:, None],
            jnp.ones((tok_dev, summary_count * BLK), jnp.bool_),
        ],
        axis=1,
    )
    allowed = token_ok & causal

    scores = (
        jnp.einsum("qhd,khd->hqk", query_rows, key_rows, preferred_element_type=jnp.float32)
        * score_scale
    )
    scores = jnp.where(allowed[None], scores, -jnp.inf)
    row_top = jnp.max(scores, axis=-1, keepdims=True)
    log_total = row_top + jnp.log(jnp.sum(jnp.exp(scores - row_top), axis=-1, keepdims=True))
    probs = jnp.exp(scores - log_total)
    probs_low = probs.astype(jnp.bfloat16)
    bias = jnp.where(allowed, 0.0, -jnp.inf).astype(jnp.float32)
    attn_out = attention_out(queries, all_kv, bias, score_scale).reshape(tok_dev, heads_here, HD)
    delta = jnp.transpose(
        jnp.sum(attn_out.astype(jnp.float32) * grad_rows.astype(jnp.float32), axis=-1)
    )[..., None]
    dprobs = jnp.einsum("qhd,khd->hqk", grad_rows, value_rows, preferred_element_type=jnp.float32)
    dscores = (score_scale * probs * (dprobs - delta)).astype(jnp.bfloat16)
    query_grad = jnp.einsum(
        "hqk,khd->qhd", dscores, key_rows, preferred_element_type=jnp.float32
    ).astype(jnp.bfloat16)
    key_part = jnp.einsum("hqk,qhd->khd", dscores, query_rows, preferred_element_type=jnp.float32)
    value_part = jnp.einsum(
        "hqk,qhd->khd", probs_low, grad_rows, preferred_element_type=jnp.float32
    )
    grad_kv = jnp.concatenate(
        [key_part.reshape(-1, width), value_part.reshape(-1, width)], axis=1
    )

    part = grad_kv[pool_blocks * BLK :].reshape(summary_count, BLK, 2 * width)
    span = groups // 2
    while span >= 1:
        half = part.shape[0] // 2
        upper = (my_group // span) % 2 == 1
        keep = jnp.where(upper, part[half:], part[:half])
        send = jnp.where(upper, part[:half], part[half:])
        route = [(d, d ^ (span * group)) for d in range(seq_size)]
        part = keep + lax.ppermute(send.astype(jnp.bfloat16), "seq", route).astype(jnp.float32)
        span //= 2
    part = part[0]
    lanes = group // 2
    lane = in_group % lanes
    rel_lane = (lane - lead) % lanes
    route = [(g * group + (r ^ lanes), g * group + r) for g in range(groups) for r in range(group)]
    moved = lax.ppermute(part.astype(jnp.bfloat16), "seq", route).astype(jnp.float32)
    part = jnp.where(in_group < lanes, part + moved, part)
    for hop in (2, 1):
        route = [
            (g * group + r - r % lanes + (r % lanes + hop) % lanes, g * group + r)
            for g in range(groups)
            for r in range(group)
        ]
        moved = lax.ppermute(part.astype(jnp.bfloat16), "seq", route).astype(jnp.float32)
        part = jnp.where(rel_lane < hop, part + moved, part)
    own_local = jnp.arange(blocks_dev, dtype=jnp.int32)
    far_here = (rel == 0) & (own_local == sum_local)
    far_add = jnp.where(far_here[:, None, None], part[None], 0.0)

    own_grad = grad_kv[back_blocks * BLK : pool_blocks * BLK]
    pool_start = 0
    for distance in range(reach_back, 0, -1):
        rows_needed = span_blocks[distance - 1] * BLK
        back = passed_along(
            grad_kv[pool_start : pool_start + rows_needed].astype(jnp.bfloat16), "seq", -distance
        ).astype(jnp.float32)
        own_grad = own_grad.at[tok_dev - rows_needed :].add(back)
        pool_start = pool_start + rows_needed
    total = own_grad.reshape(blocks_dev, BLK, 2 * width) + far_add
    total = total.reshape(tok_dev, 2 * width).astype(jnp.bfloat16)

    proj_grad = lax.psum_scatter(
        lax.dot_general(
            out_grad,
            attn_out.reshape(tok_dev, width),
            (((0,), (0,)), ((), ())),
            preferred_element_type=jnp.float32,
        ),
        "seq",
        scatter_dimension=0,
        tiled=True,
    )
    return (
        query_grad.reshape(tok_dev, width),
        total[:, :width],
        total[:, width:],
        proj_grad,
    )


def solution(mesh):
    return jax.shard_map(
        local,
        mesh=mesh,
        in_specs=(
            P(("dp", "seq"), "head"),
            P(("dp", "seq"), "head"),
            P(("dp", "seq"), "head"),
            P(("dp", "seq"), None),
            P(None, "head"),
            P(),
        ),
        out_specs=(
            P(("dp", "seq"), "head"),
            P(("dp", "seq"), "head"),
            P(("dp", "seq"), "head"),
            P(("dp", "seq"), "head"),
        ),
        check_vma=False,
    )
```

```python
import functools

import jax
import jax.numpy as jnp
from jax import lax
from jax.experimental import pallas as pl
from jax.experimental.pallas import tpu as pltpu
from jax.sharding import PartitionSpec as P

HD = 128
BLK = 128
LOCAL = 8
STRIDE = 16


def passed_along(block, axis, distance):
    devices = range(lax.axis_size(axis))
    route = [(i - distance, i) for i in devices if i - distance in devices]
    return lax.ppermute(block, axis, route)


def listed(table_rows, block_ids):
    hit = jnp.any(table_rows[:, None, :] == block_ids[:, :, None], axis=2)
    return hit & (block_ids >= 0)


def exchange_kernel(dims, ctl_ref, kv_ref, win_out, far_out, win_buf, hop_buf, cross1, cross2, held, pair, sends, recvs):
    seq_size, group, spans = dims
    groups = seq_size // group
    me = lax.axis_index("seq")
    in_group = me % group
    base = me - in_group
    my_group = me // group
    lead = ctl_ref[0]
    sum_local = ctl_ref[1]
    lanes = group // 2
    lane = in_group % lanes
    lane_base = in_group - lane
    rel_lane = (lane - lead + lanes) % lanes
    mesh_id = pl.DeviceIdType.MESH

    def ring(step):
        return (me + step + seq_size) % seq_size

    def in_ring(step):
        return base + lane_base + (lane + step + lanes) % lanes

    def flip():
        return me + lanes - 2 * lanes * (in_group // lanes)

    def across(span):
        upper = (my_group // span) % 2
        return me + span * group - 2 * span * group * upper

    barrier = pltpu.get_barrier_semaphore()
    partners = []
    for distance in range(1, len(spans) + 1):
        partners += [ring(distance), ring(-distance)]
    for hop in (1, 2):
        partners += [in_ring(hop), in_ring(-hop)]
    partners += [flip(), flip()]
    span = 1
    while span < groups:
        partners += [across(span), across(span)]
        span *= 2
    for partner in partners:
        pl.semaphore_signal(barrier, 1, device_id={"seq": partner}, device_id_type=mesh_id)
    pl.semaphore_wait(barrier, len(partners))

    tok_dev = kv_ref.shape[0]
    window = []
    starts = {}
    start = 0
    for distance in range(len(spans), 0, -1):
        starts[distance] = start
        start += spans[distance - 1] * BLK

    def send_window(distance):
        rows = spans[distance - 1] * BLK
        copy = pltpu.make_async_remote_copy(
            src_ref=kv_ref.at[pl.ds(tok_dev - rows, rows)],
            dst_ref=win_buf.at[pl.ds(starts[distance], rows)],
            send_sem=sends.at[distance - 1],
            recv_sem=recvs.at[distance - 1],
            device_id={"seq": ring(distance)},
            device_id_type=mesh_id,
        )
        copy.start()
        window.append(copy)

    mine = kv_ref[0:BLK, :]
    for block in range(1, tok_dev // BLK):
        mine = jnp.where(sum_local == block, kv_ref[block * BLK : (block + 1) * BLK, :], mine)
    held[...] = mine
    slot = len(spans)
    steps = [(in_ring(1), rel_lane == 1), (in_ring(2), rel_lane >= 2), (flip(), in_group >= lanes)]
    for stage, (target, take) in enumerate(steps):
        copy = pltpu.make_async_remote_copy(
            src_ref=held,
            dst_ref=hop_buf.at[stage],
            send_sem=sends.at[slot],
            recv_sem=recvs.at[slot],
            device_id={"seq": target},
            device_id_type=mesh_id,
        )
        copy.start()
        copy.wait()
        held[...] = jnp.where(take, hop_buf[stage], held[...])
        slot += 1

    copy = pltpu.make_async_remote_copy(
        src_ref=held,
        dst_ref=cross1,
        send_sem=sends.at[slot],
        recv_sem=recvs.at[slot],
        device_id={"seq": across(1)},
        device_id_type=mesh_id,
    )
    copy.start()
    copy.wait()
    upper = (my_group % 2) == 1
    pair[0] = jnp.where(upper, cross1[...], held[...])
    pair[1] = jnp.where(upper, held[...], cross1[...])
    slot += 1
    copy = pltpu.make_async_remote_copy(
        src_ref=pair,
        dst_ref=cross2,
        send_sem=sends.at[slot],
        recv_sem=recvs.at[slot],
        device_id={"seq": across(2)},
        device_id_type=mesh_id,
    )
    copy.start()
    copy.wait()
    for distance in range(len(spans), 0, -1):
        send_window(distance)
    upper = ((my_group // 2) % 2) == 1
    for index in range(2):
        far_out[index] = jnp.where(upper, cross2[index], pair[index])
        far_out[2 + index] = jnp.where(upper, pair[index], cross2[index])
    for copy in window:
        copy.wait()
    win_out[...] = win_buf[...]


def exchange(kv, lead, sum_local, spans, seq_size, group):
    tok_dev, cols = kv.shape
    back_rows = sum(spans) * BLK
    groups = seq_size // group
    copies = len(spans) + 5
    ctl = jnp.stack([lead, sum_local]).astype(jnp.int32)
    return pl.pallas_call(
        functools.partial(exchange_kernel, (seq_size, group, spans)),
        out_shape=(
            jax.ShapeDtypeStruct((back_rows, cols), kv.dtype),
            jax.ShapeDtypeStruct((groups, BLK, cols), kv.dtype),
        ),
        in_specs=[
            pl.BlockSpec(memory_space=pltpu.SMEM),
            pl.BlockSpec(memory_space=pltpu.VMEM),
        ],
        out_specs=(
            pl.BlockSpec(memory_space=pltpu.VMEM),
            pl.BlockSpec(memory_space=pltpu.VMEM),
        ),
        scratch_shapes=[
            pltpu.VMEM((back_rows, cols), kv.dtype),
            pltpu.VMEM((3, BLK, cols), kv.dtype),
            pltpu.VMEM((BLK, cols), kv.dtype),
            pltpu.VMEM((2, BLK, cols), kv.dtype),
            pltpu.VMEM((BLK, cols), kv.dtype),
            pltpu.VMEM((2, BLK, cols), kv.dtype),
            pltpu.SemaphoreType.DMA((copies,)),
            pltpu.SemaphoreType.DMA((copies,)),
        ],
        compiler_params=pltpu.CompilerParams(
            collective_id=0, has_side_effects=True, vmem_limit_bytes=48 * 1024 * 1024
        ),
    )(ctl, kv)


def forward_kernel(scale, q_ref, k_ref, v_ref, bias_ref, o_ref):
    scores = lax.dot_general(
        q_ref[...], k_ref[...], (((1,), (1,)), ((), ())), preferred_element_type=jnp.float32
    )
    scores = scores * scale + bias_ref[...]
    row_top = jnp.max(scores, axis=1, keepdims=True)
    log_total = row_top + jnp.log(jnp.sum(jnp.exp(scores - row_top), axis=1, keepdims=True))
    probs_low = jnp.exp(scores - log_total).astype(jnp.bfloat16)
    o_ref[...] = jnp.dot(probs_low, v_ref[...], preferred_element_type=jnp.float32).astype(o_ref.dtype)


def attention_out(queries, all_kv, bias, scale):
    rows, width = queries.shape
    keys_total = all_kv.shape[0]
    heads_here = width // HD
    return pl.pallas_call(
        functools.partial(forward_kernel, scale),
        out_shape=jax.ShapeDtypeStruct((rows, width), jnp.bfloat16),
        grid=(heads_here,),
        in_specs=[
            pl.BlockSpec((rows, HD), lambda h: (0, h)),
            pl.BlockSpec((keys_total, HD), lambda h: (0, h)),
            pl.BlockSpec((keys_total, HD), lambda h: (0, h + heads_here)),
            pl.BlockSpec((rows, keys_total), lambda h: (0, 0)),
        ],
        out_specs=pl.BlockSpec((rows, HD), lambda h: (0, h)),
        cost_estimate=pl.CostEstimate(
            flops=4 * rows * keys_total * width,
            transcendentals=2 * rows * keys_total * heads_here,
            bytes_accessed=2 * (2 * rows * width + 2 * keys_total * width) + 4 * rows * keys_total,
        ),
    )(queries, all_kv, all_kv, bias)


def local(queries, keys, values, out_grad, proj_weight, layout):
    tok_dev = queries.shape[0]
    width = queries.shape[1]
    heads_here = width // HD
    blocks_dev = tok_dev // BLK
    block_count = layout.shape[0]
    summary_count = block_count // STRIDE
    score_scale = HD ** (-0.5)
    me = lax.axis_index("seq")
    first_block = me * blocks_dev
    offset_block = layout[block_count - 1, 0] % STRIDE
    reach_back = (LOCAL - 2) // blocks_dev + 1
    span_blocks = [
        min(blocks_dev, LOCAL - 1 - hop_index * blocks_dev) for hop_index in range(reach_back)
    ]
    back_blocks = sum(span_blocks)
    pool_blocks = back_blocks + blocks_dev

    attn_grad = jnp.dot(out_grad, proj_weight, preferred_element_type=jnp.float32).astype(
        jnp.bfloat16
    )
    kv = jnp.concatenate([keys, values], axis=1)

    seq_size = lax.axis_size("seq")
    group = STRIDE // blocks_dev
    groups = seq_size // group
    assert groups == summary_count == 4 and group == 8
    assert (STRIDE - LOCAL) // blocks_dev <= group // 2 and group == 8
    far_ids = jnp.arange(summary_count, dtype=jnp.int32) * STRIDE + offset_block
    lead = offset_block // blocks_dev
    sum_local = offset_block % blocks_dev
    in_group = me % group
    my_group = me // group
    rel = (in_group - lead) % group
    win_kv, far_blocks = exchange(kv, lead, sum_local, span_blocks, seq_size, group)
    pool_kv = jnp.concatenate([win_kv, kv], axis=0)
    far_kv = far_blocks.reshape(summary_count * BLK, 2 * width)

    all_kv = jnp.concatenate([pool_kv, far_kv], axis=0)
    key_rows = all_kv[:, :width].reshape(-1, heads_here, HD)
    value_rows = all_kv[:, width:].reshape(-1, heads_here, HD)
    query_rows = queries.reshape(tok_dev, heads_here, HD)
    grad_rows = attn_grad.reshape(tok_dev, heads_here, HD)

    own_ids = first_block + jnp.arange(blocks_dev, dtype=jnp.int32)
    table_rows = lax.dynamic_slice_in_dim(layout, first_block, blocks_dev, 0)
    pool_ids = first_block - back_blocks + jnp.arange(pool_blocks, dtype=jnp.int32)
    pool_ids_b = jnp.broadcast_to(pool_ids[None, :], (blocks_dev, pool_blocks))
    plain = (pool_ids_b % STRIDE != offset_block) | (pool_ids_b == own_ids[:, None])
    pool_ok = listed(table_rows, pool_ids_b) & plain
    far_ids_b = jnp.broadcast_to(far_ids[None, :], (blocks_dev, summary_count))
    far_ok = listed(table_rows, far_ids_b) & (far_ids_b < own_ids[:, None])
    block_ok = jnp.concatenate([pool_ok, far_ok], axis=1)
    token_ok = jnp.repeat(jnp.repeat(block_ok, BLK, axis=0), BLK, axis=1)
    query_pos = jnp.arange(tok_dev, dtype=jnp.int32)
    pool_pos = jnp.arange(pool_blocks * BLK, dtype=jnp.int32) - back_blocks * BLK
    causal = jnp.concatenate(
        [
            pool_pos[None, :] <= query_pos[:, None],
            jnp.ones((tok_dev, summary_count * BLK), jnp.bool_),
        ],
        axis=1,
    )
    allowed = token_ok & causal

    scores = (
        jnp.einsum("qhd,khd->hqk", query_rows, key_rows, preferred_element_type=jnp.float32)
        * score_scale
    )
    scores = jnp.where(allowed[None], scores, -jnp.inf)
    row_top = jnp.max(scores, axis=-1, keepdims=True)
    log_total = row_top + jnp.log(jnp.sum(jnp.exp(scores - row_top), axis=-1, keepdims=True))
    probs = jnp.exp(scores - log_total)
    probs_low = probs.astype(jnp.bfloat16)
    bias = jnp.where(allowed, 0.0, -jnp.inf).astype(jnp.float32)
    attn_out = attention_out(queries, all_kv, bias, score_scale).reshape(tok_dev, heads_here, HD)
    delta = jnp.transpose(
        jnp.sum(attn_out.astype(jnp.float32) * grad_rows.astype(jnp.float32), axis=-1)
    )[..., None]
    dprobs = jnp.einsum("qhd,khd->hqk", grad_rows, value_rows, preferred_element_type=jnp.float32)
    dscores = (score_scale * probs * (dprobs - delta)).astype(jnp.bfloat16)
    query_grad = jnp.einsum(
        "hqk,khd->qhd", dscores, key_rows, preferred_element_type=jnp.float32
    ).astype(jnp.bfloat16)
    key_part = jnp.einsum("hqk,qhd->khd", dscores, query_rows, preferred_element_type=jnp.float32)
    value_part = jnp.einsum(
        "hqk,qhd->khd", probs_low, grad_rows, preferred_element_type=jnp.float32
    )
    grad_kv = jnp.concatenate(
        [key_part.reshape(-1, width), value_part.reshape(-1, width)], axis=1
    )

    part = grad_kv[pool_blocks * BLK :].reshape(summary_count, BLK, 2 * width)
    span = groups // 2
    while span >= 1:
        half = part.shape[0] // 2
        upper = (my_group // span) % 2 == 1
        keep = jnp.where(upper, part[half:], part[:half])
        send = jnp.where(upper, part[:half], part[half:])
        route = [(d, d ^ (span * group)) for d in range(seq_size)]
        part = keep + lax.ppermute(send.astype(jnp.bfloat16), "seq", route).astype(jnp.float32)
        span //= 2
    part = part[0]
    lanes = group // 2
    lane = in_group % lanes
    rel_lane = (lane - lead) % lanes
    route = [(g * group + (r ^ lanes), g * group + r) for g in range(groups) for r in range(group)]
    moved = lax.ppermute(part.astype(jnp.bfloat16), "seq", route).astype(jnp.float32)
    part = jnp.where(in_group < lanes, part + moved, part)
    def from_lane(hop):
        return [
            (g * group + r - r % lanes + (r % lanes + hop) % lanes, g * group + r)
            for g in range(groups)
            for r in range(group)
        ]

    sent = part.astype(jnp.bfloat16)
    ahead = lax.ppermute(sent, "seq", from_lane(1)).astype(jnp.float32)
    behind = lax.ppermute(sent, "seq", from_lane(-1)).astype(jnp.float32)
    part = part + jnp.where(rel_lane == 1, ahead, 0.0) + jnp.where(rel_lane == 0, behind, 0.0)
    ahead = lax.ppermute(part.astype(jnp.bfloat16), "seq", from_lane(1)).astype(jnp.float32)
    part = jnp.where(rel_lane == 0, part + ahead, part)
    own_local = jnp.arange(blocks_dev, dtype=jnp.int32)
    far_here = (rel == 0) & (own_local == sum_local)
    far_add = jnp.where(far_here[:, None, None], part[None], 0.0)

    own_grad = grad_kv[back_blocks * BLK : pool_blocks * BLK]
    pool_start = 0
    for distance in range(reach_back, 0, -1):
        rows_needed = span_blocks[distance - 1] * BLK
        back = passed_along(
            grad_kv[pool_start : pool_start + rows_needed].astype(jnp.bfloat16), "seq", -distance
        ).astype(jnp.float32)
        own_grad = own_grad.at[tok_dev - rows_needed :].add(back)
        pool_start = pool_start + rows_needed
    total = own_grad.reshape(blocks_dev, BLK, 2 * width) + far_add
    total = total.reshape(tok_dev, 2 * width).astype(jnp.bfloat16)

    proj_grad = lax.psum_scatter(
        lax.dot_general(
            out_grad,
            attn_out.reshape(tok_dev, width),
            (((0,), (0,)), ((), ())),
            preferred_element_type=jnp.float32,
        ),
        "seq",
        scatter_dimension=0,
        tiled=True,
    )
    return (
        query_grad.reshape(tok_dev, width),
        total[:, :width],
        total[:, width:],
        proj_grad,
    )


def solution(mesh):
    return jax.shard_map(
        local,
        mesh=mesh,
        in_specs=(
            P(("dp", "seq"), "head"),
            P(("dp", "seq"), "head"),
            P(("dp", "seq"), "head"),
            P(("dp", "seq"), None),
            P(None, "head"),
            P(),
        ),
        out_specs=(
            P(("dp", "seq"), "head"),
            P(("dp", "seq"), "head"),
            P(("dp", "seq"), "head"),
            P(("dp", "seq"), "head"),
        ),
        check_vma=False,
    )
```

```python
import functools

import jax
import jax.numpy as jnp
from jax import lax
from jax.experimental import pallas as pl
from jax.experimental.pallas import tpu as pltpu
from jax.sharding import PartitionSpec as P

HD = 128
BLK = 128
LOCAL = 8
STRIDE = 16


def passed_along(block, axis, distance):
    devices = range(lax.axis_size(axis))
    route = [(i - distance, i) for i in devices if i - distance in devices]
    return lax.ppermute(block, axis, route)


def listed(table_rows, block_ids):
    hit = jnp.any(table_rows[:, None, :] == block_ids[:, :, None], axis=2)
    return hit & (block_ids >= 0)


def exchange_kernel(dims, ctl_ref, kv_ref, win_out, far_out, win_buf, hop_buf, cross1, cross2, held, pair, sends, recvs):
    seq_size, group, spans = dims
    groups = seq_size // group
    me = lax.axis_index("seq")
    in_group = me % group
    base = me - in_group
    my_group = me // group
    lead = ctl_ref[0]
    sum_local = ctl_ref[1]
    lanes = group // 2
    lane = in_group % lanes
    lane_base = in_group - lane
    rel_lane = (lane - lead + lanes) % lanes
    mesh_id = pl.DeviceIdType.MESH

    def ring(step):
        return (me + step + seq_size) % seq_size

    def in_ring(step):
        return base + lane_base + (lane + step + lanes) % lanes

    def flip():
        return me + lanes - 2 * lanes * (in_group // lanes)

    def across(span):
        upper = (my_group // span) % 2
        return me + span * group - 2 * span * group * upper

    barrier = pltpu.get_barrier_semaphore()
    partners = []
    for distance in range(1, len(spans) + 1):
        partners += [ring(distance), ring(-distance)]
    for hop in (1, 2):
        partners += [in_ring(hop), in_ring(-hop)]
    partners += [flip(), flip()]
    span = 1
    while span < groups:
        partners += [across(span), across(span)]
        span *= 2
    for partner in partners:
        pl.semaphore_signal(barrier, 1, device_id={"seq": partner}, device_id_type=mesh_id)
    pl.semaphore_wait(barrier, len(partners))

    tok_dev = kv_ref.shape[0]
    window = []
    starts = {}
    start = 0
    for distance in range(len(spans), 0, -1):
        starts[distance] = start
        start += spans[distance - 1] * BLK

    def send_window(distance):
        rows = spans[distance - 1] * BLK
        copy = pltpu.make_async_remote_copy(
            src_ref=kv_ref.at[pl.ds(tok_dev - rows, rows)],
            dst_ref=win_buf.at[pl.ds(starts[distance], rows)],
            send_sem=sends.at[distance - 1],
            recv_sem=recvs.at[distance - 1],
            device_id={"seq": ring(distance)},
            device_id_type=mesh_id,
        )
        copy.start()
        window.append(copy)

    mine = kv_ref[0:BLK, :]
    for block in range(1, tok_dev // BLK):
        mine = jnp.where(sum_local == block, kv_ref[block * BLK : (block + 1) * BLK, :], mine)
    held[...] = mine
    slot = len(spans)
    steps = [(in_ring(1), rel_lane == 1), (in_ring(2), rel_lane >= 2), (flip(), in_group >= lanes)]
    for stage, (target, take) in enumerate(steps):
        copy = pltpu.make_async_remote_copy(
            src_ref=held,
            dst_ref=hop_buf.at[stage],
            send_sem=sends.at[slot],
            recv_sem=recvs.at[slot],
            device_id={"seq": target},
            device_id_type=mesh_id,
        )
        copy.start()
        copy.wait()
        held[...] = jnp.where(take, hop_buf[stage], held[...])
        slot += 1

    copy = pltpu.make_async_remote_copy(
        src_ref=held,
        dst_ref=cross1,
        send_sem=sends.at[slot],
        recv_sem=recvs.at[slot],
        device_id={"seq": across(1)},
        device_id_type=mesh_id,
    )
    copy.start()
    copy.wait()
    upper = (my_group % 2) == 1
    pair[0] = jnp.where(upper, cross1[...], held[...])
    pair[1] = jnp.where(upper, held[...], cross1[...])
    slot += 1
    copy = pltpu.make_async_remote_copy(
        src_ref=pair,
        dst_ref=cross2,
        send_sem=sends.at[slot],
        recv_sem=recvs.at[slot],
        device_id={"seq": across(2)},
        device_id_type=mesh_id,
    )
    copy.start()
    copy.wait()
    for distance in range(len(spans), 0, -1):
        send_window(distance)
    upper = ((my_group // 2) % 2) == 1
    for index in range(2):
        far_out[index] = jnp.where(upper, cross2[index], pair[index])
        far_out[2 + index] = jnp.where(upper, pair[index], cross2[index])
    for copy in window:
        copy.wait()
    win_out[...] = win_buf[...]


def exchange(kv, lead, sum_local, spans, seq_size, group):
    tok_dev, cols = kv.shape
    back_rows = sum(spans) * BLK
    groups = seq_size // group
    copies = len(spans) + 5
    ctl = jnp.stack([lead, sum_local]).astype(jnp.int32)
    return pl.pallas_call(
        functools.partial(exchange_kernel, (seq_size, group, spans)),
        out_shape=(
            jax.ShapeDtypeStruct((back_rows, cols), kv.dtype),
            jax.ShapeDtypeStruct((groups, BLK, cols), kv.dtype),
        ),
        in_specs=[
            pl.BlockSpec(memory_space=pltpu.SMEM),
            pl.BlockSpec(memory_space=pltpu.VMEM),
        ],
        out_specs=(
            pl.BlockSpec(memory_space=pltpu.VMEM),
            pl.BlockSpec(memory_space=pltpu.VMEM),
        ),
        scratch_shapes=[
            pltpu.VMEM((back_rows, cols), kv.dtype),
            pltpu.VMEM((3, BLK, cols), kv.dtype),
            pltpu.VMEM((BLK, cols), kv.dtype),
            pltpu.VMEM((2, BLK, cols), kv.dtype),
            pltpu.VMEM((BLK, cols), kv.dtype),
            pltpu.VMEM((2, BLK, cols), kv.dtype),
            pltpu.SemaphoreType.DMA((copies,)),
            pltpu.SemaphoreType.DMA((copies,)),
        ],
        compiler_params=pltpu.CompilerParams(
            collective_id=0, has_side_effects=True, vmem_limit_bytes=48 * 1024 * 1024
        ),
    )(ctl, kv)


def forward_kernel(scale, q_ref, k_ref, v_ref, bias_ref, o_ref):
    scores = lax.dot_general(
        q_ref[...], k_ref[...], (((1,), (1,)), ((), ())), preferred_element_type=jnp.float32
    )
    scores = scores * scale + bias_ref[...]
    row_top = jnp.max(scores, axis=1, keepdims=True)
    log_total = row_top + jnp.log(jnp.sum(jnp.exp(scores - row_top), axis=1, keepdims=True))
    probs_low = jnp.exp(scores - log_total).astype(jnp.bfloat16)
    o_ref[...] = jnp.dot(probs_low, v_ref[...], preferred_element_type=jnp.float32).astype(o_ref.dtype)


def attention_out(queries, all_kv, bias, scale):
    rows, width = queries.shape
    keys_total = all_kv.shape[0]
    heads_here = width // HD
    return pl.pallas_call(
        functools.partial(forward_kernel, scale),
        out_shape=jax.ShapeDtypeStruct((rows, width), jnp.bfloat16),
        grid=(heads_here,),
        in_specs=[
            pl.BlockSpec((rows, HD), lambda h: (0, h)),
            pl.BlockSpec((keys_total, HD), lambda h: (0, h)),
            pl.BlockSpec((keys_total, HD), lambda h: (0, h + heads_here)),
            pl.BlockSpec((rows, keys_total), lambda h: (0, 0)),
        ],
        out_specs=pl.BlockSpec((rows, HD), lambda h: (0, h)),
        cost_estimate=pl.CostEstimate(
            flops=4 * rows * keys_total * width,
            transcendentals=2 * rows * keys_total * heads_here,
            bytes_accessed=2 * (2 * rows * width + 2 * keys_total * width) + 4 * rows * keys_total,
        ),
    )(queries, all_kv, all_kv, bias)


def local(queries, keys, values, out_grad, proj_weight, layout):
    tok_dev = queries.shape[0]
    width = queries.shape[1]
    heads_here = width // HD
    blocks_dev = tok_dev // BLK
    block_count = layout.shape[0]
    summary_count = block_count // STRIDE
    score_scale = HD ** (-0.5)
    me = lax.axis_index("seq")
    first_block = me * blocks_dev
    offset_block = layout[block_count - 1, 0] % STRIDE
    reach_back = (LOCAL - 2) // blocks_dev + 1
    span_blocks = [
        min(blocks_dev, LOCAL - 1 - hop_index * blocks_dev) for hop_index in range(reach_back)
    ]
    back_blocks = sum(span_blocks)
    pool_blocks = back_blocks + blocks_dev

    attn_grad = jnp.dot(out_grad, proj_weight, preferred_element_type=jnp.float32).astype(
        jnp.bfloat16
    )
    kv = jnp.concatenate([keys, values], axis=1)

    seq_size = lax.axis_size("seq")
    group = STRIDE // blocks_dev
    groups = seq_size // group
    assert groups == summary_count == 4 and group == 8
    assert (STRIDE - LOCAL) // blocks_dev <= group // 2 and group == 8
    far_ids = jnp.arange(summary_count, dtype=jnp.int32) * STRIDE + offset_block
    lead = offset_block // blocks_dev
    sum_local = offset_block % blocks_dev
    in_group = me % group
    my_group = me // group
    rel = (in_group - lead) % group
    win_kv, far_blocks = exchange(kv, lead, sum_local, span_blocks, seq_size, group)
    pool_kv = jnp.concatenate([win_kv, kv], axis=0)
    far_kv = far_blocks.reshape(summary_count * BLK, 2 * width)

    all_kv = jnp.concatenate([pool_kv, far_kv], axis=0)
    key_rows = all_kv[:, :width].reshape(-1, heads_here, HD)
    value_rows = all_kv[:, width:].reshape(-1, heads_here, HD)
    query_rows = queries.reshape(tok_dev, heads_here, HD)
    grad_rows = attn_grad.reshape(tok_dev, heads_here, HD)

    own_ids = first_block + jnp.arange(blocks_dev, dtype=jnp.int32)
    table_rows = lax.dynamic_slice_in_dim(layout, first_block, blocks_dev, 0)
    pool_ids = first_block - back_blocks + jnp.arange(pool_blocks, dtype=jnp.int32)
    pool_ids_b = jnp.broadcast_to(pool_ids[None, :], (blocks_dev, pool_blocks))
    plain = (pool_ids_b % STRIDE != offset_block) | (pool_ids_b == own_ids[:, None])
    pool_ok = listed(table_rows, pool_ids_b) & plain
    far_ids_b = jnp.broadcast_to(far_ids[None, :], (blocks_dev, summary_count))
    far_ok = listed(table_rows, far_ids_b) & (far_ids_b < own_ids[:, None])
    block_ok = jnp.concatenate([pool_ok, far_ok], axis=1)
    token_ok = jnp.repeat(jnp.repeat(block_ok, BLK, axis=0), BLK, axis=1)
    query_pos = jnp.arange(tok_dev, dtype=jnp.int32)
    pool_pos = jnp.arange(pool_blocks * BLK, dtype=jnp.int32) - back_blocks * BLK
    causal = jnp.concatenate(
        [
            pool_pos[None, :] <= query_pos[:, None],
            jnp.ones((tok_dev, summary_count * BLK), jnp.bool_),
        ],
        axis=1,
    )
    allowed = token_ok & causal

    scores = (
        jnp.einsum("qhd,khd->hqk", query_rows, key_rows, preferred_element_type=jnp.float32)
        * score_scale
    )
    scores = jnp.where(allowed[None], scores, -jnp.inf)
    row_top = jnp.max(scores, axis=-1, keepdims=True)
    log_total = row_top + jnp.log(jnp.sum(jnp.exp(scores - row_top), axis=-1, keepdims=True))
    probs = jnp.exp(scores - log_total)
    probs_low = probs.astype(jnp.bfloat16)
    bias = jnp.where(allowed, 0.0, -jnp.inf).astype(jnp.float32)
    attn_out = attention_out(queries, all_kv, bias, score_scale).reshape(tok_dev, heads_here, HD)
    delta = jnp.transpose(
        jnp.sum(attn_out.astype(jnp.float32) * grad_rows.astype(jnp.float32), axis=-1)
    )[..., None]
    dprobs = jnp.einsum("qhd,khd->hqk", grad_rows, value_rows, preferred_element_type=jnp.float32)
    dscores = (score_scale * probs * (dprobs - delta)).astype(jnp.bfloat16)
    query_grad = jnp.einsum(
        "hqk,khd->qhd", dscores, key_rows, preferred_element_type=jnp.float32
    ).astype(jnp.bfloat16)
    key_part = jnp.einsum("hqk,qhd->khd", dscores, query_rows, preferred_element_type=jnp.float32)
    value_part = jnp.einsum(
        "hqk,qhd->khd", probs_low, grad_rows, preferred_element_type=jnp.float32
    )
    grad_kv = jnp.concatenate(
        [key_part.reshape(-1, width), value_part.reshape(-1, width)], axis=1
    )

    part = grad_kv[pool_blocks * BLK :].reshape(summary_count, BLK, 2 * width)
    half_rows = BLK // 2
    forward_acc = part[:, :half_rows]
    backward_acc = part[:, half_rows:]
    to_next = [(d, (d + group) % seq_size) for d in range(seq_size)]
    to_prev = [(d, (d - group) % seq_size) for d in range(seq_size)]
    for step in range(groups - 1):
        out_f = lax.dynamic_index_in_dim(forward_acc, (my_group - step - 1) % groups, 0, keepdims=False)
        out_b = lax.dynamic_index_in_dim(backward_acc, (my_group + step + 1) % groups, 0, keepdims=False)
        in_f = lax.ppermute(out_f.astype(jnp.bfloat16), "seq", to_next).astype(jnp.float32)
        in_b = lax.ppermute(out_b.astype(jnp.bfloat16), "seq", to_prev).astype(jnp.float32)
        slot_f = (my_group - step - 2) % groups
        slot_b = (my_group + step + 2) % groups
        forward_acc = lax.dynamic_update_index_in_dim(
            forward_acc, lax.dynamic_index_in_dim(forward_acc, slot_f, 0, keepdims=False) + in_f, slot_f, 0
        )
        backward_acc = lax.dynamic_update_index_in_dim(
            backward_acc, lax.dynamic_index_in_dim(backward_acc, slot_b, 0, keepdims=False) + in_b, slot_b, 0
        )
    part = jnp.concatenate(
        [
            lax.dynamic_index_in_dim(forward_acc, my_group, 0, keepdims=False),
            lax.dynamic_index_in_dim(backward_acc, my_group, 0, keepdims=False),
        ],
        axis=0,
    )
    lanes = group // 2
    lane = in_group % lanes
    rel_lane = (lane - lead) % lanes
    route = [(g * group + (r ^ lanes), g * group + r) for g in range(groups) for r in range(group)]
    moved = lax.ppermute(part.astype(jnp.bfloat16), "seq", route).astype(jnp.float32)
    part = jnp.where(in_group < lanes, part + moved, part)
    def from_lane(hop):
        return [
            (g * group + r - r % lanes + (r % lanes + hop) % lanes, g * group + r)
            for g in range(groups)
            for r in range(group)
        ]

    sent = part.astype(jnp.bfloat16)
    ahead = lax.ppermute(sent, "seq", from_lane(1)).astype(jnp.float32)
    behind = lax.ppermute(sent, "seq", from_lane(-1)).astype(jnp.float32)
    part = part + jnp.where(rel_lane == 1, ahead, 0.0) + jnp.where(rel_lane == 0, behind, 0.0)
    ahead = lax.ppermute(part.astype(jnp.bfloat16), "seq", from_lane(1)).astype(jnp.float32)
    part = jnp.where(rel_lane == 0, part + ahead, part)
    own_local = jnp.arange(blocks_dev, dtype=jnp.int32)
    far_here = (rel == 0) & (own_local == sum_local)
    far_add = jnp.where(far_here[:, None, None], part[None], 0.0)

    own_grad = grad_kv[back_blocks * BLK : pool_blocks * BLK]
    pool_start = 0
    for distance in range(reach_back, 0, -1):
        rows_needed = span_blocks[distance - 1] * BLK
        back = passed_along(
            grad_kv[pool_start : pool_start + rows_needed].astype(jnp.bfloat16), "seq", -distance
        ).astype(jnp.float32)
        own_grad = own_grad.at[tok_dev - rows_needed :].add(back)
        pool_start = pool_start + rows_needed
    total = own_grad.reshape(blocks_dev, BLK, 2 * width) + far_add
    total = total.reshape(tok_dev, 2 * width).astype(jnp.bfloat16)

    proj_grad = lax.psum_scatter(
        lax.dot_general(
            out_grad,
            attn_out.reshape(tok_dev, width),
            (((0,), (0,)), ((), ())),
            preferred_element_type=jnp.float32,
        ),
        "seq",
        scatter_dimension=0,
        tiled=True,
    )
    return (
        query_grad.reshape(tok_dev, width),
        total[:, :width],
        total[:, width:],
        proj_grad,
    )


def solution(mesh):
    return jax.shard_map(
        local,
        mesh=mesh,
        in_specs=(
            P(("dp", "seq"), "head"),
            P(("dp", "seq"), "head"),
            P(("dp", "seq"), "head"),
            P(("dp", "seq"), None),
            P(None, "head"),
            P(),
        ),
        out_specs=(
            P(("dp", "seq"), "head"),
            P(("dp", "seq"), "head"),
            P(("dp", "seq"), "head"),
            P(("dp", "seq"), "head"),
        ),
        check_vma=False,
    )
```

```python
import functools

import jax
import jax.numpy as jnp
from jax import lax
from jax.experimental import pallas as pl
from jax.experimental.pallas import tpu as pltpu
from jax.sharding import PartitionSpec as P

HD = 128
BLK = 128
LOCAL = 8
STRIDE = 16


def passed_along(block, axis, distance):
    devices = range(lax.axis_size(axis))
    route = [(i - distance, i) for i in devices if i - distance in devices]
    return lax.ppermute(block, axis, route)


def listed(table_rows, block_ids):
    hit = jnp.any(table_rows[:, None, :] == block_ids[:, :, None], axis=2)
    return hit & (block_ids >= 0)


def exchange_kernel(dims, ctl_ref, kv_ref, win_out, far_out, win_buf, hop_buf, cross1, cross2, held, pair, sends, recvs):
    seq_size, group, spans = dims
    groups = seq_size // group
    me = lax.axis_index("seq")
    in_group = me % group
    base = me - in_group
    my_group = me // group
    lead = ctl_ref[0]
    sum_local = ctl_ref[1]
    lanes = group // 2
    lane = in_group % lanes
    lane_base = in_group - lane
    rel_lane = (lane - lead + lanes) % lanes
    mesh_id = pl.DeviceIdType.MESH

    def ring(step):
        return (me + step + seq_size) % seq_size

    def in_ring(step):
        return base + lane_base + (lane + step + lanes) % lanes

    def flip():
        return me + lanes - 2 * lanes * (in_group // lanes)

    def across(span):
        upper = (my_group // span) % 2
        return me + span * group - 2 * span * group * upper

    barrier = pltpu.get_barrier_semaphore()
    partners = []
    for distance in range(1, len(spans) + 1):
        partners += [ring(distance), ring(-distance)]
    for hop in (1, 2):
        partners += [in_ring(hop), in_ring(-hop)]
    partners += [flip(), flip()]
    span = 1
    while span < groups:
        partners += [across(span), across(span)]
        span *= 2
    for partner in partners:
        pl.semaphore_signal(barrier, 1, device_id={"seq": partner}, device_id_type=mesh_id)
    pl.semaphore_wait(barrier, len(partners))

    tok_dev = kv_ref.shape[0]
    window = []
    starts = {}
    start = 0
    for distance in range(len(spans), 0, -1):
        starts[distance] = start
        start += spans[distance - 1] * BLK

    def send_window(distance):
        rows = spans[distance - 1] * BLK
        copy = pltpu.make_async_remote_copy(
            src_ref=kv_ref.at[pl.ds(tok_dev - rows, rows)],
            dst_ref=win_buf.at[pl.ds(starts[distance], rows)],
            send_sem=sends.at[distance - 1],
            recv_sem=recvs.at[distance - 1],
            device_id={"seq": ring(distance)},
            device_id_type=mesh_id,
        )
        copy.start()
        window.append(copy)

    mine = kv_ref[0:BLK, :]
    for block in range(1, tok_dev // BLK):
        mine = jnp.where(sum_local == block, kv_ref[block * BLK : (block + 1) * BLK, :], mine)
    held[...] = mine
    slot = len(spans)
    stages = [
        [(in_ring(1), rel_lane == 1), (in_ring(-1), rel_lane == lanes - 1)],
        [(in_ring(1), rel_lane == 2)],
        [(flip(), in_group >= lanes)],
    ]
    stage = 0
    for moves in stages:
        copies = []
        for target, take in moves:
            copy = pltpu.make_async_remote_copy(
                src_ref=held,
                dst_ref=hop_buf.at[stage],
                send_sem=sends.at[slot],
                recv_sem=recvs.at[slot],
                device_id={"seq": target},
                device_id_type=mesh_id,
            )
            copy.start()
            copies.append((copy, stage, take))
            slot += 1
            stage += 1
        for copy, _, _ in copies:
            copy.wait()
        for _, index, take in copies:
            held[...] = jnp.where(take, hop_buf[index], held[...])

    copy = pltpu.make_async_remote_copy(
        src_ref=held,
        dst_ref=cross1,
        send_sem=sends.at[slot],
        recv_sem=recvs.at[slot],
        device_id={"seq": across(1)},
        device_id_type=mesh_id,
    )
    copy.start()
    copy.wait()
    upper = (my_group % 2) == 1
    pair[0] = jnp.where(upper, cross1[...], held[...])
    pair[1] = jnp.where(upper, held[...], cross1[...])
    slot += 1
    copy = pltpu.make_async_remote_copy(
        src_ref=pair,
        dst_ref=cross2,
        send_sem=sends.at[slot],
        recv_sem=recvs.at[slot],
        device_id={"seq": across(2)},
        device_id_type=mesh_id,
    )
    copy.start()
    copy.wait()
    for distance in range(len(spans), 0, -1):
        send_window(distance)
    upper = ((my_group // 2) % 2) == 1
    for index in range(2):
        far_out[index] = jnp.where(upper, cross2[index], pair[index])
        far_out[2 + index] = jnp.where(upper, pair[index], cross2[index])
    for copy in window:
        copy.wait()
    win_out[...] = win_buf[...]


def exchange(kv, lead, sum_local, spans, seq_size, group):
    tok_dev, cols = kv.shape
    back_rows = sum(spans) * BLK
    groups = seq_size // group
    copies = len(spans) + 6
    ctl = jnp.stack([lead, sum_local]).astype(jnp.int32)
    return pl.pallas_call(
        functools.partial(exchange_kernel, (seq_size, group, spans)),
        out_shape=(
            jax.ShapeDtypeStruct((back_rows, cols), kv.dtype),
            jax.ShapeDtypeStruct((groups, BLK, cols), kv.dtype),
        ),
        in_specs=[
            pl.BlockSpec(memory_space=pltpu.SMEM),
            pl.BlockSpec(memory_space=pltpu.VMEM),
        ],
        out_specs=(
            pl.BlockSpec(memory_space=pltpu.VMEM),
            pl.BlockSpec(memory_space=pltpu.VMEM),
        ),
        scratch_shapes=[
            pltpu.VMEM((back_rows, cols), kv.dtype),
            pltpu.VMEM((4, BLK, cols), kv.dtype),
            pltpu.VMEM((BLK, cols), kv.dtype),
            pltpu.VMEM((2, BLK, cols), kv.dtype),
            pltpu.VMEM((BLK, cols), kv.dtype),
            pltpu.VMEM((2, BLK, cols), kv.dtype),
            pltpu.SemaphoreType.DMA((copies,)),
            pltpu.SemaphoreType.DMA((copies,)),
        ],
        compiler_params=pltpu.CompilerParams(
            collective_id=0, has_side_effects=True, vmem_limit_bytes=48 * 1024 * 1024
        ),
    )(ctl, kv)


def forward_kernel(scale, q_ref, k_ref, v_ref, bias_ref, o_ref):
    scores = lax.dot_general(
        q_ref[...], k_ref[...], (((1,), (1,)), ((), ())), preferred_element_type=jnp.float32
    )
    scores = scores * scale + bias_ref[...]
    row_top = jnp.max(scores, axis=1, keepdims=True)
    log_total = row_top + jnp.log(jnp.sum(jnp.exp(scores - row_top), axis=1, keepdims=True))
    probs_low = jnp.exp(scores - log_total).astype(jnp.bfloat16)
    o_ref[...] = jnp.dot(probs_low, v_ref[...], preferred_element_type=jnp.float32).astype(o_ref.dtype)


def attention_out(queries, all_kv, bias, scale):
    rows, width = queries.shape
    keys_total = all_kv.shape[0]
    heads_here = width // HD
    return pl.pallas_call(
        functools.partial(forward_kernel, scale),
        out_shape=jax.ShapeDtypeStruct((rows, width), jnp.bfloat16),
        grid=(heads_here,),
        in_specs=[
            pl.BlockSpec((rows, HD), lambda h: (0, h)),
            pl.BlockSpec((keys_total, HD), lambda h: (0, h)),
            pl.BlockSpec((keys_total, HD), lambda h: (0, h + heads_here)),
            pl.BlockSpec((rows, keys_total), lambda h: (0, 0)),
        ],
        out_specs=pl.BlockSpec((rows, HD), lambda h: (0, h)),
        cost_estimate=pl.CostEstimate(
            flops=4 * rows * keys_total * width,
            transcendentals=2 * rows * keys_total * heads_here,
            bytes_accessed=2 * (2 * rows * width + 2 * keys_total * width) + 4 * rows * keys_total,
        ),
    )(queries, all_kv, all_kv, bias)


def local(queries, keys, values, out_grad, proj_weight, layout):
    tok_dev = queries.shape[0]
    width = queries.shape[1]
    heads_here = width // HD
    blocks_dev = tok_dev // BLK
    block_count = layout.shape[0]
    summary_count = block_count // STRIDE
    score_scale = HD ** (-0.5)
    me = lax.axis_index("seq")
    first_block = me * blocks_dev
    offset_block = layout[block_count - 1, 0] % STRIDE
    reach_back = (LOCAL - 2) // blocks_dev + 1
    span_blocks = [
        min(blocks_dev, LOCAL - 1 - hop_index * blocks_dev) for hop_index in range(reach_back)
    ]
    back_blocks = sum(span_blocks)
    pool_blocks = back_blocks + blocks_dev

    attn_grad = jnp.dot(out_grad, proj_weight, preferred_element_type=jnp.float32).astype(
        jnp.bfloat16
    )
    kv = jnp.concatenate([keys, values], axis=1)

    seq_size = lax.axis_size("seq")
    group = STRIDE // blocks_dev
    groups = seq_size // group
    assert groups == summary_count == 4 and group == 8
    assert (STRIDE - LOCAL) // blocks_dev <= group // 2 and group == 8
    far_ids = jnp.arange(summary_count, dtype=jnp.int32) * STRIDE + offset_block
    lead = offset_block // blocks_dev
    sum_local = offset_block % blocks_dev
    in_group = me % group
    my_group = me // group
    rel = (in_group - lead) % group
    win_kv, far_blocks = exchange(kv, lead, sum_local, span_blocks, seq_size, group)
    pool_kv = jnp.concatenate([win_kv, kv], axis=0)
    far_kv = far_blocks.reshape(summary_count * BLK, 2 * width)

    all_kv = jnp.concatenate([pool_kv, far_kv], axis=0)
    key_rows = all_kv[:, :width].reshape(-1, heads_here, HD)
    value_rows = all_kv[:, width:].reshape(-1, heads_here, HD)
    query_rows = queries.reshape(tok_dev, heads_here, HD)
    grad_rows = attn_grad.reshape(tok_dev, heads_here, HD)

    own_ids = first_block + jnp.arange(blocks_dev, dtype=jnp.int32)
    table_rows = lax.dynamic_slice_in_dim(layout, first_block, blocks_dev, 0)
    pool_ids = first_block - back_blocks + jnp.arange(pool_blocks, dtype=jnp.int32)
    pool_ids_b = jnp.broadcast_to(pool_ids[None, :], (blocks_dev, pool_blocks))
    plain = (pool_ids_b % STRIDE != offset_block) | (pool_ids_b == own_ids[:, None])
    pool_ok = listed(table_rows, pool_ids_b) & plain
    far_ids_b = jnp.broadcast_to(far_ids[None, :], (blocks_dev, summary_count))
    far_ok = listed(table_rows, far_ids_b) & (far_ids_b < own_ids[:, None])
    block_ok = jnp.concatenate([pool_ok, far_ok], axis=1)
    token_ok = jnp.repeat(jnp.repeat(block_ok, BLK, axis=0), BLK, axis=1)
    query_pos = jnp.arange(tok_dev, dtype=jnp.int32)
    pool_pos = jnp.arange(pool_blocks * BLK, dtype=jnp.int32) - back_blocks * BLK
    causal = jnp.concatenate(
        [
            pool_pos[None, :] <= query_pos[:, None],
            jnp.ones((tok_dev, summary_count * BLK), jnp.bool_),
        ],
        axis=1,
    )
    allowed = token_ok & causal

    scores = (
        jnp.einsum("qhd,khd->hqk", query_rows, key_rows, preferred_element_type=jnp.float32)
        * score_scale
    )
    scores = jnp.where(allowed[None], scores, -jnp.inf)
    row_top = jnp.max(scores, axis=-1, keepdims=True)
    log_total = row_top + jnp.log(jnp.sum(jnp.exp(scores - row_top), axis=-1, keepdims=True))
    probs = jnp.exp(scores - log_total)
    probs_low = probs.astype(jnp.bfloat16)
    bias = jnp.where(allowed, 0.0, -jnp.inf).astype(jnp.float32)
    attn_out = attention_out(queries, all_kv, bias, score_scale).reshape(tok_dev, heads_here, HD)
    delta = jnp.transpose(
        jnp.sum(attn_out.astype(jnp.float32) * grad_rows.astype(jnp.float32), axis=-1)
    )[..., None]
    dprobs = jnp.einsum("qhd,khd->hqk", grad_rows, value_rows, preferred_element_type=jnp.float32)
    dscores = (score_scale * probs * (dprobs - delta)).astype(jnp.bfloat16)
    query_grad = jnp.einsum(
        "hqk,khd->qhd", dscores, key_rows, preferred_element_type=jnp.float32
    ).astype(jnp.bfloat16)
    key_part = jnp.einsum("hqk,qhd->khd", dscores, query_rows, preferred_element_type=jnp.float32)
    value_part = jnp.einsum(
        "hqk,qhd->khd", probs_low, grad_rows, preferred_element_type=jnp.float32
    )
    grad_kv = jnp.concatenate(
        [key_part.reshape(-1, width), value_part.reshape(-1, width)], axis=1
    )

    part = grad_kv[pool_blocks * BLK :].reshape(summary_count, BLK, 2 * width)
    half_rows = BLK // 2
    forward_acc = part[:, :half_rows]
    backward_acc = part[:, half_rows:]
    to_next = [(d, (d + group) % seq_size) for d in range(seq_size)]
    to_prev = [(d, (d - group) % seq_size) for d in range(seq_size)]
    for step in range(groups - 1):
        out_f = lax.dynamic_index_in_dim(forward_acc, (my_group - step - 1) % groups, 0, keepdims=False)
        out_b = lax.dynamic_index_in_dim(backward_acc, (my_group + step + 1) % groups, 0, keepdims=False)
        in_f = lax.ppermute(out_f.astype(jnp.bfloat16), "seq", to_next).astype(jnp.float32)
        in_b = lax.ppermute(out_b.astype(jnp.bfloat16), "seq", to_prev).astype(jnp.float32)
        slot_f = (my_group - step - 2) % groups
        slot_b = (my_group + step + 2) % groups
        forward_acc = lax.dynamic_update_index_in_dim(
            forward_acc, lax.dynamic_index_in_dim(forward_acc, slot_f, 0, keepdims=False) + in_f, slot_f, 0
        )
        backward_acc = lax.dynamic_update_index_in_dim(
            backward_acc, lax.dynamic_index_in_dim(backward_acc, slot_b, 0, keepdims=False) + in_b, slot_b, 0
        )
    part = jnp.concatenate(
        [
            lax.dynamic_index_in_dim(forward_acc, my_group, 0, keepdims=False),
            lax.dynamic_index_in_dim(backward_acc, my_group, 0, keepdims=False),
        ],
        axis=0,
    )
    lanes = group // 2
    lane = in_group % lanes
    rel_lane = (lane - lead) % lanes
    route = [(g * group + (r ^ lanes), g * group + r) for g in range(groups) for r in range(group)]
    moved = lax.ppermute(part.astype(jnp.bfloat16), "seq", route).astype(jnp.float32)
    part = jnp.where(in_group < lanes, part + moved, part)
    def from_lane(hop):
        return [
            (g * group + r - r % lanes + (r % lanes + hop) % lanes, g * group + r)
            for g in range(groups)
            for r in range(group)
        ]

    sent = part.astype(jnp.bfloat16)
    ahead = lax.ppermute(sent, "seq", from_lane(1)).astype(jnp.float32)
    behind = lax.ppermute(sent, "seq", from_lane(-1)).astype(jnp.float32)
    part = part + jnp.where(rel_lane == 1, ahead, 0.0) + jnp.where(rel_lane == 0, behind, 0.0)
    ahead = lax.ppermute(part.astype(jnp.bfloat16), "seq", from_lane(1)).astype(jnp.float32)
    part = jnp.where(rel_lane == 0, part + ahead, part)
    own_local = jnp.arange(blocks_dev, dtype=jnp.int32)
    far_here = (rel == 0) & (own_local == sum_local)
    far_add = jnp.where(far_here[:, None, None], part[None], 0.0)

    own_grad = grad_kv[back_blocks * BLK : pool_blocks * BLK]
    pool_start = 0
    for distance in range(reach_back, 0, -1):
        rows_needed = span_blocks[distance - 1] * BLK
        back = passed_along(
            grad_kv[pool_start : pool_start + rows_needed].astype(jnp.bfloat16), "seq", -distance
        ).astype(jnp.float32)
        own_grad = own_grad.at[tok_dev - rows_needed :].add(back)
        pool_start = pool_start + rows_needed
    total = own_grad.reshape(blocks_dev, BLK, 2 * width) + far_add
    total = total.reshape(tok_dev, 2 * width).astype(jnp.bfloat16)

    proj_grad = lax.psum_scatter(
        lax.dot_general(
            out_grad,
            attn_out.reshape(tok_dev, width),
            (((0,), (0,)), ((), ())),
            preferred_element_type=jnp.float32,
        ),
        "seq",
        scatter_dimension=0,
        tiled=True,
    )
    return (
        query_grad.reshape(tok_dev, width),
        total[:, :width],
        total[:, width:],
        proj_grad,
    )


def solution(mesh):
    return jax.shard_map(
        local,
        mesh=mesh,
        in_specs=(
            P(("dp", "seq"), "head"),
            P(("dp", "seq"), "head"),
            P(("dp", "seq"), "head"),
            P(("dp", "seq"), None),
            P(None, "head"),
            P(),
        ),
        out_specs=(
            P(("dp", "seq"), "head"),
            P(("dp", "seq"), "head"),
            P(("dp", "seq"), "head"),
            P(("dp", "seq"), "head"),
        ),
        check_vma=False,
    )
```

```python
import functools

import jax
import jax.numpy as jnp
from jax import lax
from jax.experimental import pallas as pl
from jax.experimental.pallas import tpu as pltpu
from jax.sharding import PartitionSpec as P

HD = 128
BLK = 128
LOCAL = 8
STRIDE = 16


def passed_along(block, axis, distance):
    devices = range(lax.axis_size(axis))
    route = [(i - distance, i) for i in devices if i - distance in devices]
    return lax.ppermute(block, axis, route)


def listed(table_rows, block_ids):
    hit = jnp.any(table_rows[:, None, :] == block_ids[:, :, None], axis=2)
    return hit & (block_ids >= 0)


def exchange_kernel(dims, ctl_ref, kv_ref, win_out, far_out, win_buf, hop_buf, cross1, cross2, held, pair, sends, recvs):
    seq_size, group, spans = dims
    groups = seq_size // group
    me = lax.axis_index("seq")
    in_group = me % group
    base = me - in_group
    my_group = me // group
    lead = ctl_ref[0]
    sum_local = ctl_ref[1]
    lanes = group // 2
    lane = in_group % lanes
    lane_base = in_group - lane
    rel_lane = (lane - lead + lanes) % lanes
    mesh_id = pl.DeviceIdType.MESH

    def ring(step):
        return (me + step + seq_size) % seq_size

    def in_ring(step):
        return base + lane_base + (lane + step + lanes) % lanes

    def flip():
        return me + lanes - 2 * lanes * (in_group // lanes)

    def across(span):
        upper = (my_group // span) % 2
        return me + span * group - 2 * span * group * upper

    barrier = pltpu.get_barrier_semaphore()
    partners = []
    for distance in range(1, len(spans) + 1):
        partners += [ring(distance), ring(-distance)]
    for hop in (1, 2):
        partners += [in_ring(hop), in_ring(-hop)]
    partners += [flip(), flip()]
    span = 1
    while span < groups:
        partners += [across(span), across(span)]
        span *= 2
    for partner in partners:
        pl.semaphore_signal(barrier, 1, device_id={"seq": partner}, device_id_type=mesh_id)
    pl.semaphore_wait(barrier, len(partners))

    tok_dev = kv_ref.shape[0]
    window = []
    starts = {}
    start = 0
    for distance in range(len(spans), 0, -1):
        starts[distance] = start
        start += spans[distance - 1] * BLK

    def send_window(distance):
        rows = spans[distance - 1] * BLK
        copy = pltpu.make_async_remote_copy(
            src_ref=kv_ref.at[pl.ds(tok_dev - rows, rows)],
            dst_ref=win_buf.at[pl.ds(starts[distance], rows)],
            send_sem=sends.at[distance - 1],
            recv_sem=recvs.at[distance - 1],
            device_id={"seq": ring(distance)},
            device_id_type=mesh_id,
        )
        copy.start()
        window.append(copy)

    mine = kv_ref[0:BLK, :]
    for block in range(1, tok_dev // BLK):
        mine = jnp.where(sum_local == block, kv_ref[block * BLK : (block + 1) * BLK, :], mine)
    held[...] = mine
    slot = len(spans)
    stages = [
        [(in_ring(1), rel_lane == 1), (in_ring(-1), rel_lane == lanes - 1)],
        [(in_ring(1), rel_lane == 2)],
        [(flip(), in_group >= lanes)],
    ]
    stage = 0
    for moves in stages:
        copies = []
        for target, take in moves:
            copy = pltpu.make_async_remote_copy(
                src_ref=held,
                dst_ref=hop_buf.at[stage],
                send_sem=sends.at[slot],
                recv_sem=recvs.at[slot],
                device_id={"seq": target},
                device_id_type=mesh_id,
            )
            copy.start()
            copies.append((copy, stage, take))
            slot += 1
            stage += 1
        for copy, _, _ in copies:
            copy.wait()
        for _, index, take in copies:
            held[...] = jnp.where(take, hop_buf[index], held[...])

    copy = pltpu.make_async_remote_copy(
        src_ref=held,
        dst_ref=cross1,
        send_sem=sends.at[slot],
        recv_sem=recvs.at[slot],
        device_id={"seq": across(1)},
        device_id_type=mesh_id,
    )
    copy.start()
    copy.wait()
    upper = (my_group % 2) == 1
    pair[0] = jnp.where(upper, cross1[...], held[...])
    pair[1] = jnp.where(upper, held[...], cross1[...])
    slot += 1
    copy = pltpu.make_async_remote_copy(
        src_ref=pair,
        dst_ref=cross2,
        send_sem=sends.at[slot],
        recv_sem=recvs.at[slot],
        device_id={"seq": across(2)},
        device_id_type=mesh_id,
    )
    copy.start()
    copy.wait()
    for distance in range(len(spans), 0, -1):
        send_window(distance)
    upper = ((my_group // 2) % 2) == 1
    for index in range(2):
        far_out[index] = jnp.where(upper, cross2[index], pair[index])
        far_out[2 + index] = jnp.where(upper, pair[index], cross2[index])
    for copy in window:
        copy.wait()
    win_out[...] = win_buf[...]


def exchange(kv, lead, sum_local, spans, seq_size, group):
    tok_dev, cols = kv.shape
    back_rows = sum(spans) * BLK
    groups = seq_size // group
    copies = len(spans) + 6
    ctl = jnp.stack([lead, sum_local]).astype(jnp.int32)
    return pl.pallas_call(
        functools.partial(exchange_kernel, (seq_size, group, spans)),
        out_shape=(
            jax.ShapeDtypeStruct((back_rows, cols), kv.dtype),
            jax.ShapeDtypeStruct((groups, BLK, cols), kv.dtype),
        ),
        in_specs=[
            pl.BlockSpec(memory_space=pltpu.SMEM),
            pl.BlockSpec(memory_space=pltpu.VMEM),
        ],
        out_specs=(
            pl.BlockSpec(memory_space=pltpu.VMEM),
            pl.BlockSpec(memory_space=pltpu.VMEM),
        ),
        scratch_shapes=[
            pltpu.VMEM((back_rows, cols), kv.dtype),
            pltpu.VMEM((4, BLK, cols), kv.dtype),
            pltpu.VMEM((BLK, cols), kv.dtype),
            pltpu.VMEM((2, BLK, cols), kv.dtype),
            pltpu.VMEM((BLK, cols), kv.dtype),
            pltpu.VMEM((2, BLK, cols), kv.dtype),
            pltpu.SemaphoreType.DMA((copies,)),
            pltpu.SemaphoreType.DMA((copies,)),
        ],
        compiler_params=pltpu.CompilerParams(
            collective_id=0, has_side_effects=True, vmem_limit_bytes=48 * 1024 * 1024
        ),
    )(ctl, kv)


def forward_kernel(scale, q_ref, k_ref, v_ref, bias_ref, o_ref):
    scores = lax.dot_general(
        q_ref[...], k_ref[...], (((1,), (1,)), ((), ())), preferred_element_type=jnp.float32
    )
    scores = scores * scale + bias_ref[...]
    row_top = jnp.max(scores, axis=1, keepdims=True)
    log_total = row_top + jnp.log(jnp.sum(jnp.exp(scores - row_top), axis=1, keepdims=True))
    probs_low = jnp.exp(scores - log_total).astype(jnp.bfloat16)
    o_ref[...] = jnp.dot(probs_low, v_ref[...], preferred_element_type=jnp.float32).astype(o_ref.dtype)


def attention_out(queries, all_kv, bias, scale):
    rows, width = queries.shape
    keys_total = all_kv.shape[0]
    heads_here = width // HD
    return pl.pallas_call(
        functools.partial(forward_kernel, scale),
        out_shape=jax.ShapeDtypeStruct((rows, width), jnp.bfloat16),
        grid=(heads_here,),
        in_specs=[
            pl.BlockSpec((rows, HD), lambda h: (0, h)),
            pl.BlockSpec((keys_total, HD), lambda h: (0, h)),
            pl.BlockSpec((keys_total, HD), lambda h: (0, h + heads_here)),
            pl.BlockSpec((rows, keys_total), lambda h: (0, 0)),
        ],
        out_specs=pl.BlockSpec((rows, HD), lambda h: (0, h)),
        cost_estimate=pl.CostEstimate(
            flops=4 * rows * keys_total * width,
            transcendentals=2 * rows * keys_total * heads_here,
            bytes_accessed=2 * (2 * rows * width + 2 * keys_total * width) + 4 * rows * keys_total,
        ),
    )(queries, all_kv, all_kv, bias)


def local(queries, keys, values, out_grad, proj_weight, layout):
    tok_dev = queries.shape[0]
    width = queries.shape[1]
    heads_here = width // HD
    blocks_dev = tok_dev // BLK
    block_count = layout.shape[0]
    summary_count = block_count // STRIDE
    score_scale = HD ** (-0.5)
    me = lax.axis_index("seq")
    first_block = me * blocks_dev
    offset_block = layout[block_count - 1, 0] % STRIDE
    reach_back = (LOCAL - 2) // blocks_dev + 1
    span_blocks = [
        min(blocks_dev, LOCAL - 1 - hop_index * blocks_dev) for hop_index in range(reach_back)
    ]
    back_blocks = sum(span_blocks)
    pool_blocks = back_blocks + blocks_dev

    attn_grad = jnp.dot(out_grad, proj_weight, preferred_element_type=jnp.float32).astype(
        jnp.bfloat16
    )
    kv = jnp.concatenate([keys, values], axis=1)

    seq_size = lax.axis_size("seq")
    group = STRIDE // blocks_dev
    groups = seq_size // group
    assert groups == summary_count == 4 and group == 8
    assert (STRIDE - LOCAL) // blocks_dev <= group // 2 and group == 8
    far_ids = jnp.arange(summary_count, dtype=jnp.int32) * STRIDE + offset_block
    lead = offset_block // blocks_dev
    sum_local = offset_block % blocks_dev
    in_group = me % group
    my_group = me // group
    rel = (in_group - lead) % group
    win_kv, far_blocks = exchange(kv, lead, sum_local, span_blocks, seq_size, group)
    pool_kv = jnp.concatenate([win_kv, kv], axis=0)
    far_kv = far_blocks.reshape(summary_count * BLK, 2 * width)

    all_kv = jnp.concatenate([pool_kv, far_kv], axis=0)
    key_rows = all_kv[:, :width].reshape(-1, heads_here, HD)
    value_rows = all_kv[:, width:].reshape(-1, heads_here, HD)
    query_rows = queries.reshape(tok_dev, heads_here, HD)
    grad_rows = attn_grad.reshape(tok_dev, heads_here, HD)

    own_ids = first_block + jnp.arange(blocks_dev, dtype=jnp.int32)
    table_rows = lax.dynamic_slice_in_dim(layout, first_block, blocks_dev, 0)
    pool_ids = first_block - back_blocks + jnp.arange(pool_blocks, dtype=jnp.int32)
    pool_ids_b = jnp.broadcast_to(pool_ids[None, :], (blocks_dev, pool_blocks))
    plain = (pool_ids_b % STRIDE != offset_block) | (pool_ids_b == own_ids[:, None])
    pool_ok = listed(table_rows, pool_ids_b) & plain
    far_ids_b = jnp.broadcast_to(far_ids[None, :], (blocks_dev, summary_count))
    far_ok = listed(table_rows, far_ids_b) & (far_ids_b < own_ids[:, None])
    block_ok = jnp.concatenate([pool_ok, far_ok], axis=1)
    token_ok = jnp.repeat(jnp.repeat(block_ok, BLK, axis=0), BLK, axis=1)
    query_pos = jnp.arange(tok_dev, dtype=jnp.int32)
    pool_pos = jnp.arange(pool_blocks * BLK, dtype=jnp.int32) - back_blocks * BLK
    causal = jnp.concatenate(
        [
            pool_pos[None, :] <= query_pos[:, None],
            jnp.ones((tok_dev, summary_count * BLK), jnp.bool_),
        ],
        axis=1,
    )
    allowed = token_ok & causal

    scores = (
        jnp.einsum("qhd,khd->hqk", query_rows, key_rows, preferred_element_type=jnp.float32)
        * score_scale
    )
    scores = jnp.where(allowed[None], scores, -jnp.inf)
    row_top = jnp.max(scores, axis=-1, keepdims=True)
    log_total = row_top + jnp.log(jnp.sum(jnp.exp(scores - row_top), axis=-1, keepdims=True))
    probs = jnp.exp(scores - log_total)
    probs_low = probs.astype(jnp.bfloat16)
    bias = jnp.where(allowed, 0.0, -jnp.inf).astype(jnp.float32)
    attn_out = attention_out(queries, all_kv, bias, score_scale).reshape(tok_dev, heads_here, HD)
    delta = jnp.transpose(
        jnp.sum(attn_out.astype(jnp.float32) * grad_rows.astype(jnp.float32), axis=-1)
    )[..., None]
    dprobs = jnp.einsum("qhd,khd->hqk", grad_rows, value_rows, preferred_element_type=jnp.float32)
    dscores = (score_scale * probs * (dprobs - delta)).astype(jnp.bfloat16)
    query_grad = jnp.einsum(
        "hqk,khd->qhd", dscores, key_rows, preferred_element_type=jnp.float32
    ).astype(jnp.bfloat16)
    key_part = jnp.einsum("hqk,qhd->khd", dscores, query_rows, preferred_element_type=jnp.float32)
    value_part = jnp.einsum(
        "hqk,qhd->khd", probs_low, grad_rows, preferred_element_type=jnp.float32
    )
    grad_kv = jnp.concatenate(
        [key_part.reshape(-1, width), value_part.reshape(-1, width)], axis=1
    )

    own_grad = grad_kv[back_blocks * BLK : pool_blocks * BLK]
    pool_start = 0
    for distance in range(reach_back, 0, -1):
        rows_needed = span_blocks[distance - 1] * BLK
        back = passed_along(
            grad_kv[pool_start : pool_start + rows_needed].astype(jnp.bfloat16), "seq", -distance
        ).astype(jnp.float32)
        own_grad = own_grad.at[tok_dev - rows_needed :].add(back)
        pool_start = pool_start + rows_needed
    part = grad_kv[pool_blocks * BLK :].reshape(summary_count, BLK, 2 * width)
    own_grad, part = lax.optimization_barrier((own_grad, part))
    half_rows = BLK // 2
    forward_acc = part[:, :half_rows]
    backward_acc = part[:, half_rows:]
    to_next = [(d, (d + group) % seq_size) for d in range(seq_size)]
    to_prev = [(d, (d - group) % seq_size) for d in range(seq_size)]
    for step in range(groups - 1):
        out_f = lax.dynamic_index_in_dim(forward_acc, (my_group - step - 1) % groups, 0, keepdims=False)
        out_b = lax.dynamic_index_in_dim(backward_acc, (my_group + step + 1) % groups, 0, keepdims=False)
        in_f = lax.ppermute(out_f.astype(jnp.bfloat16), "seq", to_next).astype(jnp.float32)
        in_b = lax.ppermute(out_b.astype(jnp.bfloat16), "seq", to_prev).astype(jnp.float32)
        slot_f = (my_group - step - 2) % groups
        slot_b = (my_group + step + 2) % groups
        forward_acc = lax.dynamic_update_index_in_dim(
            forward_acc, lax.dynamic_index_in_dim(forward_acc, slot_f, 0, keepdims=False) + in_f, slot_f, 0
        )
        backward_acc = lax.dynamic_update_index_in_dim(
            backward_acc, lax.dynamic_index_in_dim(backward_acc, slot_b, 0, keepdims=False) + in_b, slot_b, 0
        )
    part = jnp.concatenate(
        [
            lax.dynamic_index_in_dim(forward_acc, my_group, 0, keepdims=False),
            lax.dynamic_index_in_dim(backward_acc, my_group, 0, keepdims=False),
        ],
        axis=0,
    )
    lanes = group // 2
    lane = in_group % lanes
    rel_lane = (lane - lead) % lanes
    route = [(g * group + (r ^ lanes), g * group + r) for g in range(groups) for r in range(group)]
    moved = lax.ppermute(part.astype(jnp.bfloat16), "seq", route).astype(jnp.float32)
    part = jnp.where(in_group < lanes, part + moved, part)
    def from_lane(hop):
        return [
            (g * group + r - r % lanes + (r % lanes + hop) % lanes, g * group + r)
            for g in range(groups)
            for r in range(group)
        ]

    sent = part.astype(jnp.bfloat16)
    ahead = lax.ppermute(sent, "seq", from_lane(1)).astype(jnp.float32)
    behind = lax.ppermute(sent, "seq", from_lane(-1)).astype(jnp.float32)
    part = part + jnp.where(rel_lane == 1, ahead, 0.0) + jnp.where(rel_lane == 0, behind, 0.0)
    ahead = lax.ppermute(part.astype(jnp.bfloat16), "seq", from_lane(1)).astype(jnp.float32)
    part = jnp.where(rel_lane == 0, part + ahead, part)
    own_local = jnp.arange(blocks_dev, dtype=jnp.int32)
    far_here = (rel == 0) & (own_local == sum_local)
    far_add = jnp.where(far_here[:, None, None], part[None], 0.0)

    total = own_grad.reshape(blocks_dev, BLK, 2 * width) + far_add
    total = total.reshape(tok_dev, 2 * width).astype(jnp.bfloat16)

    proj_grad = lax.psum_scatter(
        lax.dot_general(
            out_grad,
            attn_out.reshape(tok_dev, width),
            (((0,), (0,)), ((), ())),
            preferred_element_type=jnp.float32,
        ),
        "seq",
        scatter_dimension=0,
        tiled=True,
    )
    return (
        query_grad.reshape(tok_dev, width),
        total[:, :width],
        total[:, width:],
        proj_grad,
    )


def solution(mesh):
    return jax.shard_map(
        local,
        mesh=mesh,
        in_specs=(
            P(("dp", "seq"), "head"),
            P(("dp", "seq"), "head"),
            P(("dp", "seq"), "head"),
            P(("dp", "seq"), None),
            P(None, "head"),
            P(),
        ),
        out_specs=(
            P(("dp", "seq"), "head"),
            P(("dp", "seq"), "head"),
            P(("dp", "seq"), "head"),
            P(("dp", "seq"), "head"),
        ),
        check_vma=False,
    )
```

```python
import functools

import jax
import jax.numpy as jnp
from jax import lax
from jax.experimental import pallas as pl
from jax.experimental.pallas import tpu as pltpu
from jax.sharding import PartitionSpec as P

HD = 128
BLK = 128
LOCAL = 8
STRIDE = 16


def passed_along(block, axis, distance):
    devices = range(lax.axis_size(axis))
    route = [(i - distance, i) for i in devices if i - distance in devices]
    return lax.ppermute(block, axis, route)


def listed(table_rows, block_ids):
    hit = jnp.any(table_rows[:, None, :] == block_ids[:, :, None], axis=2)
    return hit & (block_ids >= 0)


def exchange_kernel(dims, ctl_ref, kv_ref, win_out, far_out, win_buf, hop_buf, cross1, cross2, held, pair, sends, recvs):
    seq_size, group, spans = dims
    groups = seq_size // group
    me = lax.axis_index("seq")
    in_group = me % group
    base = me - in_group
    my_group = me // group
    lead = ctl_ref[0]
    sum_local = ctl_ref[1]
    lanes = group // 2
    lane = in_group % lanes
    lane_base = in_group - lane
    rel_lane = (lane - lead + lanes) % lanes
    mesh_id = pl.DeviceIdType.MESH

    def ring(step):
        return (me + step + seq_size) % seq_size

    def in_ring(step):
        return base + lane_base + (lane + step + lanes) % lanes

    def flip():
        return me + lanes - 2 * lanes * (in_group // lanes)

    def across(span):
        upper = (my_group // span) % 2
        return me + span * group - 2 * span * group * upper

    barrier = pltpu.get_barrier_semaphore()
    partners = []
    for distance in range(1, len(spans) + 1):
        partners += [ring(distance), ring(-distance)]
    for hop in (1, 2):
        partners += [in_ring(hop), in_ring(-hop)]
    partners += [flip(), flip()]
    span = 1
    while span < groups:
        partners += [across(span), across(span)]
        span *= 2
    for partner in partners:
        pl.semaphore_signal(barrier, 1, device_id={"seq": partner}, device_id_type=mesh_id)
    pl.semaphore_wait(barrier, len(partners))

    tok_dev = kv_ref.shape[0]
    window = []
    starts = {}
    start = 0
    for distance in range(len(spans), 0, -1):
        starts[distance] = start
        start += spans[distance - 1] * BLK

    def send_window(distance):
        rows = spans[distance - 1] * BLK
        copy = pltpu.make_async_remote_copy(
            src_ref=kv_ref.at[pl.ds(tok_dev - rows, rows)],
            dst_ref=win_buf.at[pl.ds(starts[distance], rows)],
            send_sem=sends.at[distance - 1],
            recv_sem=recvs.at[distance - 1],
            device_id={"seq": ring(distance)},
            device_id_type=mesh_id,
        )
        copy.start()
        window.append(copy)

    mine = kv_ref[0:BLK, :]
    for block in range(1, tok_dev // BLK):
        mine = jnp.where(sum_local == block, kv_ref[block * BLK : (block + 1) * BLK, :], mine)
    held[...] = mine
    slot = len(spans)
    stages = [
        [(in_ring(1), rel_lane == 1), (in_ring(-1), rel_lane == lanes - 1)],
        [(in_ring(1), rel_lane == 2)],
        [(flip(), in_group >= lanes)],
    ]
    stage = 0
    for moves in stages:
        copies = []
        for target, take in moves:
            copy = pltpu.make_async_remote_copy(
                src_ref=held,
                dst_ref=hop_buf.at[stage],
                send_sem=sends.at[slot],
                recv_sem=recvs.at[slot],
                device_id={"seq": target},
                device_id_type=mesh_id,
            )
            copy.start()
            copies.append((copy, stage, take))
            slot += 1
            stage += 1
        for copy, _, _ in copies:
            copy.wait()
        for _, index, take in copies:
            held[...] = jnp.where(take, hop_buf[index], held[...])

    copy = pltpu.make_async_remote_copy(
        src_ref=held,
        dst_ref=cross1,
        send_sem=sends.at[slot],
        recv_sem=recvs.at[slot],
        device_id={"seq": across(1)},
        device_id_type=mesh_id,
    )
    copy.start()
    copy.wait()
    upper = (my_group % 2) == 1
    pair[0] = jnp.where(upper, cross1[...], held[...])
    pair[1] = jnp.where(upper, held[...], cross1[...])
    slot += 1
    copy = pltpu.make_async_remote_copy(
        src_ref=pair,
        dst_ref=cross2,
        send_sem=sends.at[slot],
        recv_sem=recvs.at[slot],
        device_id={"seq": across(2)},
        device_id_type=mesh_id,
    )
    copy.start()
    copy.wait()
    for distance in range(len(spans), 0, -1):
        send_window(distance)
    upper = ((my_group // 2) % 2) == 1
    for index in range(2):
        far_out[index] = jnp.where(upper, cross2[index], pair[index])
        far_out[2 + index] = jnp.where(upper, pair[index], cross2[index])
    for copy in window:
        copy.wait()
    win_out[...] = win_buf[...]


def exchange(kv, lead, sum_local, spans, seq_size, group):
    tok_dev, cols = kv.shape
    back_rows = sum(spans) * BLK
    groups = seq_size // group
    copies = len(spans) + 6
    ctl = jnp.stack([lead, sum_local]).astype(jnp.int32)
    return pl.pallas_call(
        functools.partial(exchange_kernel, (seq_size, group, spans)),
        out_shape=(
            jax.ShapeDtypeStruct((back_rows, cols), kv.dtype),
            jax.ShapeDtypeStruct((groups, BLK, cols), kv.dtype),
        ),
        in_specs=[
            pl.BlockSpec(memory_space=pltpu.SMEM),
            pl.BlockSpec(memory_space=pltpu.VMEM),
        ],
        out_specs=(
            pl.BlockSpec(memory_space=pltpu.VMEM),
            pl.BlockSpec(memory_space=pltpu.VMEM),
        ),
        scratch_shapes=[
            pltpu.VMEM((back_rows, cols), kv.dtype),
            pltpu.VMEM((4, BLK, cols), kv.dtype),
            pltpu.VMEM((BLK, cols), kv.dtype),
            pltpu.VMEM((2, BLK, cols), kv.dtype),
            pltpu.VMEM((BLK, cols), kv.dtype),
            pltpu.VMEM((2, BLK, cols), kv.dtype),
            pltpu.SemaphoreType.DMA((copies,)),
            pltpu.SemaphoreType.DMA((copies,)),
        ],
        compiler_params=pltpu.CompilerParams(
            collective_id=0, has_side_effects=True, vmem_limit_bytes=48 * 1024 * 1024
        ),
    )(ctl, kv)


def forward_kernel(scale, q_ref, k_ref, v_ref, bias_ref, o_ref):
    scores = lax.dot_general(
        q_ref[...], k_ref[...], (((1,), (1,)), ((), ())), preferred_element_type=jnp.float32
    )
    scores = scores * scale + bias_ref[...]
    row_top = jnp.max(scores, axis=1, keepdims=True)
    log_total = row_top + jnp.log(jnp.sum(jnp.exp(scores - row_top), axis=1, keepdims=True))
    probs_low = jnp.exp(scores - log_total).astype(jnp.bfloat16)
    o_ref[...] = jnp.dot(probs_low, v_ref[...], preferred_element_type=jnp.float32).astype(o_ref.dtype)


def attention_out(queries, all_kv, bias, scale):
    rows, width = queries.shape
    keys_total = all_kv.shape[0]
    heads_here = width // HD
    return pl.pallas_call(
        functools.partial(forward_kernel, scale),
        out_shape=jax.ShapeDtypeStruct((rows, width), jnp.bfloat16),
        grid=(heads_here,),
        in_specs=[
            pl.BlockSpec((rows, HD), lambda h: (0, h)),
            pl.BlockSpec((keys_total, HD), lambda h: (0, h)),
            pl.BlockSpec((keys_total, HD), lambda h: (0, h + heads_here)),
            pl.BlockSpec((rows, keys_total), lambda h: (0, 0)),
        ],
        out_specs=pl.BlockSpec((rows, HD), lambda h: (0, h)),
        cost_estimate=pl.CostEstimate(
            flops=4 * rows * keys_total * width,
            transcendentals=2 * rows * keys_total * heads_here,
            bytes_accessed=2 * (2 * rows * width + 2 * keys_total * width) + 4 * rows * keys_total,
        ),
    )(queries, all_kv, all_kv, bias)


def local(queries, keys, values, out_grad, proj_weight, layout):
    tok_dev = queries.shape[0]
    width = queries.shape[1]
    heads_here = width // HD
    blocks_dev = tok_dev // BLK
    block_count = layout.shape[0]
    summary_count = block_count // STRIDE
    score_scale = HD ** (-0.5)
    me = lax.axis_index("seq")
    first_block = me * blocks_dev
    offset_block = layout[block_count - 1, 0] % STRIDE
    reach_back = (LOCAL - 2) // blocks_dev + 1
    span_blocks = [
        min(blocks_dev, LOCAL - 1 - hop_index * blocks_dev) for hop_index in range(reach_back)
    ]
    back_blocks = sum(span_blocks)
    pool_blocks = back_blocks + blocks_dev

    attn_grad = jnp.dot(out_grad, proj_weight, preferred_element_type=jnp.float32).astype(
        jnp.bfloat16
    )
    kv = jnp.concatenate([keys, values], axis=1)

    seq_size = lax.axis_size("seq")
    group = STRIDE // blocks_dev
    groups = seq_size // group
    assert groups == summary_count == 4 and group == 8
    assert (STRIDE - LOCAL) // blocks_dev <= group // 2 and group == 8
    far_ids = jnp.arange(summary_count, dtype=jnp.int32) * STRIDE + offset_block
    lead = offset_block // blocks_dev
    sum_local = offset_block % blocks_dev
    in_group = me % group
    my_group = me // group
    rel = (in_group - lead) % group
    win_kv, far_blocks = exchange(kv, lead, sum_local, span_blocks, seq_size, group)
    pool_kv = jnp.concatenate([win_kv, kv], axis=0)
    far_kv = far_blocks.reshape(summary_count * BLK, 2 * width)

    all_kv = jnp.concatenate([pool_kv, far_kv], axis=0)
    key_rows = all_kv[:, :width].reshape(-1, heads_here, HD)
    value_rows = all_kv[:, width:].reshape(-1, heads_here, HD)
    query_rows = queries.reshape(tok_dev, heads_here, HD)
    grad_rows = attn_grad.reshape(tok_dev, heads_here, HD)

    own_ids = first_block + jnp.arange(blocks_dev, dtype=jnp.int32)
    table_rows = lax.dynamic_slice_in_dim(layout, first_block, blocks_dev, 0)
    pool_ids = first_block - back_blocks + jnp.arange(pool_blocks, dtype=jnp.int32)
    pool_ids_b = jnp.broadcast_to(pool_ids[None, :], (blocks_dev, pool_blocks))
    plain = (pool_ids_b % STRIDE != offset_block) | (pool_ids_b == own_ids[:, None])
    pool_ok = listed(table_rows, pool_ids_b) & plain
    far_ids_b = jnp.broadcast_to(far_ids[None, :], (blocks_dev, summary_count))
    far_ok = listed(table_rows, far_ids_b) & (far_ids_b < own_ids[:, None])
    block_ok = jnp.concatenate([pool_ok, far_ok], axis=1)
    token_ok = jnp.repeat(jnp.repeat(block_ok, BLK, axis=0), BLK, axis=1)
    query_pos = jnp.arange(tok_dev, dtype=jnp.int32)
    pool_pos = jnp.arange(pool_blocks * BLK, dtype=jnp.int32) - back_blocks * BLK
    causal = jnp.concatenate(
        [
            pool_pos[None, :] <= query_pos[:, None],
            jnp.ones((tok_dev, summary_count * BLK), jnp.bool_),
        ],
        axis=1,
    )
    allowed = token_ok & causal

    scores = (
        jnp.einsum("qhd,khd->hqk", query_rows, key_rows, preferred_element_type=jnp.float32)
        * score_scale
    )
    scores = jnp.where(allowed[None], scores, -jnp.inf)
    row_top = jnp.max(scores, axis=-1, keepdims=True)
    log_total = row_top + jnp.log(jnp.sum(jnp.exp(scores - row_top), axis=-1, keepdims=True))
    probs = jnp.exp(scores - log_total)
    probs_low = probs.astype(jnp.bfloat16)
    bias = jnp.where(allowed, 0.0, -jnp.inf).astype(jnp.float32)
    attn_out = attention_out(queries, all_kv, bias, score_scale).reshape(tok_dev, heads_here, HD)
    delta = jnp.transpose(
        jnp.sum(attn_out.astype(jnp.float32) * grad_rows.astype(jnp.float32), axis=-1)
    )[..., None]
    dprobs = jnp.einsum("qhd,khd->hqk", grad_rows, value_rows, preferred_element_type=jnp.float32)
    dscores = (score_scale * probs * (dprobs - delta)).astype(jnp.bfloat16)
    query_grad = jnp.einsum(
        "hqk,khd->qhd", dscores, key_rows, preferred_element_type=jnp.float32
    ).astype(jnp.bfloat16)
    key_part = jnp.einsum("hqk,qhd->khd", dscores, query_rows, preferred_element_type=jnp.float32)
    value_part = jnp.einsum(
        "hqk,qhd->khd", probs_low, grad_rows, preferred_element_type=jnp.float32
    )
    grad_kv = jnp.concatenate(
        [key_part.reshape(-1, width), value_part.reshape(-1, width)], axis=1
    )

    part = grad_kv[pool_blocks * BLK :].reshape(summary_count, BLK, 2 * width)
    half_rows = BLK // 2
    forward_acc = part[:, :half_rows]
    backward_acc = part[:, half_rows:]
    to_next = [(d, (d + group) % seq_size) for d in range(seq_size)]
    to_prev = [(d, (d - group) % seq_size) for d in range(seq_size)]
    for step in range(groups - 1):
        out_f = lax.dynamic_index_in_dim(forward_acc, (my_group - step - 1) % groups, 0, keepdims=False)
        out_b = lax.dynamic_index_in_dim(backward_acc, (my_group + step + 1) % groups, 0, keepdims=False)
        in_f = lax.ppermute(out_f.astype(jnp.bfloat16), "seq", to_next).astype(jnp.float32)
        in_b = lax.ppermute(out_b.astype(jnp.bfloat16), "seq", to_prev).astype(jnp.float32)
        slot_f = (my_group - step - 2) % groups
        slot_b = (my_group + step + 2) % groups
        forward_acc = lax.dynamic_update_index_in_dim(
            forward_acc, lax.dynamic_index_in_dim(forward_acc, slot_f, 0, keepdims=False) + in_f, slot_f, 0
        )
        backward_acc = lax.dynamic_update_index_in_dim(
            backward_acc, lax.dynamic_index_in_dim(backward_acc, slot_b, 0, keepdims=False) + in_b, slot_b, 0
        )
    part = jnp.concatenate(
        [
            lax.dynamic_index_in_dim(forward_acc, my_group, 0, keepdims=False),
            lax.dynamic_index_in_dim(backward_acc, my_group, 0, keepdims=False),
        ],
        axis=0,
    )
    lanes = group // 2
    lane = in_group % lanes
    rel_lane = (lane - lead) % lanes
    route = [(g * group + (r ^ lanes), g * group + r) for g in range(groups) for r in range(group)]
    moved = lax.ppermute(part.astype(jnp.bfloat16), "seq", route).astype(jnp.float32)
    part = jnp.where(in_group < lanes, part + moved, part)
    def from_lane(hop):
        return [
            (g * group + r - r % lanes + (r % lanes + hop) % lanes, g * group + r)
            for g in range(groups)
            for r in range(group)
        ]

    sent = part.astype(jnp.bfloat16)
    ahead = lax.ppermute(sent, "seq", from_lane(1)).astype(jnp.float32)
    behind = lax.ppermute(sent, "seq", from_lane(-1)).astype(jnp.float32)
    opposite = lax.ppermute(sent, "seq", from_lane(2)).astype(jnp.float32)
    part = jnp.where(rel_lane == 0, part + ahead + behind + opposite, part)
    own_local = jnp.arange(blocks_dev, dtype=jnp.int32)
    far_here = (rel == 0) & (own_local == sum_local)
    far_add = jnp.where(far_here[:, None, None], part[None], 0.0)

    own_grad = grad_kv[back_blocks * BLK : pool_blocks * BLK]
    pool_start = 0
    for distance in range(reach_back, 0, -1):
        rows_needed = span_blocks[distance - 1] * BLK
        back = passed_along(
            grad_kv[pool_start : pool_start + rows_needed].astype(jnp.bfloat16), "seq", -distance
        ).astype(jnp.float32)
        own_grad = own_grad.at[tok_dev - rows_needed :].add(back)
        pool_start = pool_start + rows_needed
    total = own_grad.reshape(blocks_dev, BLK, 2 * width) + far_add
    total = total.reshape(tok_dev, 2 * width).astype(jnp.bfloat16)

    proj_grad = lax.psum_scatter(
        lax.dot_general(
            out_grad,
            attn_out.reshape(tok_dev, width),
            (((0,), (0,)), ((), ())),
            preferred_element_type=jnp.float32,
        ),
        "seq",
        scatter_dimension=0,
        tiled=True,
    )
    return (
        query_grad.reshape(tok_dev, width),
        total[:, :width],
        total[:, width:],
        proj_grad,
    )


def solution(mesh):
    return jax.shard_map(
        local,
        mesh=mesh,
        in_specs=(
            P(("dp", "seq"), "head"),
            P(("dp", "seq"), "head"),
            P(("dp", "seq"), "head"),
            P(("dp", "seq"), None),
            P(None, "head"),
            P(),
        ),
        out_specs=(
            P(("dp", "seq"), "head"),
            P(("dp", "seq"), "head"),
            P(("dp", "seq"), "head"),
            P(("dp", "seq"), "head"),
        ),
        check_vma=False,
    )
```

```python
import functools

import jax
import jax.numpy as jnp
from jax import lax
from jax.experimental import pallas as pl
from jax.experimental.pallas import tpu as pltpu
from jax.sharding import PartitionSpec as P

HD = 128
BLK = 128
LOCAL = 8
STRIDE = 16


def passed_along(block, axis, distance):
    devices = range(lax.axis_size(axis))
    route = [(i - distance, i) for i in devices if i - distance in devices]
    return lax.ppermute(block, axis, route)


def listed(table_rows, block_ids):
    hit = jnp.any(table_rows[:, None, :] == block_ids[:, :, None], axis=2)
    return hit & (block_ids >= 0)


def exchange_kernel(dims, ctl_ref, kv_ref, win_out, far_out, win_buf, hop_buf, cross1, cross2, held, pair, sends, recvs):
    seq_size, group, spans = dims
    groups = seq_size // group
    me = lax.axis_index("seq")
    in_group = me % group
    base = me - in_group
    my_group = me // group
    lead = ctl_ref[0]
    sum_local = ctl_ref[1]
    lanes = group // 2
    lane = in_group % lanes
    lane_base = in_group - lane
    rel_lane = (lane - lead + lanes) % lanes
    mesh_id = pl.DeviceIdType.MESH

    def ring(step):
        return (me + step + seq_size) % seq_size

    def in_ring(step):
        return base + lane_base + (lane + step + lanes) % lanes

    def flip():
        return me + lanes - 2 * lanes * (in_group // lanes)

    def across(span):
        upper = (my_group // span) % 2
        return me + span * group - 2 * span * group * upper

    barrier = pltpu.get_barrier_semaphore()
    partners = []
    for distance in range(1, len(spans) + 1):
        partners += [ring(distance), ring(-distance)]
    for hop in (1, 2):
        partners += [in_ring(hop), in_ring(-hop)]
    partners += [flip(), flip()]
    span = 1
    while span < groups:
        partners += [across(span), across(span)]
        span *= 2
    for partner in partners:
        pl.semaphore_signal(barrier, 1, device_id={"seq": partner}, device_id_type=mesh_id)
    pl.semaphore_wait(barrier, len(partners))

    tok_dev = kv_ref.shape[0]
    window = []
    starts = {}
    start = 0
    for distance in range(len(spans), 0, -1):
        starts[distance] = start
        start += spans[distance - 1] * BLK

    def send_window(distance):
        rows = spans[distance - 1] * BLK
        copy = pltpu.make_async_remote_copy(
            src_ref=kv_ref.at[pl.ds(tok_dev - rows, rows)],
            dst_ref=win_buf.at[pl.ds(starts[distance], rows)],
            send_sem=sends.at[distance - 1],
            recv_sem=recvs.at[distance - 1],
            device_id={"seq": ring(distance)},
            device_id_type=mesh_id,
        )
        copy.start()
        window.append(copy)

    mine = kv_ref[0:BLK, :]
    for block in range(1, tok_dev // BLK):
        mine = jnp.where(sum_local == block, kv_ref[block * BLK : (block + 1) * BLK, :], mine)
    held[...] = mine
    slot = len(spans)
    stages = [
        [(in_ring(1), rel_lane == 1), (in_ring(-1), rel_lane == lanes - 1)],
        [(in_ring(1), rel_lane == 2)],
        [(flip(), in_group >= lanes)],
    ]
    stage = 0
    for moves in stages:
        copies = []
        for target, take in moves:
            copy = pltpu.make_async_remote_copy(
                src_ref=held,
                dst_ref=hop_buf.at[stage],
                send_sem=sends.at[slot],
                recv_sem=recvs.at[slot],
                device_id={"seq": target},
                device_id_type=mesh_id,
            )
            copy.start()
            copies.append((copy, stage, take))
            slot += 1
            stage += 1
        for copy, _, _ in copies:
            copy.wait()
        for _, index, take in copies:
            held[...] = jnp.where(take, hop_buf[index], held[...])

    copy = pltpu.make_async_remote_copy(
        src_ref=held,
        dst_ref=cross1,
        send_sem=sends.at[slot],
        recv_sem=recvs.at[slot],
        device_id={"seq": across(1)},
        device_id_type=mesh_id,
    )
    copy.start()
    copy.wait()
    upper = (my_group % 2) == 1
    pair[0] = jnp.where(upper, cross1[...], held[...])
    pair[1] = jnp.where(upper, held[...], cross1[...])
    slot += 1
    for distance in range(len(spans), 0, -1):
        send_window(distance)
    copy = pltpu.make_async_remote_copy(
        src_ref=pair,
        dst_ref=cross2,
        send_sem=sends.at[slot],
        recv_sem=recvs.at[slot],
        device_id={"seq": across(2)},
        device_id_type=mesh_id,
    )
    copy.start()
    copy.wait()
    upper = ((my_group // 2) % 2) == 1
    for index in range(2):
        far_out[index] = jnp.where(upper, cross2[index], pair[index])
        far_out[2 + index] = jnp.where(upper, pair[index], cross2[index])
    for copy in window:
        copy.wait()
    win_out[...] = win_buf[...]


def exchange(kv, lead, sum_local, spans, seq_size, group):
    tok_dev, cols = kv.shape
    back_rows = sum(spans) * BLK
    groups = seq_size // group
    copies = len(spans) + 6
    ctl = jnp.stack([lead, sum_local]).astype(jnp.int32)
    return pl.pallas_call(
        functools.partial(exchange_kernel, (seq_size, group, spans)),
        out_shape=(
            jax.ShapeDtypeStruct((back_rows, cols), kv.dtype),
            jax.ShapeDtypeStruct((groups, BLK, cols), kv.dtype),
        ),
        in_specs=[
            pl.BlockSpec(memory_space=pltpu.SMEM),
            pl.BlockSpec(memory_space=pltpu.VMEM),
        ],
        out_specs=(
            pl.BlockSpec(memory_space=pltpu.VMEM),
            pl.BlockSpec(memory_space=pltpu.VMEM),
        ),
        scratch_shapes=[
            pltpu.VMEM((back_rows, cols), kv.dtype),
            pltpu.VMEM((4, BLK, cols), kv.dtype),
            pltpu.VMEM((BLK, cols), kv.dtype),
            pltpu.VMEM((2, BLK, cols), kv.dtype),
            pltpu.VMEM((BLK, cols), kv.dtype),
            pltpu.VMEM((2, BLK, cols), kv.dtype),
            pltpu.SemaphoreType.DMA((copies,)),
            pltpu.SemaphoreType.DMA((copies,)),
        ],
        compiler_params=pltpu.CompilerParams(
            collective_id=0, has_side_effects=True, vmem_limit_bytes=48 * 1024 * 1024
        ),
    )(ctl, kv)


def forward_kernel(scale, q_ref, k_ref, v_ref, bias_ref, o_ref):
    scores = lax.dot_general(
        q_ref[...], k_ref[...], (((1,), (1,)), ((), ())), preferred_element_type=jnp.float32
    )
    scores = scores * scale + bias_ref[...]
    row_top = jnp.max(scores, axis=1, keepdims=True)
    log_total = row_top + jnp.log(jnp.sum(jnp.exp(scores - row_top), axis=1, keepdims=True))
    probs_low = jnp.exp(scores - log_total).astype(jnp.bfloat16)
    o_ref[...] = jnp.dot(probs_low, v_ref[...], preferred_element_type=jnp.float32).astype(o_ref.dtype)


def attention_out(queries, all_kv, bias, scale):
    rows, width = queries.shape
    keys_total = all_kv.shape[0]
    heads_here = width // HD
    return pl.pallas_call(
        functools.partial(forward_kernel, scale),
        out_shape=jax.ShapeDtypeStruct((rows, width), jnp.bfloat16),
        grid=(heads_here,),
        in_specs=[
            pl.BlockSpec((rows, HD), lambda h: (0, h)),
            pl.BlockSpec((keys_total, HD), lambda h: (0, h)),
            pl.BlockSpec((keys_total, HD), lambda h: (0, h + heads_here)),
            pl.BlockSpec((rows, keys_total), lambda h: (0, 0)),
        ],
        out_specs=pl.BlockSpec((rows, HD), lambda h: (0, h)),
        cost_estimate=pl.CostEstimate(
            flops=4 * rows * keys_total * width,
            transcendentals=2 * rows * keys_total * heads_here,
            bytes_accessed=2 * (2 * rows * width + 2 * keys_total * width) + 4 * rows * keys_total,
        ),
    )(queries, all_kv, all_kv, bias)


def local(queries, keys, values, out_grad, proj_weight, layout):
    tok_dev = queries.shape[0]
    width = queries.shape[1]
    heads_here = width // HD
    blocks_dev = tok_dev // BLK
    block_count = layout.shape[0]
    summary_count = block_count // STRIDE
    score_scale = HD ** (-0.5)
    me = lax.axis_index("seq")
    first_block = me * blocks_dev
    offset_block = layout[block_count - 1, 0] % STRIDE
    reach_back = (LOCAL - 2) // blocks_dev + 1
    span_blocks = [
        min(blocks_dev, LOCAL - 1 - hop_index * blocks_dev) for hop_index in range(reach_back)
    ]
    back_blocks = sum(span_blocks)
    pool_blocks = back_blocks + blocks_dev

    attn_grad = jnp.dot(out_grad, proj_weight, preferred_element_type=jnp.float32).astype(
        jnp.bfloat16
    )
    kv = jnp.concatenate([keys, values], axis=1)

    seq_size = lax.axis_size("seq")
    group = STRIDE // blocks_dev
    groups = seq_size // group
    assert groups == summary_count == 4 and group == 8
    assert (STRIDE - LOCAL) // blocks_dev <= group // 2 and group == 8
    far_ids = jnp.arange(summary_count, dtype=jnp.int32) * STRIDE + offset_block
    lead = offset_block // blocks_dev
    sum_local = offset_block % blocks_dev
    in_group = me % group
    my_group = me // group
    rel = (in_group - lead) % group
    win_kv, far_blocks = exchange(kv, lead, sum_local, span_blocks, seq_size, group)
    pool_kv = jnp.concatenate([win_kv, kv], axis=0)
    far_kv = far_blocks.reshape(summary_count * BLK, 2 * width)

    all_kv = jnp.concatenate([pool_kv, far_kv], axis=0)
    key_rows = all_kv[:, :width].reshape(-1, heads_here, HD)
    value_rows = all_kv[:, width:].reshape(-1, heads_here, HD)
    query_rows = queries.reshape(tok_dev, heads_here, HD)
    grad_rows = attn_grad.reshape(tok_dev, heads_here, HD)

    own_ids = first_block + jnp.arange(blocks_dev, dtype=jnp.int32)
    table_rows = lax.dynamic_slice_in_dim(layout, first_block, blocks_dev, 0)
    pool_ids = first_block - back_blocks + jnp.arange(pool_blocks, dtype=jnp.int32)
    pool_ids_b = jnp.broadcast_to(pool_ids[None, :], (blocks_dev, pool_blocks))
    plain = (pool_ids_b % STRIDE != offset_block) | (pool_ids_b == own_ids[:, None])
    pool_ok = listed(table_rows, pool_ids_b) & plain
    far_ids_b = jnp.broadcast_to(far_ids[None, :], (blocks_dev, summary_count))
    far_ok = listed(table_rows, far_ids_b) & (far_ids_b < own_ids[:, None])
    block_ok = jnp.concatenate([pool_ok, far_ok], axis=1)
    token_ok = jnp.repeat(jnp.repeat(block_ok, BLK, axis=0), BLK, axis=1)
    query_pos = jnp.arange(tok_dev, dtype=jnp.int32)
    pool_pos = jnp.arange(pool_blocks * BLK, dtype=jnp.int32) - back_blocks * BLK
    causal = jnp.concatenate(
        [
            pool_pos[None, :] <= query_pos[:, None],
            jnp.ones((tok_dev, summary_count * BLK), jnp.bool_),
        ],
        axis=1,
    )
    allowed = token_ok & causal

    scores = (
        jnp.einsum("qhd,khd->hqk", query_rows, key_rows, preferred_element_type=jnp.float32)
        * score_scale
    )
    scores = jnp.where(allowed[None], scores, -jnp.inf)
    row_top = jnp.max(scores, axis=-1, keepdims=True)
    log_total = row_top + jnp.log(jnp.sum(jnp.exp(scores - row_top), axis=-1, keepdims=True))
    probs = jnp.exp(scores - log_total)
    probs_low = probs.astype(jnp.bfloat16)
    bias = jnp.where(allowed, 0.0, -jnp.inf).astype(jnp.float32)
    attn_out = attention_out(queries, all_kv, bias, score_scale).reshape(tok_dev, heads_here, HD)
    delta = jnp.transpose(
        jnp.sum(attn_out.astype(jnp.float32) * grad_rows.astype(jnp.float32), axis=-1)
    )[..., None]
    dprobs = jnp.einsum("qhd,khd->hqk", grad_rows, value_rows, preferred_element_type=jnp.float32)
    dscores = (score_scale * probs * (dprobs - delta)).astype(jnp.bfloat16)
    query_grad = jnp.einsum(
        "hqk,khd->qhd", dscores, key_rows, preferred_element_type=jnp.float32
    ).astype(jnp.bfloat16)
    key_part = jnp.einsum("hqk,qhd->khd", dscores, query_rows, preferred_element_type=jnp.float32)
    value_part = jnp.einsum(
        "hqk,qhd->khd", probs_low, grad_rows, preferred_element_type=jnp.float32
    )
    grad_kv = jnp.concatenate(
        [key_part.reshape(-1, width), value_part.reshape(-1, width)], axis=1
    )

    part = grad_kv[pool_blocks * BLK :].reshape(summary_count, BLK, 2 * width)
    half_rows = BLK // 2
    forward_acc = part[:, :half_rows]
    backward_acc = part[:, half_rows:]
    to_next = [(d, (d + group) % seq_size) for d in range(seq_size)]
    to_prev = [(d, (d - group) % seq_size) for d in range(seq_size)]
    for step in range(groups - 1):
        out_f = lax.dynamic_index_in_dim(forward_acc, (my_group - step - 1) % groups, 0, keepdims=False)
        out_b = lax.dynamic_index_in_dim(backward_acc, (my_group + step + 1) % groups, 0, keepdims=False)
        in_f = lax.ppermute(out_f.astype(jnp.bfloat16), "seq", to_next).astype(jnp.float32)
        in_b = lax.ppermute(out_b.astype(jnp.bfloat16), "seq", to_prev).astype(jnp.float32)
        slot_f = (my_group - step - 2) % groups
        slot_b = (my_group + step + 2) % groups
        forward_acc = lax.dynamic_update_index_in_dim(
            forward_acc, lax.dynamic_index_in_dim(forward_acc, slot_f, 0, keepdims=False) + in_f, slot_f, 0
        )
        backward_acc = lax.dynamic_update_index_in_dim(
            backward_acc, lax.dynamic_index_in_dim(backward_acc, slot_b, 0, keepdims=False) + in_b, slot_b, 0
        )
    part = jnp.concatenate(
        [
            lax.dynamic_index_in_dim(forward_acc, my_group, 0, keepdims=False),
            lax.dynamic_index_in_dim(backward_acc, my_group, 0, keepdims=False),
        ],
        axis=0,
    )
    lanes = group // 2
    lane = in_group % lanes
    rel_lane = (lane - lead) % lanes
    route = [(g * group + (r ^ lanes), g * group + r) for g in range(groups) for r in range(group)]
    moved = lax.ppermute(part.astype(jnp.bfloat16), "seq", route).astype(jnp.float32)
    part = jnp.where(in_group < lanes, part + moved, part)
    def from_lane(hop):
        return [
            (g * group + r - r % lanes + (r % lanes + hop) % lanes, g * group + r)
            for g in range(groups)
            for r in range(group)
        ]

    sent = part.astype(jnp.bfloat16)
    ahead = lax.ppermute(sent, "seq", from_lane(1)).astype(jnp.float32)
    behind = lax.ppermute(sent, "seq", from_lane(-1)).astype(jnp.float32)
    part = part + jnp.where(rel_lane == 1, ahead, 0.0) + jnp.where(rel_lane == 0, behind, 0.0)
    ahead = lax.ppermute(part.astype(jnp.bfloat16), "seq", from_lane(1)).astype(jnp.float32)
    part = jnp.where(rel_lane == 0, part + ahead, part)
    own_local = jnp.arange(blocks_dev, dtype=jnp.int32)
    far_here = (rel == 0) & (own_local == sum_local)
    far_add = jnp.where(far_here[:, None, None], part[None], 0.0)

    own_grad = grad_kv[back_blocks * BLK : pool_blocks * BLK]
    pool_start = 0
    for distance in range(reach_back, 0, -1):
        rows_needed = span_blocks[distance - 1] * BLK
        back = passed_along(
            grad_kv[pool_start : pool_start + rows_needed].astype(jnp.bfloat16), "seq", -distance
        ).astype(jnp.float32)
        own_grad = own_grad.at[tok_dev - rows_needed :].add(back)
        pool_start = pool_start + rows_needed
    total = own_grad.reshape(blocks_dev, BLK, 2 * width) + far_add
    total = total.reshape(tok_dev, 2 * width).astype(jnp.bfloat16)

    proj_grad = lax.psum_scatter(
        lax.dot_general(
            out_grad,
            attn_out.reshape(tok_dev, width),
            (((0,), (0,)), ((), ())),
            preferred_element_type=jnp.float32,
        ),
        "seq",
        scatter_dimension=0,
        tiled=True,
    )
    return (
        query_grad.reshape(tok_dev, width),
        total[:, :width],
        total[:, width:],
        proj_grad,
    )


def solution(mesh):
    return jax.shard_map(
        local,
        mesh=mesh,
        in_specs=(
            P(("dp", "seq"), "head"),
            P(("dp", "seq"), "head"),
            P(("dp", "seq"), "head"),
            P(("dp", "seq"), None),
            P(None, "head"),
            P(),
        ),
        out_specs=(
            P(("dp", "seq"), "head"),
            P(("dp", "seq"), "head"),
            P(("dp", "seq"), "head"),
            P(("dp", "seq"), "head"),
        ),
        check_vma=False,
    )
```

```python
import functools

import jax
import jax.numpy as jnp
from jax import lax
from jax.experimental import pallas as pl
from jax.experimental.pallas import tpu as pltpu
from jax.sharding import PartitionSpec as P

HD = 128
BLK = 128
LOCAL = 8
STRIDE = 16


def passed_along(block, axis, distance):
    devices = range(lax.axis_size(axis))
    route = [(i - distance, i) for i in devices if i - distance in devices]
    return lax.ppermute(block, axis, route)


def listed(table_rows, block_ids):
    hit = jnp.any(table_rows[:, None, :] == block_ids[:, :, None], axis=2)
    return hit & (block_ids >= 0)


def exchange_kernel(dims, ctl_ref, kv_ref, win_out, far_out, win_buf, hop_buf, cross1, cross2, held, pair, sends, recvs):
    seq_size, group, spans = dims
    groups = seq_size // group
    me = lax.axis_index("seq")
    in_group = me % group
    base = me - in_group
    my_group = me // group
    lead = ctl_ref[0]
    sum_local = ctl_ref[1]
    lanes = group // 2
    lane = in_group % lanes
    lane_base = in_group - lane
    rel_lane = (lane - lead + lanes) % lanes
    mesh_id = pl.DeviceIdType.MESH

    def ring(step):
        return (me + step + seq_size) % seq_size

    def in_ring(step):
        return base + lane_base + (lane + step + lanes) % lanes

    def flip():
        return me + lanes - 2 * lanes * (in_group // lanes)

    def across(span):
        upper = (my_group // span) % 2
        return me + span * group - 2 * span * group * upper

    barrier = pltpu.get_barrier_semaphore()
    partners = []
    for distance in range(1, len(spans) + 1):
        partners += [ring(distance), ring(-distance)]
    for hop in (1, 2):
        partners += [in_ring(hop), in_ring(-hop)]
    partners += [flip(), flip()]
    span = 1
    while span < groups:
        partners += [across(span), across(span)]
        span *= 2
    for partner in partners:
        pl.semaphore_signal(barrier, 1, device_id={"seq": partner}, device_id_type=mesh_id)
    pl.semaphore_wait(barrier, len(partners))

    tok_dev = kv_ref.shape[0]
    window = []
    starts = {}
    start = 0
    for distance in range(len(spans), 0, -1):
        starts[distance] = start
        start += spans[distance - 1] * BLK

    def send_window(distance):
        rows = spans[distance - 1] * BLK
        copy = pltpu.make_async_remote_copy(
            src_ref=kv_ref.at[pl.ds(tok_dev - rows, rows)],
            dst_ref=win_buf.at[pl.ds(starts[distance], rows)],
            send_sem=sends.at[distance - 1],
            recv_sem=recvs.at[distance - 1],
            device_id={"seq": ring(distance)},
            device_id_type=mesh_id,
        )
        copy.start()
        window.append(copy)

    mine = kv_ref[0:BLK, :]
    for block in range(1, tok_dev // BLK):
        mine = jnp.where(sum_local == block, kv_ref[block * BLK : (block + 1) * BLK, :], mine)
    held[...] = mine
    slot = len(spans)
    stages = [
        [(in_ring(1), rel_lane == 1), (in_ring(-1), rel_lane == lanes - 1)],
        [(in_ring(1), rel_lane == 2)],
        [(flip(), in_group >= lanes)],
    ]
    stage = 0
    for moves in stages:
        copies = []
        for target, take in moves:
            copy = pltpu.make_async_remote_copy(
                src_ref=held,
                dst_ref=hop_buf.at[stage],
                send_sem=sends.at[slot],
                recv_sem=recvs.at[slot],
                device_id={"seq": target},
                device_id_type=mesh_id,
            )
            copy.start()
            copies.append((copy, stage, take))
            slot += 1
            stage += 1
        for copy, _, _ in copies:
            copy.wait()
        for _, index, take in copies:
            held[...] = jnp.where(take, hop_buf[index], held[...])

    copy = pltpu.make_async_remote_copy(
        src_ref=held,
        dst_ref=cross1,
        send_sem=sends.at[slot],
        recv_sem=recvs.at[slot],
        device_id={"seq": across(1)},
        device_id_type=mesh_id,
    )
    copy.start()
    copy.wait()
    upper = (my_group % 2) == 1
    pair[0] = jnp.where(upper, cross1[...], held[...])
    pair[1] = jnp.where(upper, held[...], cross1[...])
    slot += 1
    copy = pltpu.make_async_remote_copy(
        src_ref=pair,
        dst_ref=cross2,
        send_sem=sends.at[slot],
        recv_sem=recvs.at[slot],
        device_id={"seq": across(2)},
        device_id_type=mesh_id,
    )
    copy.start()
    copy.wait()
    for distance in range(len(spans), 0, -1):
        send_window(distance)
    upper = ((my_group // 2) % 2) == 1
    for index in range(2):
        far_out[index] = jnp.where(upper, cross2[index], pair[index])
        far_out[2 + index] = jnp.where(upper, pair[index], cross2[index])
    for copy in window:
        copy.wait()
    win_out[...] = win_buf[...]


def exchange(kv, lead, sum_local, spans, seq_size, group):
    tok_dev, cols = kv.shape
    back_rows = sum(spans) * BLK
    groups = seq_size // group
    copies = len(spans) + 6
    ctl = jnp.stack([lead, sum_local]).astype(jnp.int32)
    return pl.pallas_call(
        functools.partial(exchange_kernel, (seq_size, group, spans)),
        out_shape=(
            jax.ShapeDtypeStruct((back_rows, cols), kv.dtype),
            jax.ShapeDtypeStruct((groups, BLK, cols), kv.dtype),
        ),
        in_specs=[
            pl.BlockSpec(memory_space=pltpu.SMEM),
            pl.BlockSpec(memory_space=pltpu.VMEM),
        ],
        out_specs=(
            pl.BlockSpec(memory_space=pltpu.VMEM),
            pl.BlockSpec(memory_space=pltpu.VMEM),
        ),
        scratch_shapes=[
            pltpu.VMEM((back_rows, cols), kv.dtype),
            pltpu.VMEM((4, BLK, cols), kv.dtype),
            pltpu.VMEM((BLK, cols), kv.dtype),
            pltpu.VMEM((2, BLK, cols), kv.dtype),
            pltpu.VMEM((BLK, cols), kv.dtype),
            pltpu.VMEM((2, BLK, cols), kv.dtype),
            pltpu.SemaphoreType.DMA((copies,)),
            pltpu.SemaphoreType.DMA((copies,)),
        ],
        compiler_params=pltpu.CompilerParams(
            collective_id=0, has_side_effects=True, vmem_limit_bytes=48 * 1024 * 1024
        ),
    )(ctl, kv)


def forward_kernel(scale, q_ref, k_ref, v_ref, bias_ref, o_ref):
    scores = lax.dot_general(
        q_ref[...], k_ref[...], (((1,), (1,)), ((), ())), preferred_element_type=jnp.float32
    )
    scores = scores * scale + bias_ref[...]
    row_top = jnp.max(scores, axis=1, keepdims=True)
    log_total = row_top + jnp.log(jnp.sum(jnp.exp(scores - row_top), axis=1, keepdims=True))
    probs_low = jnp.exp(scores - log_total).astype(jnp.bfloat16)
    o_ref[...] = jnp.dot(probs_low, v_ref[...], preferred_element_type=jnp.float32).astype(o_ref.dtype)


def attention_out(queries, all_kv, bias, scale):
    rows, width = queries.shape
    keys_total = all_kv.shape[0]
    heads_here = width // HD
    return pl.pallas_call(
        functools.partial(forward_kernel, scale),
        out_shape=jax.ShapeDtypeStruct((rows, width), jnp.bfloat16),
        grid=(heads_here,),
        in_specs=[
            pl.BlockSpec((rows, HD), lambda h: (0, h)),
            pl.BlockSpec((keys_total, HD), lambda h: (0, h)),
            pl.BlockSpec((keys_total, HD), lambda h: (0, h + heads_here)),
            pl.BlockSpec((rows, keys_total), lambda h: (0, 0)),
        ],
        out_specs=pl.BlockSpec((rows, HD), lambda h: (0, h)),
        cost_estimate=pl.CostEstimate(
            flops=4 * rows * keys_total * width,
            transcendentals=2 * rows * keys_total * heads_here,
            bytes_accessed=2 * (2 * rows * width + 2 * keys_total * width) + 4 * rows * keys_total,
        ),
    )(queries, all_kv, all_kv, bias)


def local(queries, keys, values, out_grad, proj_weight, layout):
    tok_dev = queries.shape[0]
    width = queries.shape[1]
    heads_here = width // HD
    blocks_dev = tok_dev // BLK
    block_count = layout.shape[0]
    summary_count = block_count // STRIDE
    score_scale = HD ** (-0.5)
    me = lax.axis_index("seq")
    first_block = me * blocks_dev
    offset_block = layout[block_count - 1, 0] % STRIDE
    reach_back = (LOCAL - 2) // blocks_dev + 1
    span_blocks = [
        min(blocks_dev, LOCAL - 1 - hop_index * blocks_dev) for hop_index in range(reach_back)
    ]
    back_blocks = sum(span_blocks)
    pool_blocks = back_blocks + blocks_dev

    attn_grad = jnp.dot(out_grad, proj_weight, preferred_element_type=jnp.float32).astype(
        jnp.bfloat16
    )
    kv = jnp.concatenate([keys, values], axis=1)

    seq_size = lax.axis_size("seq")
    group = STRIDE // blocks_dev
    groups = seq_size // group
    assert groups == summary_count == 4 and group == 8
    assert (STRIDE - LOCAL) // blocks_dev <= group // 2 and group == 8
    far_ids = jnp.arange(summary_count, dtype=jnp.int32) * STRIDE + offset_block
    lead = offset_block // blocks_dev
    sum_local = offset_block % blocks_dev
    in_group = me % group
    my_group = me // group
    rel = (in_group - lead) % group
    win_kv, far_blocks = exchange(kv, lead, sum_local, span_blocks, seq_size, group)
    pool_kv = jnp.concatenate([win_kv, kv], axis=0)
    far_kv = far_blocks.reshape(summary_count * BLK, 2 * width)

    all_kv = jnp.concatenate([pool_kv, far_kv], axis=0)
    key_rows = all_kv[:, :width].reshape(-1, heads_here, HD)
    value_rows = all_kv[:, width:].reshape(-1, heads_here, HD)
    query_rows = queries.reshape(tok_dev, heads_here, HD)
    grad_rows = attn_grad.reshape(tok_dev, heads_here, HD)

    own_ids = first_block + jnp.arange(blocks_dev, dtype=jnp.int32)
    table_rows = lax.dynamic_slice_in_dim(layout, first_block, blocks_dev, 0)
    pool_ids = first_block - back_blocks + jnp.arange(pool_blocks, dtype=jnp.int32)
    pool_ids_b = jnp.broadcast_to(pool_ids[None, :], (blocks_dev, pool_blocks))
    plain = (pool_ids_b % STRIDE != offset_block) | (pool_ids_b == own_ids[:, None])
    pool_ok = listed(table_rows, pool_ids_b) & plain
    far_ids_b = jnp.broadcast_to(far_ids[None, :], (blocks_dev, summary_count))
    far_ok = listed(table_rows, far_ids_b) & (far_ids_b < own_ids[:, None])
    block_ok = jnp.concatenate([pool_ok, far_ok], axis=1)
    token_ok = jnp.repeat(jnp.repeat(block_ok, BLK, axis=0), BLK, axis=1)
    query_pos = jnp.arange(tok_dev, dtype=jnp.int32)
    pool_pos = jnp.arange(pool_blocks * BLK, dtype=jnp.int32) - back_blocks * BLK
    causal = jnp.concatenate(
        [
            pool_pos[None, :] <= query_pos[:, None],
            jnp.ones((tok_dev, summary_count * BLK), jnp.bool_),
        ],
        axis=1,
    )
    allowed = token_ok & causal

    scores = (
        jnp.einsum("qhd,khd->hqk", query_rows, key_rows, preferred_element_type=jnp.float32)
        * score_scale
    )
    scores = jnp.where(allowed[None], scores, -jnp.inf)
    row_top = jnp.max(scores, axis=-1, keepdims=True)
    log_total = row_top + jnp.log(jnp.sum(jnp.exp(scores - row_top), axis=-1, keepdims=True))
    probs = jnp.exp(scores - log_total)
    probs_low = probs.astype(jnp.bfloat16)
    bias = jnp.where(allowed, 0.0, -jnp.inf).astype(jnp.float32)
    attn_out = attention_out(queries, all_kv, bias, score_scale).reshape(tok_dev, heads_here, HD)
    delta = jnp.transpose(
        jnp.sum(attn_out.astype(jnp.float32) * grad_rows.astype(jnp.float32), axis=-1)
    )[..., None]
    dprobs = jnp.einsum("qhd,khd->hqk", grad_rows, value_rows, preferred_element_type=jnp.float32)
    dscores = (score_scale * probs * (dprobs - delta)).astype(jnp.bfloat16)
    query_grad = jnp.einsum(
        "hqk,khd->qhd", dscores, key_rows, preferred_element_type=jnp.float32
    ).astype(jnp.bfloat16)
    key_part = jnp.einsum("hqk,qhd->khd", dscores, query_rows, preferred_element_type=jnp.float32)
    value_part = jnp.einsum(
        "hqk,qhd->khd", probs_low, grad_rows, preferred_element_type=jnp.float32
    )
    grad_kv = jnp.concatenate(
        [key_part.reshape(-1, width), value_part.reshape(-1, width)], axis=1
    )

    part = grad_kv[pool_blocks * BLK :].reshape(summary_count, BLK, 2 * width)
    half_rows = BLK // 2
    to_next = [(d, (d + group) % seq_size) for d in range(seq_size)]
    to_prev = [(d, (d - group) % seq_size) for d in range(seq_size)]

    def slot(shift):
        return lax.dynamic_index_in_dim(part, (my_group + shift) % groups, 0, keepdims=False)

    opposite = slot(2)
    send_next = jnp.concatenate([slot(1), opposite[:half_rows]], 0).astype(jnp.bfloat16)
    send_prev = jnp.concatenate([slot(-1), opposite[half_rows:]], 0).astype(jnp.bfloat16)
    from_prev = lax.ppermute(send_next, "seq", to_next)
    from_next = lax.ppermute(send_prev, "seq", to_prev)
    far_lo = lax.ppermute(from_prev[BLK:], "seq", to_next).astype(jnp.float32)
    far_hi = lax.ppermute(from_next[BLK:], "seq", to_prev).astype(jnp.float32)
    part = (
        slot(0)
        + from_prev[:BLK].astype(jnp.float32)
        + from_next[:BLK].astype(jnp.float32)
        + jnp.concatenate([far_lo, far_hi], 0)
    )
    lanes = group // 2
    lane = in_group % lanes
    rel_lane = (lane - lead) % lanes
    route = [(g * group + (r ^ lanes), g * group + r) for g in range(groups) for r in range(group)]
    moved = lax.ppermute(part.astype(jnp.bfloat16), "seq", route).astype(jnp.float32)
    part = jnp.where(in_group < lanes, part + moved, part)
    def from_lane(hop):
        return [
            (g * group + r - r % lanes + (r % lanes + hop) % lanes, g * group + r)
            for g in range(groups)
            for r in range(group)
        ]

    sent = part.astype(jnp.bfloat16)
    ahead = lax.ppermute(sent, "seq", from_lane(1)).astype(jnp.float32)
    behind = lax.ppermute(sent, "seq", from_lane(-1)).astype(jnp.float32)
    part = part + jnp.where(rel_lane == 1, ahead, 0.0) + jnp.where(rel_lane == 0, behind, 0.0)
    ahead = lax.ppermute(part.astype(jnp.bfloat16), "seq", from_lane(1)).astype(jnp.float32)
    part = jnp.where(rel_lane == 0, part + ahead, part)
    own_local = jnp.arange(blocks_dev, dtype=jnp.int32)
    far_here = (rel == 0) & (own_local == sum_local)
    far_add = jnp.where(far_here[:, None, None], part[None], 0.0)

    own_grad = grad_kv[back_blocks * BLK : pool_blocks * BLK]
    pool_start = 0
    for distance in range(reach_back, 0, -1):
        rows_needed = span_blocks[distance - 1] * BLK
        back = passed_along(
            grad_kv[pool_start : pool_start + rows_needed].astype(jnp.bfloat16), "seq", -distance
        ).astype(jnp.float32)
        own_grad = own_grad.at[tok_dev - rows_needed :].add(back)
        pool_start = pool_start + rows_needed
    total = own_grad.reshape(blocks_dev, BLK, 2 * width) + far_add
    total = total.reshape(tok_dev, 2 * width).astype(jnp.bfloat16)

    proj_grad = lax.psum_scatter(
        lax.dot_general(
            out_grad,
            attn_out.reshape(tok_dev, width),
            (((0,), (0,)), ((), ())),
            preferred_element_type=jnp.float32,
        ),
        "seq",
        scatter_dimension=0,
        tiled=True,
    )
    return (
        query_grad.reshape(tok_dev, width),
        total[:, :width],
        total[:, width:],
        proj_grad,
    )


def solution(mesh):
    return jax.shard_map(
        local,
        mesh=mesh,
        in_specs=(
            P(("dp", "seq"), "head"),
            P(("dp", "seq"), "head"),
            P(("dp", "seq"), "head"),
            P(("dp", "seq"), None),
            P(None, "head"),
            P(),
        ),
        out_specs=(
            P(("dp", "seq"), "head"),
            P(("dp", "seq"), "head"),
            P(("dp", "seq"), "head"),
            P(("dp", "seq"), "head"),
        ),
        check_vma=False,
    )
```
